32 devices in a mesh: src: 8 (over z, y), rcv: 4 (over x, core).
Axes of the slice: x: 2, y: 2, z: 4, core: 2. Of those that a mesh axis runs over, the one named last changes fastest.
Arguments:
- history: bfloat16 [12, 24576], P(None, 'src'), may hold values from 0.19921875 to 2
- kernel: bfloat16 [12, 8, 4, 24, 64, 128], P(None, 'src', 'rcv'), may hold values from -0.15625 to 0.15625
- scales: float32 [12, 8, 4, 24], P(None, 'src', 'rcv'), may hold values from 0.25 to 4
- block_rows: int32 [12, 8, 4, 24], P(None, 'src', 'rcv'), may hold values from 0 to 95
- block_cols: int32 [12, 8, 4, 24], P(None, 'src', 'rcv'), may hold values from 0 to 47
- shear_pre: float32 [24576], P(('src', 'rcv')), may hold values from 0.5 to 2
- sigma_pre: float32 [24576], P(('src', 'rcv')), may hold values from 2 to 4
- friction_a: float32 [24576], P(('src', 'rcv')), may hold values from 0.15 to 0.5
- state_rate: float32 [24576], P(('src', 'rcv')), may hold values from 0.5 to 2
- state_init: float32 [24576], P(('src', 'rcv')), may hold values from -1 to 1
Outputs:
- slip_rates: float32 [4, 24576], P(None, ('src', 'rcv'))
- state_final: float32 [24576], P(('src', 'rcv'))
The draws below stay inside these ranges and needn't reach their ends.
All inputs are finite; a program needn't handle non-finite values.
Results may differ from the reference program's by a relative error of at most 0.0022.
Values may be sent and summed in bfloat16 or wider, within the bound.
No kernel may reach another device: no remote copies, remote signals or barrier semaphores. Data moves between devices by JAX's collectives and lax.ppermute only.
A program may use at most 64 MiB of HBM per device.

```python
import math
import jax
import jax.numpy as jnp
from jax import lax

BLOCK = 64
SRC_BLOCKS = 48
LAGS = 12
SLOTS = 24
STEPS = 4
NEWTON_ITERS = 4
SRC_ELEMS = 3072
ELEMENTS = 24576
GROUP_BLOCKS = 12
RCV_BLOCKS = 96
N_SRC = 8
N_RCV = 4


def touch_ends(array, own_key, smallest, largest):
    place = [jax.random.randint(jax.random.fold_in(own_key, axis), (), 0, length) for axis, length in enumerate(array.shape)]
    widest = array.shape.index(max(array.shape))
    next_to = place[:widest] + [(place[widest] + 1) % array.shape[widest]] + place[widest + 1:]
    return array.at[tuple(place)].set(smallest).at[tuple(next_to)].set(largest)


def block_levels(own_key, shape, shards, smallest, high):
    def one(dim, shards_of):
        steps = jax.random.uniform(jax.random.fold_in(jax.random.fold_in(own_key, 6), dim), (shards_of,), jnp.float32, smallest / len(shards), high / len(shards))
        return jnp.repeat(jnp.exp(steps), shape[dim] // shards_of).reshape((-1,) + (1,) * (len(shape) - dim - 1))

    gain = one(*shards[0])
    for cut in shards[1:]:
        gain = gain * one(*cut)
    return gain


def gaussian(stream_key, shape, width, most, split=(), kind=jnp.bfloat16):
    factor_of = block_levels(stream_key, shape, split, -0.22, 0.18) if split else 1.0
    values = jax.random.normal(stream_key, shape, jnp.float32) * width * factor_of
    return jnp.minimum(jnp.maximum(values, -most), most).astype(kind)


def setup_inputs(seed: int = 0) -> dict:
    streams_of = jax.random.split(jax.random.key(seed), 11)
    history = jnp.clip(0.19921875 + 1.8007812 * jax.random.uniform(streams_of[0], (LAGS, ELEMENTS), jnp.float32) ** block_levels(streams_of[0], (LAGS, ELEMENTS), ((1, 8),), -0.2, 0.2), 0.19921875, 2.0).astype(jnp.bfloat16)
    kernel = gaussian(streams_of[1], (LAGS, N_SRC, N_RCV, SLOTS, BLOCK, 2 * BLOCK), (LAGS * SLOTS * N_RCV * BLOCK // SRC_BLOCKS) ** -0.5, 0.15625, ((1, 8), (2, 4)))
    scales = jnp.clip(jnp.exp(math.log(4.0) - 2.7725887 * jax.random.uniform(streams_of[2], (LAGS, N_SRC, N_RCV, SLOTS), jnp.float32) ** block_levels(streams_of[2], (LAGS, N_SRC, N_RCV, SLOTS), ((1, 8), (2, 4)), -0.2, 0.2)), 0.25, 4.0)
    block_rows = touch_ends(jax.random.randint(streams_of[3], (LAGS, N_SRC, N_RCV, SLOTS), 0, RCV_BLOCKS), jax.random.fold_in(streams_of[3], 1), 0, RCV_BLOCKS - 1).astype(jnp.int32)
    block_cols = touch_ends(jax.random.randint(streams_of[4], (LAGS, N_SRC, N_RCV, SLOTS), 0, SRC_BLOCKS), jax.random.fold_in(streams_of[4], 1), 0, SRC_BLOCKS - 1).astype(jnp.int32)
    shear_pre = jnp.clip(0.5 + 1.5 * jax.random.uniform(streams_of[5], (ELEMENTS,), jnp.float32) ** block_levels(streams_of[5], (ELEMENTS,), ((0, 32),), -0.2, 0.2), 0.5, 2.0)
    sigma_pre = jnp.clip(2.0 + 2.0 * jax.random.uniform(streams_of[6], (ELEMENTS,), jnp.float32) ** block_levels(streams_of[6], (ELEMENTS,), ((0, 32),), -0.2, 0.2), 2.0, 4.0)
    friction_a = jnp.clip(jnp.exp(math.log(0.5) - 1.2039728 * jax.random.uniform(streams_of[7], (ELEMENTS,), jnp.float32) ** block_levels(streams_of[7], (ELEMENTS,), ((0, 32),), -0.2, 0.2)), 0.15, 0.5)
    state_rate = jnp.clip(jnp.exp(math.log(2.0) - 1.3862944 * jax.random.uniform(streams_of[8], (ELEMENTS,), jnp.float32) ** block_levels(streams_of[8], (ELEMENTS,), ((0, 32),), -0.2, 0.2)), 0.5, 2.0)
    state_init = jnp.clip(jax.random.uniform(streams_of[9], (ELEMENTS,), jnp.float32, -1.0, 1.0) * block_levels(streams_of[9], (ELEMENTS,), ((0, 32),), -0.4, 0.0), -1.0, 1.0)
    return dict(history=history, kernel=kernel, scales=scales, block_rows=block_rows, block_cols=block_cols, shear_pre=shear_pre, sigma_pre=sigma_pre, friction_a=friction_a, state_rate=state_rate, state_init=state_init)


DAMPING = 1.0
LOADING = 0.05
TIME_STEP = 0.2

def inverse_sinh(value):
    magnitude = jnp.abs(value)
    result = jnp.log(magnitude + jnp.sqrt(1.0 + magnitude * magnitude))
    return jnp.where(value < 0.0, -result, result)

def friction_solve(stress, step_no, guess, state_now, shear_pre, sigma_pre, friction_a, state_rate):
    comp_width = stress.shape[1] // 2
    shear_total = stress[:, :comp_width].reshape(-1) + shear_pre + LOADING * (step_no + 1)
    normal = sigma_pre * (1.0 + 0.5 * jnp.tanh(stress[:, comp_width:].reshape(-1)))
    strength = friction_a * normal
    factor = 0.5 * jnp.exp(state_now)
    slip_rate = guess
    for attempt in range(NEWTON_ITERS):
        scaled = slip_rate * factor
        misfit = shear_total - DAMPING * slip_rate - strength * inverse_sinh(scaled)
        derivative = -DAMPING - strength * factor / jnp.sqrt(1.0 + scaled * scaled)
        slip_rate = slip_rate - misfit / derivative
    next_state = state_now + TIME_STEP * state_rate * jnp.tanh(jnp.exp(-state_now) - jnp.abs(slip_rate))
    return (slip_rate, next_state)

def step_stress(kernel, scales, global_rows, block_cols, sources):

    def one_source(running, src_index):
        panel = lax.dynamic_index_in_dim(kernel, src_index, 1, keepdims=False).astype(jnp.float32)
        weight = lax.dynamic_index_in_dim(scales, src_index, 1, keepdims=False)
        col_ids = lax.dynamic_index_in_dim(block_cols, src_index, 1, keepdims=False)
        row_ids = lax.dynamic_index_in_dim(global_rows, src_index, 1, keepdims=False)
        src_slab = lax.dynamic_slice_in_dim(sources, src_index * SRC_ELEMS, SRC_ELEMS, 1)
        src_slab = src_slab.reshape(LAGS, SRC_BLOCKS, BLOCK)
        picked = src_slab[jnp.arange(LAGS, dtype=jnp.int32)[:, None, None], col_ids].astype(jnp.float32)
        partial_terms = jnp.einsum('lrkj,lrkjm->lrkm', picked, panel, precision=lax.Precision.HIGHEST)
        partial_terms = partial_terms * weight[:, :, :, None]
        running = running + jax.ops.segment_sum(partial_terms.reshape(-1, 2 * BLOCK), row_ids.reshape(-1), num_segments=ELEMENTS // BLOCK)
        return (running, None)
    start = jnp.zeros((ELEMENTS // BLOCK, 2 * BLOCK), jnp.float32)
    running, unused = lax.scan(one_source, start, jnp.arange(N_SRC, dtype=jnp.int32))
    return running

def reference(history, kernel, scales, block_rows, block_cols, shear_pre, sigma_pre, friction_a, state_rate, state_init):
    receiver = jnp.arange(N_RCV, dtype=jnp.int32)[None, None, :, None]
    global_rows = (block_rows // GROUP_BLOCKS * N_RCV + receiver) * GROUP_BLOCKS + block_rows % GROUP_BLOCKS
    rows_list = [history[index] for index in range(LAGS)]
    guess = history[LAGS - 1].astype(jnp.float32)
    state_now = state_init
    outputs = []
    for step_no in range(STEPS):
        sources = jnp.stack(rows_list[step_no:LAGS + step_no][::-1])
        stress = step_stress(kernel, scales, global_rows, block_cols, sources)
        slip_rate, state_now = friction_solve(stress, step_no, guess, state_now, shear_pre, sigma_pre, friction_a, state_rate)
        outputs.append(slip_rate)
        rows_list.append(slip_rate.astype(jnp.bfloat16))
        guess = slip_rate
    return (jnp.stack(outputs), state_now)
```

```python
import jax
import jax.numpy as jnp
from jax import lax
from jax.experimental import pallas as pl
from jax.experimental.pallas import tpu as pltpu
from jax.sharding import PartitionSpec as P

STEPS = 4
NEWTON_ITERS = 4
DAMPING = 1.0
LOADING = 0.05
TIME_STEP = 0.2
LANES = 128
SPLIT = 3


def inverse_sinh(value):
    magnitude = jnp.abs(value)
    result = jnp.log(magnitude + jnp.sqrt(1.0 + magnitude * magnitude))
    return jnp.where(value < 0.0, -result, result)


def friction_solve(stress, step_no, guess, state_now, shear_sigma, rate_a):
    axis = stress.ndim - 1
    half = LANES // 2
    shear_total = stress + shear_sigma + LOADING * (step_no + 1)
    strength = rate_a * (shear_sigma * (1.0 + 0.5 * jnp.tanh(stress)))
    strength = pltpu.roll(strength, half, axis)
    factor = 0.5 * jnp.exp(state_now)
    slip_rate = guess
    for attempt in range(NEWTON_ITERS):
        scaled = slip_rate * factor
        misfit = shear_total - DAMPING * slip_rate - strength * inverse_sinh(scaled)
        derivative = -DAMPING - strength * factor / jnp.sqrt(1.0 + scaled * scaled)
        slip_rate = slip_rate - misfit / derivative
    next_state = state_now + TIME_STEP * rate_a * jnp.tanh(
        jnp.exp(-state_now) - jnp.abs(slip_rate)
    )
    low = lax.broadcasted_iota(jnp.int32, stress.shape, axis) < half
    return jnp.where(low, slip_rate, 0.0), jnp.where(low, next_state, 0.0)


def older_kernel(
    panels, history, rows, cols, scales, send, rest, guess, panel_buf, sources, acc, sems,
    *, lags, slots, width, n_src, n_rcv, own_blocks,
):
    src_blocks = n_rcv * own_blocks
    recv_blocks = n_src * own_blocks
    per_tile = own_blocks // SPLIT
    pad_rows = 24

    def panel_copy(lag):
        return pltpu.make_async_copy(panels.at[lag], panel_buf.at[lag], sems.at[lag])

    for lag in range(lags):
        panel_copy(lag).start()
    tail = jnp.zeros((pad_rows - lags, LANES), jnp.float32)
    for pair in range(src_blocks // 2):
        tile = history[:, pair * LANES:(pair + 1) * LANES].astype(jnp.float32)
        sources[2 * pair * pad_rows:2 * pair * pad_rows + lags, :] = tile
        sources[2 * pair * pad_rows + lags:(2 * pair + 1) * pad_rows, :] = tail
        sources[(2 * pair + 1) * pad_rows:(2 * pair + 1) * pad_rows + lags, :] = pltpu.roll(tile, width, 1)
        sources[(2 * pair + 1) * pad_rows + lags:(2 * pair + 2) * pad_rows, :] = tail
    acc[...] = jnp.zeros_like(acc)

    def one_lag(lag, carry):
        panel_copy(lag).wait()
        for slot in range(slots):
            col = cols[lag, slot]
            picked = sources[pl.ds(col * pad_rows + (lags - 1) - lag, 8), :]
            picked = picked[:, :width].astype(jnp.bfloat16)
            term = jnp.dot(picked, panel_buf[lag, slot], preferred_element_type=jnp.float32)
            at = pl.ds(pl.multiple_of(rows[lag, slot] * 8, 8), 8)
            acc[at, :] = acc[at, :] + term * scales[lag, slot]
        return carry

    lax.fori_loop(0, lags, one_lag, 0)
    for dest in range(n_src):
        for tile in range(SPLIT):
            piece = acc[pl.ds((dest * own_blocks + tile) * 8, per_tile, stride=8 * SPLIT), :]
            for dup in range(n_rcv):
                send[dest * n_rcv + dup, :, tile * LANES:(tile + 1) * LANES] = piece
    for step in range(1, STEPS):
        rest[step - 1] = acc[pl.ds(step, recv_blocks, stride=8), :]
    for tile in range(SPLIT):
        guess[tile] = sources[pl.ds(tile * pad_rows + lags - 1, src_blocks // SPLIT, stride=pad_rows * SPLIT), :]


def step_kernel(
    recv, params, guess, state_in, rest, panels, rows, cols, scales,
    send, rest_out, slip_out, state_out, total, fields, sources, acc,
    *, step_no, lags_now, slots, width, n_src, n_rcv, own_blocks, dups, first,
):
    per_tile = own_blocks // SPLIT
    for tile in range(SPLIT):
        lanes = slice(tile * LANES, (tile + 1) * LANES)
        for owner in range(n_rcv):
            part = recv[owner, :, lanes]
            for src in range(1, n_src):
                part = part + recv[src * n_rcv + owner, :, lanes]
            at = slice(owner * per_tile, (owner + 1) * per_tile)
            total[tile, at, :] = part
            for kind in range(3):
                fields[kind, tile, at, :] = params[owner, kind, :, lanes]
    state_now = fields[2] if first else state_in[...]
    slip_rate, next_state = friction_solve(
        total[...], step_no, guess[...], state_now, fields[0], fields[1]
    )
    slip_out[...] = slip_rate
    state_out[...] = next_state
    for tile in range(SPLIT):
        sources[pl.ds(tile, n_rcv * per_tile, stride=SPLIT), :] = slip_rate[tile]
    acc[...] = rest[...]
    for lag in range(lags_now):
        for slot in range(slots):
            picked = sources[pl.ds(cols[lag, slot], 1), :]
            picked = jnp.broadcast_to(picked[:, :width], (8, width)).astype(jnp.bfloat16)
            term = jnp.dot(picked, panels[lag, slot], preferred_element_type=jnp.float32)
            at = pl.ds(rows[lag, slot], 1)
            acc[lag, at, :] = acc[lag, at, :] + term[:1] * scales[lag, slot]
    for dest in range(n_src):
        for tile in range(SPLIT):
            piece = acc[0, pl.ds(dest * own_blocks + tile, per_tile, stride=SPLIT), :]
            for dup in range(dups):
                send[dest * dups + dup, :, tile * LANES:(tile + 1) * LANES] = piece
    for later in range(1, lags_now):
        rest_out[later - 1] = acc[later]


def last_kernel(recv, params, guess, state_in, slip_out, state_out, *, step_no, n_src):
    for tile in range(SPLIT):
        lanes = slice(tile * LANES, (tile + 1) * LANES)
        part = recv[0, :, lanes]
        for src in range(1, n_src):
            part = part + recv[src, :, lanes]
        slip_rate, next_state = friction_solve(
            part, step_no, guess[tile], state_in[tile], params[0, :, lanes], params[1, :, lanes]
        )
        slip_out[tile] = slip_rate
        state_out[tile] = next_state


def per_device(
    history, kernel, scales, block_rows, block_cols,
    shear_pre, sigma_pre, friction_a, state_rate, state_init,
):
    lags = kernel.shape[0]
    slots = kernel.shape[3]
    width = kernel.shape[4]
    n_src = lax.axis_size("src")
    n_rcv = lax.axis_size("rcv")
    own_blocks = shear_pre.shape[0] // width
    src_blocks = n_rcv * own_blocks
    recv_blocks = n_src * own_blocks
    per_tile = own_blocks // SPLIT
    wide = SPLIT * LANES
    panels = kernel.reshape(lags, slots, width, 2 * width)
    weights = scales.reshape(lags, slots)
    row_ids = block_rows.reshape(lags, slots)
    col_ids = block_cols.reshape(lags, slots)
    sizes = dict(slots=slots, width=width, n_src=n_src, n_rcv=n_rcv, own_blocks=own_blocks)
    vmem = pl.BlockSpec(memory_space=pltpu.VMEM)
    smem = pl.BlockSpec(memory_space=pltpu.SMEM)
    f32 = jnp.float32

    def shape(*dims):
        return jax.ShapeDtypeStruct(dims, f32)

    def paired(low, high):
        both = jnp.stack([low.reshape(-1, width), high.reshape(-1, width)], axis=1)
        return both.reshape(per_tile, wide)

    own_params = jnp.stack(
        [paired(shear_pre, sigma_pre), paired(state_rate, friction_a), paired(state_init, state_init)]
    )
    params = lax.all_gather(own_params, "rcv", axis=0)

    send, rest, guess = pl.pallas_call(
        lambda *refs: older_kernel(*refs, lags=lags, **sizes),
        in_specs=[pl.BlockSpec(memory_space=pl.ANY), vmem, smem, smem, smem],
        out_specs=[vmem] * 3,
        out_shape=[
            shape(n_src * n_rcv, per_tile, wide),
            shape(STEPS - 1, recv_blocks, LANES),
            shape(SPLIT, src_blocks // SPLIT, LANES),
        ],
        scratch_shapes=[
            pltpu.VMEM((lags, slots, width, 2 * width), jnp.bfloat16),
            pltpu.VMEM((src_blocks * 24, LANES), f32),
            pltpu.VMEM((recv_blocks * 8, LANES), f32),
            pltpu.SemaphoreType.DMA((lags,)),
        ],
        compiler_params=pltpu.CompilerParams(vmem_limit_bytes=32 * 1024 * 1024),
        name="older",
    )(panels, history, row_ids, col_ids, weights)

    state = guess
    outputs = []
    recent = panels[:STEPS - 1]
    for step_no in range(STEPS - 1):
        recv = lax.all_to_all(send, ("src", "rcv"), 0, 0, tiled=True)
        lags_now = STEPS - 1 - step_no
        dups = n_rcv if lags_now > 1 else 1
        u_shape = shape(SPLIT, src_blocks // SPLIT, LANES)
        outs = pl.pallas_call(
            lambda *refs, step_no=step_no, lags_now=lags_now, dups=dups: step_kernel(
                *refs, step_no=step_no, lags_now=lags_now, dups=dups, first=step_no == 0, **sizes
            ),
            in_specs=[vmem] * 6 + [smem] * 3,
            out_specs=[vmem] * 4,
            out_shape=[
                shape(n_src * dups, per_tile, wide),
                shape(max(lags_now - 1, 1), recv_blocks, LANES),
                u_shape,
                u_shape,
            ],
            scratch_shapes=[
                pltpu.VMEM((SPLIT, src_blocks // SPLIT, LANES), f32),
                pltpu.VMEM((3, SPLIT, src_blocks // SPLIT, LANES), f32),
                pltpu.VMEM((src_blocks, LANES), f32),
                pltpu.VMEM((lags_now, recv_blocks, LANES), f32),
            ],
            compiler_params=pltpu.CompilerParams(vmem_limit_bytes=32 * 1024 * 1024),
            name="step",
        )(recv, params, guess, state, rest, recent, row_ids, col_ids, weights)
        send, rest, guess, state = outs
        outputs.append(guess)

    recv = lax.all_to_all(send, "src", 0, 0, tiled=True)
    mine = lax.axis_index("rcv") * per_tile

    def own(field):
        return lax.dynamic_slice_in_dim(field, mine, per_tile, 1)

    small = shape(SPLIT, per_tile, LANES)
    slip_rate, state = pl.pallas_call(
        lambda *refs: last_kernel(*refs, step_no=STEPS - 1, n_src=n_src),
        in_specs=[vmem] * 4,
        out_specs=[vmem] * 2,
        out_shape=[small, small],
        name="last",
    )(recv, own_params, own(guess), own(state))

    def flat(field):
        return jnp.swapaxes(field[:, :, :width], 0, 1).reshape(-1)

    rates = [flat(own(field)) for field in outputs] + [flat(slip_rate)]
    return (jnp.stack(rates), flat(state))


def solution(mesh):
    return jax.shard_map(
        per_device,
        mesh=mesh,
        in_specs=(
            P(None, "src"),
            P(None, "src", "rcv", None, None, None),
            P(None, "src", "rcv", None),
            P(None, "src", "rcv", None),
            P(None, "src", "rcv", None),
            P(("src", "rcv")),
            P(("src", "rcv")),
            P(("src", "rcv")),
            P(("src", "rcv")),
            P(("src", "rcv")),
        ),
        out_specs=(P(None, ("src", "rcv")), P(("src", "rcv"))),
        check_vma=False,
    )
```

```python
import functools

import jax
import jax.numpy as jnp
from jax import lax
from jax.experimental import pallas as pl
from jax.experimental.pallas import tpu as pltpu
from jax.sharding import PartitionSpec as P

STEPS = 4
NEWTON_ITERS = 4
DAMPING = 1.0
LOADING = 0.05
TIME_STEP = 0.2
LANES = 128
HALF = LANES // 2
ROWS = 4
IN_FLIGHT = 3
TAPS = 24
VMEM_LIMIT = 16 * 1024 * 1024


def inverse_sinh(value):
    magnitude = jnp.abs(value)
    result = jnp.log(magnitude + jnp.sqrt(1.0 + magnitude * magnitude))
    return jnp.where(value < 0.0, -result, result)


def friction_solve(shear, normal_stress, step_no, guess, state_now, fields):
    shear_pre, sigma_pre, friction_a, state_rate = fields
    shear_total = shear + shear_pre + LOADING * (step_no + 1)
    normal = sigma_pre * (1.0 + 0.5 * jnp.tanh(normal_stress))
    strength = friction_a * normal
    factor = 0.5 * jnp.exp(state_now)
    slip_rate = guess
    for attempt in range(NEWTON_ITERS):
        scaled = slip_rate * factor
        misfit = shear_total - DAMPING * slip_rate - strength * inverse_sinh(scaled)
        derivative = -DAMPING - strength * factor / jnp.sqrt(1.0 + scaled * scaled)
        slip_rate = slip_rate - misfit / derivative
    next_state = state_now + TIME_STEP * state_rate * jnp.tanh(
        jnp.exp(-state_now) - jnp.abs(slip_rate)
    )
    return slip_rate, next_state


def split_stress(even, odd):
    low = lax.broadcasted_iota(jnp.int32, even.shape, 1) < HALF
    shear = jnp.where(low, even, pltpu.roll(odd, HALF, 1))
    normal = jnp.where(low, pltpu.roll(even, HALF, 1), odd)
    return shear, normal


def pack_messages(send, acc, own_blocks, n_dest, dups, stride):
    for dest in range(n_dest):
        for tile in range(own_blocks // ROWS):
            first = (dest * own_blocks + tile * ROWS) * stride
            rows = pl.ds(first, ROWS, stride=stride) if stride > 1 else pl.ds(first, ROWS)
            piece = acc[rows, :]
            for dup in range(dups):
                send[dest * dups + dup, :, tile * LANES:(tile + 1) * LANES] = piece


def sum_messages(recv, total, own_blocks, n_src, owners):
    for owner in range(owners):
        part = recv[owner]
        for src in range(1, n_src):
            part = part + recv[src * owners + owner]
        for tile in range(own_blocks // ROWS):
            first = owner * own_blocks + tile * ROWS
            total[first:first + ROWS, :] = part[:, tile * LANES:(tile + 1) * LANES]
    pairs = owners * own_blocks // 2
    return total[pl.ds(0, pairs, stride=2), :], total[pl.ds(1, pairs, stride=2), :]


def older_kernel(
    panels, history, rows_in, cols_in, scales_in, send, rest, guess, recent,
    panel_buf, history_buf, rows, cols, scales, sources, acc, sems, small_sems, out_sem,
    *, lags, slots, n_src, n_rcv, own_blocks,
):
    src_blocks = n_rcv * own_blocks
    recv_blocks = n_src * own_blocks
    smalls = [
        pltpu.make_async_copy(source, target, small_sems.at[at])
        for at, (source, target) in enumerate(
            [(history, history_buf), (cols_in, cols), (rows_in, rows), (scales_in, scales)]
        )
    ]

    def panel_copy(lag):
        return pltpu.make_async_copy(panels.at[lag], panel_buf.at[lag], sems.at[lag])

    for copy in smalls:
        copy.start()
    for lag in range(IN_FLIGHT):
        panel_copy(lag).start()
    acc[...] = jnp.zeros_like(acc)
    tail = jnp.zeros((TAPS - lags, LANES), jnp.float32)
    smalls[0].wait()
    for pair in range(src_blocks // 2):
        tile = history_buf[:, pair * LANES:(pair + 1) * LANES].astype(jnp.float32)
        for half in range(2):
            base = (2 * pair + half) * TAPS
            sources[base:base + lags, :] = tile if half == 0 else pltpu.roll(tile, HALF, 1)
            sources[base + lags:base + TAPS, :] = tail
    for copy in smalls[1:]:
        copy.wait()

    def one_lag(lag, carry):
        panel_copy(lag).wait()

        @pl.when(lag + IN_FLIGHT < lags)
        def _():
            panel_copy(lag + IN_FLIGHT).start()

        for slot in range(slots):
            col = cols[lag, 0, 0, slot]
            picked = sources[pl.ds(col * TAPS + (lags - 1) - lag, 8), :]
            picked = picked[:, :HALF].astype(jnp.bfloat16)
            term = jnp.dot(picked, panel_buf[lag, slot], preferred_element_type=jnp.float32)
            at = pl.ds(pl.multiple_of(rows[lag, 0, 0, slot] * 8, 8), 8)
            acc[at, :] = acc[at, :] + term * scales[lag, 0, 0, slot]
        return carry

    lax.fori_loop(0, lags, one_lag, 0)
    handed_on = pltpu.make_async_copy(panel_buf.at[pl.ds(0, STEPS - 1)], recent, out_sem)
    handed_on.start()
    pack_messages(send, acc, own_blocks, n_src, n_rcv, 8)
    for step in range(1, STEPS):
        rest[step - 1] = acc[pl.ds(step, recv_blocks, stride=8), :]
    guess[...] = sources[pl.ds(lags - 1, src_blocks // 2, stride=2 * TAPS), :]
    handed_on.wait()


def small_copies(sources, targets, sems):
    return [
        pltpu.make_async_copy(source, target, sems.at[at])
        for at, (source, target) in enumerate(zip(sources, targets))
    ]


def spread_sources(slip_rate, sources):
    pairs = slip_rate.shape[0]
    sources[pl.ds(0, pairs, stride=2), :] = slip_rate
    sources[pl.ds(1, pairs, stride=2), :] = pltpu.roll(slip_rate, HALF, 1)


def add_terms(acc_at, lag, panels, sources, rows, cols, scales, slots):
    for slot in range(slots):
        picked = sources[pl.ds(cols[lag, 0, 0, slot], 1), :]
        picked = jnp.broadcast_to(picked[:, :HALF], (8, HALF)).astype(jnp.bfloat16)
        term = jnp.dot(picked, panels[lag, slot], preferred_element_type=jnp.float32)
        at = pl.ds(rows[lag, 0, 0, slot], 1)
        acc_at[at, :] = acc_at[at, :] + term[:1] * scales[lag, 0, 0, slot]


def step_kernel(
    recv, fields, guess, state_in, rest, panels, rows_in, cols_in, scales_in,
    send, slip_out, state_out,
    rows, cols, scales, total, sources, acc, sems,
    *, step_no, rest_at, slots, n_src, n_rcv, own_blocks, dups,
):
    copies = small_copies((cols_in, rows_in, scales_in), (cols, rows, scales), sems)
    for copy in copies:
        copy.start()
    shear, normal = split_stress(*sum_messages(recv, total, own_blocks, n_src, n_rcv))
    slip_rate, next_state = friction_solve(
        shear, normal, step_no, guess[...], state_in[...], [fields[kind] for kind in range(4)]
    )
    slip_out[...] = slip_rate
    state_out[...] = next_state
    spread_sources(slip_rate, sources)
    acc[...] = rest[rest_at]
    for copy in copies:
        copy.wait()
    add_terms(acc, 0, panels, sources, rows, cols, scales, slots)
    pack_messages(send, acc, own_blocks, n_src, dups, 1)


def later_kernel(
    slip_rate, rest, panels, rows_in, cols_in, scales_in, rest_out,
    rows, cols, scales, sources, sems, *, later, slots,
):
    copies = small_copies((cols_in, rows_in, scales_in), (cols, rows, scales), sems)
    for copy in copies:
        copy.start()
    spread_sources(slip_rate[...], sources)
    for at in range(later):
        rest_out[at] = rest[at + 1]
    for copy in copies:
        copy.wait()
    for at in range(later):
        add_terms(rest_out.at[at], at + 1, panels, sources, rows, cols, scales, slots)


def last_kernel(
    recv, shear_pre, sigma_pre, friction_a, state_rate, state_in, *refs, step_no, n_src,
):
    slips, (slip_out, state_out, total) = refs[:step_no], refs[step_no:]
    pairs = slip_out.shape[1] // LANES
    mine = pl.ds(lax.axis_index("rcv") * pairs, pairs)
    shear, normal = split_stress(*sum_messages(recv, total, 2 * pairs, n_src, 1))
    fields = [ref[...] for ref in (shear_pre, sigma_pre, friction_a, state_rate)]
    slip_rate, next_state = friction_solve(
        shear, normal, step_no, slips[-1][mine, :], state_in[mine, :], fields
    )
    for step, field in enumerate([ref[mine, :] for ref in slips] + [slip_rate]):
        for row in range(pairs):
            slip_out[step:step + 1, row * LANES:(row + 1) * LANES] = field[row:row + 1]
    state_out[...] = next_state


def per_device(
    history, kernel, scales, block_rows, block_cols,
    shear_pre, sigma_pre, friction_a, state_rate, state_init,
):
    lags = kernel.shape[0]
    slots = kernel.shape[3]
    width = kernel.shape[4]
    n_src = lax.axis_size("src")
    n_rcv = lax.axis_size("rcv")
    own = shear_pre.shape[0]
    own_blocks = own // width
    pairs = own // LANES
    src_blocks = n_rcv * own_blocks
    recv_rows = n_src * own_blocks
    message = (ROWS, own_blocks // ROWS * LANES)
    panels = kernel.reshape(lags, slots, width, 2 * width)
    f32 = jnp.float32
    hbm = pl.BlockSpec(memory_space=pltpu.HBM)
    vmem = pl.BlockSpec(memory_space=pltpu.VMEM)
    sizes = dict(slots=slots, n_src=n_src, n_rcv=n_rcv, own_blocks=own_blocks)
    index_bufs = [
        pltpu.SMEM(block_rows.shape, jnp.int32),
        pltpu.SMEM(block_cols.shape, jnp.int32),
        pltpu.SMEM(scales.shape, f32),
    ]

    def shape(*dims, dtype=f32):
        return jax.ShapeDtypeStruct(dims, dtype)

    def call(body, ins, outs, scratch, name, args, flops, limit=VMEM_LIMIT):
        return pl.pallas_call(
            body, in_specs=ins, out_specs=[vmem] * len(outs), out_shape=outs, scratch_shapes=scratch,
            compiler_params=pltpu.CompilerParams(vmem_limit_bytes=limit), name=name,
            cost_estimate=pl.CostEstimate(flops=flops, bytes_accessed=flops // 64, transcendentals=0),
        )(*args)

    own_fields = [
        field.reshape(pairs, LANES)
        for field in (shear_pre, sigma_pre, friction_a, state_rate, state_init)
    ]
    fields = lax.all_gather(jnp.stack(own_fields), "rcv", axis=1, tiled=True)

    panels, history, *table = [
        pltpu.with_memory_space_constraint(array, pltpu.HBM)
        for array in (panels, history, block_rows, block_cols, scales)
    ]
    one_lag = 2 * slots * width * 2 * width * 8
    send, rest, guess, recent = call(
        functools.partial(older_kernel, lags=lags, **sizes),
        [hbm] * 5,
        [
            shape(n_src * n_rcv, *message),
            shape(STEPS - 1, recv_rows, LANES),
            shape(src_blocks // 2, LANES),
            shape(STEPS - 1, slots, width, 2 * width, dtype=panels.dtype),
        ],
        [
            pltpu.VMEM(panels.shape, panels.dtype),
            pltpu.VMEM(history.shape, history.dtype),
            *index_bufs,
            pltpu.VMEM((src_blocks * TAPS, LANES), f32),
            pltpu.VMEM((recv_rows * 8, LANES), f32),
            pltpu.SemaphoreType.DMA((lags,)),
            pltpu.SemaphoreType.DMA((4,)),
            pltpu.SemaphoreType.DMA,
        ],
        "older", [panels, history, *table], 60 * one_lag, limit=32 * 1024 * 1024,
    )

    state = fields[4]
    slips = []
    for step_no in range(STEPS - 1):
        recv = lax.all_to_all(send, ("src", "rcv"), 0, 0, tiled=True) if step_no == 0 else recv
        last = step_no == STEPS - 2
        dups = 1 if last else n_rcv
        send, slip_rate, state = call(
            functools.partial(step_kernel, step_no=step_no, rest_at=0, dups=dups, **sizes),
            [vmem] * 6 + [hbm] * 3,
            [
                shape(n_src * dups, *message),
                shape(src_blocks // 2, LANES),
                shape(src_blocks // 2, LANES),
            ],
            index_bufs + [
                pltpu.VMEM((src_blocks, LANES), f32),
                pltpu.VMEM((src_blocks, LANES), f32),
                pltpu.VMEM((recv_rows, LANES), f32),
                pltpu.SemaphoreType.DMA((3,)),
            ],
            "step", [recv, fields, guess, state, rest, recent, *table], one_lag,
        )
        guess = slip_rate
        slips.append(slip_rate)
        recv = lax.all_to_all(send, "src" if last else ("src", "rcv"), 0, 0, tiled=True)
        later = STEPS - 2 - step_no
        if later:
            rest, = call(
                functools.partial(later_kernel, later=later, slots=slots),
                [vmem] * 3 + [hbm] * 3,
                [shape(later, recv_rows, LANES)],
                index_bufs + [
                    pltpu.VMEM((src_blocks, LANES), f32),
                    pltpu.SemaphoreType.DMA((3,)),
                ],
                "later", [slip_rate, rest, recent, *table], later * one_lag,
            )

    slip_rates, state = call(
        functools.partial(last_kernel, step_no=STEPS - 1, n_src=n_src),
        [vmem] * (6 + len(slips)),
        [shape(STEPS, own), shape(pairs, LANES)],
        [pltpu.VMEM((own_blocks, LANES), f32)],
        "last", [recv, *own_fields[:4], state, *slips], 10 ** 6,
    )
    return (slip_rates, state.reshape(own))


def solution(mesh):
    return jax.shard_map(
        per_device,
        mesh=mesh,
        in_specs=(
            P(None, "src"),
            P(None, "src", "rcv", None, None, None),
            P(None, "src", "rcv", None),
            P(None, "src", "rcv", None),
            P(None, "src", "rcv", None),
            P(("src", "rcv")),
            P(("src", "rcv")),
            P(("src", "rcv")),
            P(("src", "rcv")),
            P(("src", "rcv")),
        ),
        out_specs=(P(None, ("src", "rcv")), P(("src", "rcv"))),
        check_vma=False,
    )
```

```python
import functools

import jax
import jax.numpy as jnp
from jax import lax
from jax.experimental import pallas as pl
from jax.experimental.pallas import tpu as pltpu
from jax.sharding import PartitionSpec as P

STEPS = 4
NEWTON_ITERS = 4
DAMPING = 1.0
LOADING = 0.05
TIME_STEP = 0.2
LANES = 128
HALF = LANES // 2
ROWS = 4
IN_FLIGHT = 5
GROUP = 4
SLOT_ROWS = 32
PARTS = 3
TAPS = 24
LEAD = 8
VMEM_LIMIT = 16 * 1024 * 1024


def inverse_sinh(value):
    magnitude = jnp.abs(value)
    result = jnp.log(magnitude + jnp.sqrt(1.0 + magnitude * magnitude))
    return jnp.where(value < 0.0, -result, result)


def friction_solve(shear, normal_stress, step_no, guess, state_now, fields):
    shear_pre, sigma_pre, friction_a, state_rate = fields
    shear_total = shear + shear_pre + LOADING * (step_no + 1)
    normal = sigma_pre * (1.0 + 0.5 * jnp.tanh(normal_stress))
    strength = friction_a * normal
    factor = 0.5 * jnp.exp(state_now)
    slip_rate = guess
    for attempt in range(NEWTON_ITERS):
        scaled = slip_rate * factor
        misfit = shear_total - DAMPING * slip_rate - strength * inverse_sinh(scaled)
        derivative = -DAMPING - strength * factor / jnp.sqrt(1.0 + scaled * scaled)
        slip_rate = slip_rate - misfit / derivative
    next_state = state_now + TIME_STEP * state_rate * jnp.tanh(
        jnp.exp(-state_now) - jnp.abs(slip_rate)
    )
    return slip_rate, next_state


def split_stress(even, odd):
    low = lax.broadcasted_iota(jnp.int32, even.shape, 1) < HALF
    shear = jnp.where(low, even, pltpu.roll(odd, HALF, 1))
    normal = jnp.where(low, pltpu.roll(even, HALF, 1), odd)
    return shear, normal


def pack_messages(send, partials, own_blocks, n_dest, dups):
    for dest in range(n_dest):
        for tile in range(own_blocks // ROWS):
            piece = partials(dest * own_blocks + tile * ROWS, ROWS)
            for dup in range(dups):
                send[dest * dups + dup, :, tile * LANES:(tile + 1) * LANES] = piece


def sum_messages(recv, total, own_blocks, n_src, owners):
    for owner in range(owners):
        part = recv[owner]
        for src in range(1, n_src):
            part = part + recv[src * owners + owner]
        for tile in range(own_blocks // ROWS):
            first = owner * own_blocks + tile * ROWS
            total[first:first + ROWS, :] = part[:, tile * LANES:(tile + 1) * LANES]
    pairs = owners * own_blocks // 2
    return total[pl.ds(0, pairs, stride=2), :], total[pl.ds(1, pairs, stride=2), :]


def make_tables(rows, cols, scales, gather, scatter, weights):
    slots = rows.shape[-1]
    lane = lax.broadcasted_iota(jnp.int32, (SLOT_ROWS, LANES), 1)
    diagonal = lax.broadcasted_iota(jnp.int32, (SLOT_ROWS, LANES), 0) == lane
    rest = jnp.full((1, LANES - slots), -1.0, jnp.float32)

    def widened(values):
        return jnp.concatenate([values.astype(jnp.float32), rest], axis=1)

    def column(values):
        spread = jnp.where(diagonal, jnp.broadcast_to(values, diagonal.shape), 0.0)
        return jnp.sum(spread, axis=1, keepdims=True)

    one_row = lax.broadcasted_iota(jnp.int32, (1, LANES), 1)
    block = lax.broadcasted_iota(jnp.int32, (scatter.shape[1], LANES), 0).astype(jnp.float32)
    for lag in range(STEPS - 1):
        row_ids = widened(rows[lag, 0])
        for part in range(1, PARTS):
            at = one_row >= part * SLOT_ROWS
            row_ids = jnp.where(at, pltpu.roll(widened(rows[lag, 0]), part * SLOT_ROWS, 1), row_ids)
        row_ids = jnp.where(one_row < PARTS * SLOT_ROWS, row_ids, -1.0)
        scatter[lag] = (block == row_ids).astype(jnp.float32).astype(jnp.bfloat16)
        picks = column(widened(cols[lag, 0])) == lane.astype(jnp.float32)
        gather[lag] = picks.astype(jnp.float32).astype(jnp.bfloat16)
        weights[lag] = jnp.broadcast_to(column(widened(scales[lag, 0])), weights.shape[1:])


def older_kernel(
    panels, history, rows_in, cols_in, scales_in,
    send, rest, guess, recent, gather, scatter, weights,
    panel_buf, history_buf, rows, cols, scales, rows_now, cols_now, scales_now, sources, acc,
    sems, small_sems, out_sem,
    *, lags, slots, n_src, n_rcv, own_blocks,
):
    src_blocks = n_rcv * own_blocks
    recv_blocks = n_src * own_blocks
    recent_lags = pl.ds(0, STEPS - 1)
    smalls = [
        pltpu.make_async_copy(source, target, small_sems.at[at])
        for at, (source, target) in enumerate([
            (history, history_buf), (cols_in, cols), (rows_in, rows), (scales_in, scales),
            (rows_in.at[recent_lags], rows_now), (cols_in.at[recent_lags], cols_now),
            (scales_in.at[recent_lags], scales_now),
        ])
    ]

    def panel_copy(lag):
        return pltpu.make_async_copy(panels.at[lag], panel_buf.at[lag], sems.at[lag])

    for copy in smalls:
        copy.start()
    for lag in range(IN_FLIGHT):
        panel_copy(lag).start()
    acc[...] = jnp.zeros_like(acc)
    tail = jnp.zeros((TAPS - lags, LANES), jnp.float32)
    sources[0:LEAD, :] = jnp.zeros((LEAD, LANES), jnp.float32)
    smalls[0].wait()
    for pair in range(src_blocks // 2):
        tile = history_buf[:, pair * LANES:(pair + 1) * LANES].astype(jnp.float32)
        for half in range(2):
            base = LEAD + (2 * pair + half) * TAPS
            sources[base:base + lags, :] = tile if half == 0 else pltpu.roll(tile, HALF, 1)
            sources[base + lags:base + TAPS, :] = tail
    for copy in smalls[1:]:
        copy.wait()
    make_tables(rows_now, cols_now, scales_now, gather, scatter, weights)

    top = lax.broadcasted_iota(jnp.int32, (8, LANES), 0) < STEPS
    match = top == (lax.broadcasted_iota(jnp.int32, (8, LANES), 1) < HALF)
    zero = jnp.zeros((8, LANES), jnp.float32)

    def one_lag(lag, carry):
        panel_copy(lag).wait()

        @pl.when(lag + IN_FLIGHT < lags)
        def _():
            panel_copy(lag + IN_FLIGHT).start()

        first_tap = LEAD + (lags - 1) - lag
        for group in range(0, slots, GROUP):
            pairs = []
            for slot in range(group, group + GROUP, 2):
                low = sources[pl.ds(cols[lag, 0, 0, slot] * TAPS + first_tap, 8), :]
                partner = cols[lag, 0, 0, slot + 1] ^ 1
                high = sources[pl.ds(partner * TAPS + first_tap - STEPS, 8), :]
                pairs.append(jnp.where(match, jnp.where(top, low, high), 0.0))
            columns = [
                jnp.concatenate([pair if at == to else zero for at in range(len(pairs))], axis=0)
                for to, pair in enumerate(pairs)
            ]
            picked = jnp.concatenate(columns, axis=1).astype(jnp.bfloat16)
            panel = panel_buf[lag, group:group + GROUP].reshape(GROUP * HALF, LANES)
            terms = jnp.dot(picked, panel, preferred_element_type=jnp.float32)
            for pair in range(len(pairs)):
                slot = group + 2 * pair
                scale = jnp.where(top, scales[lag, 0, 0, slot], scales[lag, 0, 0, slot + 1])
                term = terms[8 * pair:8 * pair + 8] * scale
                for part, addend in enumerate([jnp.where(top, term, 0.0), jnp.where(top, 0.0, term)]):
                    at = pl.ds(pl.multiple_of(rows[lag, 0, 0, slot + part] * 8, 8), 8)
                    acc[at, :] = acc[at, :] + addend
        return carry

    lax.fori_loop(0, lags, one_lag, 0)
    handed_on = pltpu.make_async_copy(panel_buf.at[recent_lags], recent, out_sem)
    handed_on.start()

    def partials(first_row, count, step):
        low, high = [
            acc[pl.ds(first_row * 8 + start, count, stride=8), :] for start in (step, STEPS + step)
        ]
        return low + high

    pack_messages(send, lambda first, count: partials(first, count, 0), own_blocks, n_src, n_rcv)
    for step in range(1, STEPS):
        rest[step - 1] = partials(0, recv_blocks, step)
    guess[...] = sources[pl.ds(LEAD + lags - 1, src_blocks // 2, stride=2 * TAPS), :]
    handed_on.wait()


def spread_sources(slip_rate, sources):
    pairs = slip_rate.shape[0]
    low = lax.broadcasted_iota(jnp.int32, slip_rate.shape, 1) < HALF
    turned = pltpu.roll(slip_rate, HALF, 1)
    sources[pl.ds(0, pairs, stride=2), :] = jnp.where(low, slip_rate, turned)
    sources[pl.ds(1, pairs, stride=2), :] = jnp.where(low, turned, slip_rate)


def new_terms(lag, panels, sources, gather, scatter, weights):
    slots, width, wide = panels.shape[1:]
    rounded = sources[...].astype(jnp.bfloat16)
    picked = jnp.dot(gather[lag][:, :rounded.shape[0]], rounded, preferred_element_type=jnp.float32)
    lane = lax.broadcasted_iota(jnp.int32, picked.shape, 1)
    row = lax.broadcasted_iota(jnp.int32, picked.shape, 0)
    first = row - jnp.where(lane < HALF, 0, 1)
    tiles = [
        jnp.where(first == slot, picked, 0.0).astype(jnp.bfloat16) for slot in range(0, slots, 2)
    ]
    panel = panels[lag].reshape(slots * width, wide)
    terms = jnp.dot(jnp.concatenate(tiles, axis=1), panel, preferred_element_type=jnp.float32)
    left = terms * weights[lag]
    parts = []
    for part in range(PARTS):
        parts.append(left.astype(jnp.bfloat16))
        left = left - parts[-1].astype(jnp.float32)
    stacked = jnp.concatenate(parts, axis=0)
    return jnp.dot(scatter[lag][:, :stacked.shape[0]], stacked, preferred_element_type=jnp.float32)


def step_kernel(
    recv, fields, guess, state_in, rest, panels, gather, scatter, weights,
    send, slip_out, state_out, total, sources, acc,
    *, step_no, n_src, n_rcv, own_blocks, dups,
):
    shear, normal = split_stress(*sum_messages(recv, total, own_blocks, n_src, n_rcv))
    slip_rate, next_state = friction_solve(
        shear, normal, step_no, guess[...], state_in[...], [fields[kind] for kind in range(4)]
    )
    spread_sources(slip_rate, sources)
    acc[...] = rest[0] + new_terms(0, panels, sources, gather, scatter, weights)
    pack_messages(send, lambda first, count: acc[pl.ds(first, count), :], own_blocks, n_src, dups)
    slip_out[...] = slip_rate
    state_out[...] = next_state


def later_kernel(slip_rate, rest, panels, gather, scatter, weights, rest_out, sources):
    spread_sources(slip_rate[...], sources)
    for at in range(rest_out.shape[0]):
        rest_out[at] = rest[at + 1] + new_terms(at + 1, panels, sources, gather, scatter, weights)


def last_kernel(
    recv, shear_pre, sigma_pre, friction_a, state_rate, state_in, *refs, step_no, n_src,
):
    slips, (slip_out, state_out, total) = refs[:step_no], refs[step_no:]
    pairs = slip_out.shape[1] // LANES
    mine = pl.ds(lax.axis_index("rcv") * pairs, pairs)
    shear, normal = split_stress(*sum_messages(recv, total, 2 * pairs, n_src, 1))
    fields = [ref[...] for ref in (shear_pre, sigma_pre, friction_a, state_rate)]
    slip_rate, next_state = friction_solve(
        shear, normal, step_no, slips[-1][mine, :], state_in[mine, :], fields
    )
    for step, field in enumerate([ref[mine, :] for ref in slips] + [slip_rate]):
        for row in range(pairs):
            slip_out[step:step + 1, row * LANES:(row + 1) * LANES] = field[row:row + 1]
    state_out[...] = next_state


def per_device(
    history, kernel, scales, block_rows, block_cols,
    shear_pre, sigma_pre, friction_a, state_rate, state_init,
):
    lags = kernel.shape[0]
    slots = kernel.shape[3]
    width = kernel.shape[4]
    n_src = lax.axis_size("src")
    n_rcv = lax.axis_size("rcv")
    own = shear_pre.shape[0]
    own_blocks = own // width
    pairs = own // LANES
    src_blocks = n_rcv * own_blocks
    recv_rows = n_src * own_blocks
    message = (ROWS, own_blocks // ROWS * LANES)
    panels = kernel.reshape(lags, slots, width, 2 * width)
    f32 = jnp.float32
    hbm = pl.BlockSpec(memory_space=pltpu.HBM)
    vmem = pl.BlockSpec(memory_space=pltpu.VMEM)
    sizes = dict(slots=slots, n_src=n_src, n_rcv=n_rcv, own_blocks=own_blocks)
    def shape(*dims, dtype=f32):
        return jax.ShapeDtypeStruct(dims, dtype)

    def call(body, ins, outs, scratch, name, args, flops, limit=VMEM_LIMIT):
        return pl.pallas_call(
            body, in_specs=ins, out_specs=[vmem] * len(outs), out_shape=outs, scratch_shapes=scratch,
            compiler_params=pltpu.CompilerParams(vmem_limit_bytes=limit), name=name,
            cost_estimate=pl.CostEstimate(flops=flops, bytes_accessed=flops // 64, transcendentals=0),
        )(*args)

    own_fields = [
        field.reshape(pairs, LANES)
        for field in (shear_pre, sigma_pre, friction_a, state_rate, state_init)
    ]
    fields = lax.all_gather(jnp.stack(own_fields), "rcv", axis=1, tiled=True)

    panels, history, *table = [
        pltpu.with_memory_space_constraint(array, pltpu.HBM)
        for array in (panels, history, block_rows, block_cols, scales)
    ]
    one_lag = 2 * slots * width * 2 * width * 8
    send, rest, guess, recent, *tables = call(
        functools.partial(older_kernel, lags=lags, **sizes),
        [hbm] * 5,
        [
            shape(n_src * n_rcv, *message),
            shape(STEPS - 1, recv_rows, LANES),
            shape(src_blocks // 2, LANES),
            shape(STEPS - 1, slots, width, 2 * width, dtype=panels.dtype),
            shape(STEPS - 1, SLOT_ROWS, LANES, dtype=jnp.bfloat16),
            shape(STEPS - 1, recv_rows, LANES, dtype=jnp.bfloat16),
            shape(STEPS - 1, SLOT_ROWS, LANES),
        ],
        [
            pltpu.VMEM(panels.shape, panels.dtype),
            pltpu.VMEM(history.shape, history.dtype),
            *[pltpu.SMEM(array.shape, array.dtype) for array in table],
            *[pltpu.VMEM((STEPS - 1, *array.shape[1:]), array.dtype) for array in table],
            pltpu.VMEM((LEAD + src_blocks * TAPS, LANES), f32),
            pltpu.VMEM((recv_rows * 8, LANES), f32),
            pltpu.SemaphoreType.DMA((lags,)),
            pltpu.SemaphoreType.DMA((7,)),
            pltpu.SemaphoreType.DMA,
        ],
        "older", [panels, history, *table], 60 * one_lag, limit=32 * 1024 * 1024,
    )

    state = fields[4]
    slips = []
    recv = lax.all_to_all(send, ("src", "rcv"), 0, 0, tiled=True)
    for step_no in range(STEPS - 1):
        last = step_no == STEPS - 2
        dups = 1 if last else n_rcv
        send, slip_rate, state = call(
            functools.partial(
                step_kernel, step_no=step_no, dups=dups, n_src=n_src, n_rcv=n_rcv, own_blocks=own_blocks
            ),
            [vmem] * 9,
            [
                shape(n_src * dups, *message),
                shape(src_blocks // 2, LANES),
                shape(src_blocks // 2, LANES),
            ],
            [
                pltpu.VMEM((src_blocks, LANES), f32),
                pltpu.VMEM((src_blocks, LANES), f32),
                pltpu.VMEM((recv_rows, LANES), f32),
            ],
            "step", [recv, fields, guess, state, rest, recent, *tables], one_lag,
        )
        guess = slip_rate
        slips.append(slip_rate)
        recv = lax.all_to_all(send, "src" if last else ("src", "rcv"), 0, 0, tiled=True)
        later = STEPS - 2 - step_no
        if later:
            rest, = call(
                later_kernel,
                [vmem] * 6,
                [shape(later, recv_rows, LANES)],
                [pltpu.VMEM((src_blocks, LANES), f32)],
                "later", [slip_rate, rest, recent, *tables], later * one_lag,
            )

    slip_rates, state = call(
        functools.partial(last_kernel, step_no=STEPS - 1, n_src=n_src),
        [vmem] * (6 + len(slips)),
        [shape(STEPS, own), shape(pairs, LANES)],
        [pltpu.VMEM((own_blocks, LANES), f32)],
        "last", [recv, *own_fields[:4], state, *slips], 10 ** 6,
    )
    return (slip_rates, state.reshape(own))


def solution(mesh):
    return jax.shard_map(
        per_device,
        mesh=mesh,
        in_specs=(
            P(None, "src"),
            P(None, "src", "rcv", None, None, None),
            P(None, "src", "rcv", None),
            P(None, "src", "rcv", None),
            P(None, "src", "rcv", None),
            P(("src", "rcv")),
            P(("src", "rcv")),
            P(("src", "rcv")),
            P(("src", "rcv")),
            P(("src", "rcv")),
        ),
        out_specs=(P(None, ("src", "rcv")), P(("src", "rcv"))),
        check_vma=False,
    )
```

```python
import functools

import jax
import jax.numpy as jnp
from jax import lax
from jax.experimental import pallas as pl
from jax.experimental.pallas import tpu as pltpu
from jax.sharding import PartitionSpec as P

STEPS = 4
NEWTON_ITERS = 4
DAMPING = 1.0
LOADING = 0.05
TIME_STEP = 0.2
LANES = 128
HALF = LANES // 2
ROWS = 4
IN_FLIGHT = 5
GROUP = 4
SLOT_ROWS = 32
PARTS = 3
MESSAGE_SCALE = 2.0 ** 22
TAPS = 24
LEAD = 8
VMEM_LIMIT = 16 * 1024 * 1024


def inverse_sinh(value):
    magnitude = jnp.abs(value)
    result = jnp.log(magnitude + jnp.sqrt(1.0 + magnitude * magnitude))
    return jnp.where(value < 0.0, -result, result)


def friction_solve(shear, normal_stress, step_no, guess, state_now, fields):
    shear_pre, sigma_pre, friction_a, state_rate = fields
    shear_total = shear + shear_pre + LOADING * (step_no + 1)
    normal = sigma_pre * (1.0 + 0.5 * jnp.tanh(normal_stress))
    strength = friction_a * normal
    factor = 0.5 * jnp.exp(state_now)
    slip_rate = guess
    for attempt in range(NEWTON_ITERS):
        scaled = slip_rate * factor
        misfit = shear_total - DAMPING * slip_rate - strength * inverse_sinh(scaled)
        derivative = -DAMPING - strength * factor / jnp.sqrt(1.0 + scaled * scaled)
        slip_rate = slip_rate - misfit / derivative
    next_state = state_now + TIME_STEP * state_rate * jnp.tanh(
        jnp.exp(-state_now) - jnp.abs(slip_rate)
    )
    return slip_rate, next_state


def split_stress(even, odd):
    low = lax.broadcasted_iota(jnp.int32, even.shape, 1) < HALF
    shear = jnp.where(low, even, pltpu.roll(odd, HALF, 1))
    normal = jnp.where(low, pltpu.roll(even, HALF, 1), odd)
    return shear, normal


def encode(partial):
    scaled = partial * (1.0 / MESSAGE_SCALE)
    return (scaled * scaled * scaled).astype(jnp.bfloat16)


def decode(message):
    cube = message.astype(jnp.float32)
    magnitude = jnp.abs(cube)
    root = jnp.exp2(jnp.log2(jnp.maximum(magnitude, 1e-38)) * (1.0 / 3.0)) * MESSAGE_SCALE
    root = jnp.where(cube < 0.0, -root, root)
    return jnp.where(magnitude > 0.0, root, 0.0)


def pack_messages(send, partials, own_blocks, n_dest, dups):
    for dest in range(n_dest):
        for tile in range(own_blocks // ROWS):
            piece = encode(partials(dest * own_blocks + tile * ROWS, ROWS))
            for dup in range(dups):
                send[dest * dups + dup, :, tile * LANES:(tile + 1) * LANES] = piece


def sum_messages(recv, total, own_blocks, n_src, owners):
    for owner in range(owners):
        part = decode(recv[owner])
        for src in range(1, n_src):
            part = part + decode(recv[src * owners + owner])
        for tile in range(own_blocks // ROWS):
            first = owner * own_blocks + tile * ROWS
            total[first:first + ROWS, :] = part[:, tile * LANES:(tile + 1) * LANES]
    pairs = owners * own_blocks // 2
    return total[pl.ds(0, pairs, stride=2), :], total[pl.ds(1, pairs, stride=2), :]


def make_tables(rows, cols, scales, gather, scatter, weights):
    slots = rows.shape[-1]
    lane = lax.broadcasted_iota(jnp.int32, (SLOT_ROWS, LANES), 1)
    diagonal = lax.broadcasted_iota(jnp.int32, (SLOT_ROWS, LANES), 0) == lane
    rest = jnp.full((1, LANES - slots), -1.0, jnp.float32)

    def widened(values):
        return jnp.concatenate([values.astype(jnp.float32), rest], axis=1)

    def column(values):
        spread = jnp.where(diagonal, jnp.broadcast_to(values, diagonal.shape), 0.0)
        return jnp.sum(spread, axis=1, keepdims=True)

    one_row = lax.broadcasted_iota(jnp.int32, (1, LANES), 1)
    block = lax.broadcasted_iota(jnp.int32, (scatter.shape[1], LANES), 0).astype(jnp.float32)
    for lag in range(STEPS - 1):
        row_ids = widened(rows[lag, 0])
        for part in range(1, PARTS):
            at = one_row >= part * SLOT_ROWS
            row_ids = jnp.where(at, pltpu.roll(widened(rows[lag, 0]), part * SLOT_ROWS, 1), row_ids)
        row_ids = jnp.where(one_row < PARTS * SLOT_ROWS, row_ids, -1.0)
        scatter[lag] = (block == row_ids).astype(jnp.float32).astype(jnp.bfloat16)
        picks = column(widened(cols[lag, 0])) == lane.astype(jnp.float32)
        gather[lag] = picks.astype(jnp.float32).astype(jnp.bfloat16)
        weights[lag] = jnp.broadcast_to(column(widened(scales[lag, 0])), weights.shape[1:])


def older_kernel(
    panels, history, rows_in, cols_in, scales_in,
    send, rest, guess, recent, gather, scatter, weights,
    panel_buf, history_buf, rows, cols, scales, rows_now, cols_now, scales_now, sources, acc,
    sems, small_sems, out_sem,
    *, lags, slots, n_src, n_rcv, own_blocks,
):
    src_blocks = n_rcv * own_blocks
    recv_blocks = n_src * own_blocks
    recent_lags = pl.ds(0, STEPS - 1)
    smalls = [
        pltpu.make_async_copy(source, target, small_sems.at[at])
        for at, (source, target) in enumerate([
            (history, history_buf), (cols_in, cols), (rows_in, rows), (scales_in, scales),
            (rows_in.at[recent_lags], rows_now), (cols_in.at[recent_lags], cols_now),
            (scales_in.at[recent_lags], scales_now),
        ])
    ]

    def panel_copy(lag):
        return pltpu.make_async_copy(panels.at[lag], panel_buf.at[lag], sems.at[lag])

    for copy in smalls:
        copy.start()
    for lag in range(IN_FLIGHT):
        panel_copy(lag).start()
    acc[...] = jnp.zeros_like(acc)
    tail = jnp.zeros((TAPS - lags, LANES), jnp.float32)
    sources[0:LEAD, :] = jnp.zeros((LEAD, LANES), jnp.float32)
    smalls[0].wait()
    for pair in range(src_blocks // 2):
        tile = history_buf[:, pair * LANES:(pair + 1) * LANES].astype(jnp.float32)
        for half in range(2):
            base = LEAD + (2 * pair + half) * TAPS
            sources[base:base + lags, :] = tile if half == 0 else pltpu.roll(tile, HALF, 1)
            sources[base + lags:base + TAPS, :] = tail
    for copy in smalls[1:]:
        copy.wait()
    make_tables(rows_now, cols_now, scales_now, gather, scatter, weights)

    top = lax.broadcasted_iota(jnp.int32, (8, LANES), 0) < STEPS
    match = top == (lax.broadcasted_iota(jnp.int32, (8, LANES), 1) < HALF)
    zero = jnp.zeros((8, LANES), jnp.float32)

    def one_lag(lag, carry):
        panel_copy(lag).wait()

        @pl.when(lag + IN_FLIGHT < lags)
        def _():
            panel_copy(lag + IN_FLIGHT).start()

        first_tap = LEAD + (lags - 1) - lag
        for group in range(0, slots, GROUP):
            pairs = []
            for slot in range(group, group + GROUP, 2):
                low = sources[pl.ds(cols[lag, 0, 0, slot] * TAPS + first_tap, 8), :]
                partner = cols[lag, 0, 0, slot + 1] ^ 1
                high = sources[pl.ds(partner * TAPS + first_tap - STEPS, 8), :]
                pairs.append(jnp.where(match, jnp.where(top, low, high), 0.0))
            columns = [
                jnp.concatenate([pair if at == to else zero for at in range(len(pairs))], axis=0)
                for to, pair in enumerate(pairs)
            ]
            picked = jnp.concatenate(columns, axis=1).astype(jnp.bfloat16)
            panel = panel_buf[lag, group:group + GROUP].reshape(GROUP * HALF, LANES)
            terms = jnp.dot(picked, panel, preferred_element_type=jnp.float32)
            for pair in range(len(pairs)):
                slot = group + 2 * pair
                scale = jnp.where(top, scales[lag, 0, 0, slot], scales[lag, 0, 0, slot + 1])
                term = terms[8 * pair:8 * pair + 8] * scale
                for part, addend in enumerate([jnp.where(top, term, 0.0), jnp.where(top, 0.0, term)]):
                    at = pl.ds(pl.multiple_of(rows[lag, 0, 0, slot + part] * 8, 8), 8)
                    acc[at, :] = acc[at, :] + addend
        return carry

    lax.fori_loop(0, lags, one_lag, 0)
    handed_on = pltpu.make_async_copy(panel_buf.at[recent_lags], recent, out_sem)
    handed_on.start()

    def partials(first_row, count, step):
        low, high = [
            acc[pl.ds(first_row * 8 + start, count, stride=8), :] for start in (step, STEPS + step)
        ]
        return low + high

    pack_messages(send, lambda first, count: partials(first, count, 0), own_blocks, n_src, n_rcv)
    for step in range(1, STEPS):
        rest[step - 1] = partials(0, recv_blocks, step)
    guess[...] = sources[pl.ds(LEAD + lags - 1, src_blocks // 2, stride=2 * TAPS), :]
    handed_on.wait()


def spread_sources(slip_rate, sources):
    pairs = slip_rate.shape[0]
    low = lax.broadcasted_iota(jnp.int32, slip_rate.shape, 1) < HALF
    turned = pltpu.roll(slip_rate, HALF, 1)
    sources[pl.ds(0, pairs, stride=2), :] = jnp.where(low, slip_rate, turned)
    sources[pl.ds(1, pairs, stride=2), :] = jnp.where(low, turned, slip_rate)


def new_terms(lag, panels, sources, gather, scatter, weights):
    slots, width, wide = panels.shape[1:]
    rounded = sources[...].astype(jnp.bfloat16)
    picked = jnp.dot(gather[lag][:, :rounded.shape[0]], rounded, preferred_element_type=jnp.float32)
    lane = lax.broadcasted_iota(jnp.int32, picked.shape, 1)
    row = lax.broadcasted_iota(jnp.int32, picked.shape, 0)
    first = row - jnp.where(lane < HALF, 0, 1)
    tiles = [
        jnp.where(first == slot, picked, 0.0).astype(jnp.bfloat16) for slot in range(0, slots, 2)
    ]
    panel = panels[lag].reshape(slots * width, wide)
    terms = jnp.dot(jnp.concatenate(tiles, axis=1), panel, preferred_element_type=jnp.float32)
    left = terms * weights[lag]
    parts = []
    for part in range(PARTS):
        parts.append(left.astype(jnp.bfloat16))
        left = left - parts[-1].astype(jnp.float32)
    stacked = jnp.concatenate(parts, axis=0)
    return jnp.dot(scatter[lag][:, :stacked.shape[0]], stacked, preferred_element_type=jnp.float32)


def step_kernel(
    recv, fields, guess, state_in, rest, panels, gather, scatter, weights,
    send, slip_out, state_out, total, sources, acc,
    *, step_no, n_src, n_rcv, own_blocks, dups,
):
    shear, normal = split_stress(*sum_messages(recv, total, own_blocks, n_src, n_rcv))
    slip_rate, next_state = friction_solve(
        shear, normal, step_no, guess[...], state_in[...], [fields[kind] for kind in range(4)]
    )
    spread_sources(slip_rate, sources)
    acc[...] = rest[0] + new_terms(0, panels, sources, gather, scatter, weights)
    pack_messages(send, lambda first, count: acc[pl.ds(first, count), :], own_blocks, n_src, dups)
    slip_out[...] = slip_rate
    state_out[...] = next_state


def later_kernel(slip_rate, rest, panels, gather, scatter, weights, rest_out, sources):
    spread_sources(slip_rate[...], sources)
    for at in range(rest_out.shape[0]):
        rest_out[at] = rest[at + 1] + new_terms(at + 1, panels, sources, gather, scatter, weights)


def last_kernel(
    recv, shear_pre, sigma_pre, friction_a, state_rate, state_in, *refs, step_no, n_src,
):
    slips, (slip_out, state_out, total) = refs[:step_no], refs[step_no:]
    pairs = slip_out.shape[1] // LANES
    mine = pl.ds(lax.axis_index("rcv") * pairs, pairs)
    shear, normal = split_stress(*sum_messages(recv, total, 2 * pairs, n_src, 1))
    fields = [ref[...] for ref in (shear_pre, sigma_pre, friction_a, state_rate)]
    slip_rate, next_state = friction_solve(
        shear, normal, step_no, slips[-1][mine, :], state_in[mine, :], fields
    )
    for step, field in enumerate([ref[mine, :] for ref in slips] + [slip_rate]):
        for row in range(pairs):
            slip_out[step:step + 1, row * LANES:(row + 1) * LANES] = field[row:row + 1]
    state_out[...] = next_state


def per_device(
    history, kernel, scales, block_rows, block_cols,
    shear_pre, sigma_pre, friction_a, state_rate, state_init,
):
    lags = kernel.shape[0]
    slots = kernel.shape[3]
    width = kernel.shape[4]
    n_src = lax.axis_size("src")
    n_rcv = lax.axis_size("rcv")
    own = shear_pre.shape[0]
    own_blocks = own // width
    pairs = own // LANES
    src_blocks = n_rcv * own_blocks
    recv_rows = n_src * own_blocks
    message = (ROWS, own_blocks // ROWS * LANES)
    panels = kernel.reshape(lags, slots, width, 2 * width)
    f32 = jnp.float32
    hbm = pl.BlockSpec(memory_space=pltpu.HBM)
    vmem = pl.BlockSpec(memory_space=pltpu.VMEM)
    sizes = dict(slots=slots, n_src=n_src, n_rcv=n_rcv, own_blocks=own_blocks)
    def shape(*dims, dtype=f32):
        return jax.ShapeDtypeStruct(dims, dtype)

    def call(body, ins, outs, scratch, name, args, flops, limit=VMEM_LIMIT):
        return pl.pallas_call(
            body, in_specs=ins, out_specs=[vmem] * len(outs), out_shape=outs, scratch_shapes=scratch,
            compiler_params=pltpu.CompilerParams(vmem_limit_bytes=limit), name=name,
            cost_estimate=pl.CostEstimate(flops=flops, bytes_accessed=flops // 64, transcendentals=0),
        )(*args)

    own_fields = [
        field.reshape(pairs, LANES)
        for field in (shear_pre, sigma_pre, friction_a, state_rate, state_init)
    ]
    fields = lax.all_gather(jnp.stack(own_fields), "rcv", axis=1, tiled=True)

    panels, history, *table = [
        pltpu.with_memory_space_constraint(array, pltpu.HBM)
        for array in (panels, history, block_rows, block_cols, scales)
    ]
    one_lag = 2 * slots * width * 2 * width * 8
    send, rest, guess, recent, *tables = call(
        functools.partial(older_kernel, lags=lags, **sizes),
        [hbm] * 5,
        [
            shape(n_src * n_rcv, *message, dtype=jnp.bfloat16),
            shape(STEPS - 1, recv_rows, LANES),
            shape(src_blocks // 2, LANES),
            shape(STEPS - 1, slots, width, 2 * width, dtype=panels.dtype),
            shape(STEPS - 1, SLOT_ROWS, LANES, dtype=jnp.bfloat16),
            shape(STEPS - 1, recv_rows, LANES, dtype=jnp.bfloat16),
            shape(STEPS - 1, SLOT_ROWS, LANES),
        ],
        [
            pltpu.VMEM(panels.shape, panels.dtype),
            pltpu.VMEM(history.shape, history.dtype),
            *[pltpu.SMEM(array.shape, array.dtype) for array in table],
            *[pltpu.VMEM((STEPS - 1, *array.shape[1:]), array.dtype) for array in table],
            pltpu.VMEM((LEAD + src_blocks * TAPS, LANES), f32),
            pltpu.VMEM((recv_rows * 8, LANES), f32),
            pltpu.SemaphoreType.DMA((lags,)),
            pltpu.SemaphoreType.DMA((7,)),
            pltpu.SemaphoreType.DMA,
        ],
        "older", [panels, history, *table], 60 * one_lag, limit=32 * 1024 * 1024,
    )

    state = fields[4]
    slips = []
    recv = lax.all_to_all(send, ("src", "rcv"), 0, 0, tiled=True)
    for step_no in range(STEPS - 1):
        last = step_no == STEPS - 2
        dups = 1 if last else n_rcv
        send, slip_rate, state = call(
            functools.partial(
                step_kernel, step_no=step_no, dups=dups, n_src=n_src, n_rcv=n_rcv, own_blocks=own_blocks
            ),
            [vmem] * 9,
            [
                shape(n_src * dups, *message, dtype=jnp.bfloat16),
                shape(src_blocks // 2, LANES),
                shape(src_blocks // 2, LANES),
            ],
            [
                pltpu.VMEM((src_blocks, LANES), f32),
                pltpu.VMEM((src_blocks, LANES), f32),
                pltpu.VMEM((recv_rows, LANES), f32),
            ],
            "step", [recv, fields, guess, state, rest, recent, *tables], one_lag,
        )
        guess = slip_rate
        slips.append(slip_rate)
        recv = lax.all_to_all(send, "src" if last else ("src", "rcv"), 0, 0, tiled=True)
        later = STEPS - 2 - step_no
        if later:
            rest, = call(
                later_kernel,
                [vmem] * 6,
                [shape(later, recv_rows, LANES)],
                [pltpu.VMEM((src_blocks, LANES), f32)],
                "later", [slip_rate, rest, recent, *tables], later * one_lag,
            )

    slip_rates, state = call(
        functools.partial(last_kernel, step_no=STEPS - 1, n_src=n_src),
        [vmem] * (6 + len(slips)),
        [shape(STEPS, own), shape(pairs, LANES)],
        [pltpu.VMEM((own_blocks, LANES), f32)],
        "last", [recv, *own_fields[:4], state, *slips], 10 ** 6,
    )
    return (slip_rates, state.reshape(own))


def solution(mesh):
    return jax.shard_map(
        per_device,
        mesh=mesh,
        in_specs=(
            P(None, "src"),
            P(None, "src", "rcv", None, None, None),
            P(None, "src", "rcv", None),
            P(None, "src", "rcv", None),
            P(None, "src", "rcv", None),
            P(("src", "rcv")),
            P(("src", "rcv")),
            P(("src", "rcv")),
            P(("src", "rcv")),
            P(("src", "rcv")),
        ),
        out_specs=(P(None, ("src", "rcv")), P(("src", "rcv"))),
        check_vma=False,
    )
```

```python
import functools

import jax
import jax.numpy as jnp
from jax import lax
from jax.experimental import pallas as pl
from jax.experimental.pallas import tpu as pltpu
from jax.sharding import PartitionSpec as P

STEPS = 4
NEWTON_ITERS = 4
DAMPING = 1.0
LOADING = 0.05
TIME_STEP = 0.2
LANES = 128
HALF = LANES // 2
ROWS = 4
IN_FLIGHT = 5
GROUP = 4
SLOT_ROWS = 32
PARTS = 3
MESSAGE_SCALE = 2.0 ** 22
TAPS = 24
LEAD = 8
VMEM_LIMIT = 16 * 1024 * 1024


def inverse_sinh(value):
    magnitude = jnp.abs(value)
    result = jnp.log(magnitude + jnp.sqrt(1.0 + magnitude * magnitude))
    return jnp.where(value < 0.0, -result, result)


def friction_solve(shear, normal_stress, step_no, guess, state_now, fields):
    shear_pre, sigma_pre, friction_a, state_rate = fields
    shear_total = shear + shear_pre + LOADING * (step_no + 1)
    normal = sigma_pre * (1.0 + 0.5 * jnp.tanh(normal_stress))
    strength = friction_a * normal
    factor = 0.5 * jnp.exp(state_now)
    slip_rate = guess
    for attempt in range(NEWTON_ITERS):
        scaled = slip_rate * factor
        misfit = shear_total - DAMPING * slip_rate - strength * inverse_sinh(scaled)
        derivative = -DAMPING - strength * factor / jnp.sqrt(1.0 + scaled * scaled)
        slip_rate = slip_rate - misfit / derivative
    next_state = state_now + TIME_STEP * state_rate * jnp.tanh(
        jnp.exp(-state_now) - jnp.abs(slip_rate)
    )
    return slip_rate, next_state


def split_stress(even, odd):
    low = lax.broadcasted_iota(jnp.int32, even.shape, 1) < HALF
    shear = jnp.where(low, even, pltpu.roll(odd, HALF, 1))
    normal = jnp.where(low, pltpu.roll(even, HALF, 1), odd)
    return shear, normal


def encode(partial):
    scaled = partial * (1.0 / MESSAGE_SCALE)
    return (scaled * scaled * scaled).astype(jnp.bfloat16)


def decode(message):
    cube = message.astype(jnp.float32)
    magnitude = jnp.abs(cube)
    root = jnp.exp2(jnp.log2(jnp.maximum(magnitude, 1e-38)) * (1.0 / 3.0)) * MESSAGE_SCALE
    root = jnp.where(cube < 0.0, -root, root)
    return jnp.where(magnitude > 0.0, root, 0.0)


def pack_messages(send, partials, own_blocks, n_dest, dups):
    for dest in range(n_dest):
        for tile in range(own_blocks // ROWS):
            piece = encode(partials(dest * own_blocks + tile * ROWS, ROWS))
            for dup in range(dups):
                send[dest * dups + dup, :, tile * LANES:(tile + 1) * LANES] = piece


def sum_messages(recv, total, own_blocks, n_src, owners):
    for owner in range(owners):
        part = decode(recv[owner])
        for src in range(1, n_src):
            part = part + decode(recv[src * owners + owner])
        for tile in range(own_blocks // ROWS):
            first = owner * own_blocks + tile * ROWS
            total[first:first + ROWS, :] = part[:, tile * LANES:(tile + 1) * LANES]
    pairs = owners * own_blocks // 2
    return total[pl.ds(0, pairs, stride=2), :], total[pl.ds(1, pairs, stride=2), :]


def make_tables(rows, cols, scales, gather, scatter, weights):
    slots = rows.shape[-1]
    lane = lax.broadcasted_iota(jnp.int32, (SLOT_ROWS, LANES), 1)
    diagonal = lax.broadcasted_iota(jnp.int32, (SLOT_ROWS, LANES), 0) == lane
    rest = jnp.full((1, LANES - slots), -1.0, jnp.float32)

    def widened(values):
        return jnp.concatenate([values.astype(jnp.float32), rest], axis=1)

    def column(values):
        spread = jnp.where(diagonal, jnp.broadcast_to(values, diagonal.shape), 0.0)
        return jnp.sum(spread, axis=1, keepdims=True)

    one_row = lax.broadcasted_iota(jnp.int32, (1, LANES), 1)
    block = lax.broadcasted_iota(jnp.int32, (scatter.shape[1], LANES), 0).astype(jnp.float32)
    for lag in range(STEPS - 1):
        row_ids = widened(rows[lag, 0])
        for part in range(1, PARTS):
            at = one_row >= part * SLOT_ROWS
            row_ids = jnp.where(at, pltpu.roll(widened(rows[lag, 0]), part * SLOT_ROWS, 1), row_ids)
        row_ids = jnp.where(one_row < PARTS * SLOT_ROWS, row_ids, -1.0)
        scatter[lag] = (block == row_ids).astype(jnp.float32).astype(jnp.bfloat16)
        picks = column(widened(cols[lag, 0])) == lane.astype(jnp.float32)
        gather[lag] = picks.astype(jnp.float32).astype(jnp.bfloat16)
        weights[lag] = jnp.broadcast_to(column(widened(scales[lag, 0])), weights.shape[1:])


def older_kernel(
    panels, history, rows_in, cols_in, scales_in,
    send, rest, guess, recent, gather, scatter, weights,
    panel_buf, history_buf, rows, cols, scales, rows_now, cols_now, scales_now, sources, acc,
    sems, small_sems, out_sem,
    *, lags, slots, n_src, n_rcv, own_blocks,
):
    src_blocks = n_rcv * own_blocks
    recv_blocks = n_src * own_blocks
    recent_lags = pl.ds(0, STEPS - 1)
    smalls = [
        pltpu.make_async_copy(source, target, small_sems.at[at])
        for at, (source, target) in enumerate([
            (history, history_buf), (cols_in, cols), (rows_in, rows), (scales_in, scales),
            (rows_in.at[recent_lags], rows_now), (cols_in.at[recent_lags], cols_now),
            (scales_in.at[recent_lags], scales_now),
        ])
    ]

    def panel_copy(lag):
        return pltpu.make_async_copy(panels.at[lag], panel_buf.at[lag], sems.at[lag])

    for copy in smalls:
        copy.start()
    for lag in range(IN_FLIGHT):
        panel_copy(lag).start()
    acc[...] = jnp.zeros_like(acc)
    tail = jnp.zeros((TAPS - lags, LANES), jnp.float32)
    sources[0:LEAD, :] = jnp.zeros((LEAD, LANES), jnp.float32)
    smalls[0].wait()
    for pair in range(src_blocks // 2):
        tile = history_buf[:, pair * LANES:(pair + 1) * LANES].astype(jnp.float32)
        for half in range(2):
            base = LEAD + (2 * pair + half) * TAPS
            sources[base:base + lags, :] = tile if half == 0 else pltpu.roll(tile, HALF, 1)
            sources[base + lags:base + TAPS, :] = tail
    for copy in smalls[1:]:
        copy.wait()
    make_tables(rows_now, cols_now, scales_now, gather, scatter, weights)

    top = lax.broadcasted_iota(jnp.int32, (8, LANES), 0) < STEPS
    match = top == (lax.broadcasted_iota(jnp.int32, (8, LANES), 1) < HALF)
    zero = jnp.zeros((8, LANES), jnp.float32)

    def one_lag(lag, carry):
        panel_copy(lag).wait()

        @pl.when(lag + IN_FLIGHT < lags)
        def _():
            panel_copy(lag + IN_FLIGHT).start()

        first_tap = LEAD + (lags - 1) - lag
        for group in range(0, slots, GROUP):
            pairs = []
            for slot in range(group, group + GROUP, 2):
                low = sources[pl.ds(cols[lag, 0, 0, slot] * TAPS + first_tap, 8), :]
                partner = cols[lag, 0, 0, slot + 1] ^ 1
                high = sources[pl.ds(partner * TAPS + first_tap - STEPS, 8), :]
                pairs.append(jnp.where(match, jnp.where(top, low, high), 0.0))
            columns = [
                jnp.concatenate([pair if at == to else zero for at in range(len(pairs))], axis=0)
                for to, pair in enumerate(pairs)
            ]
            picked = jnp.concatenate(columns, axis=1).astype(jnp.bfloat16)
            panel = panel_buf[lag, group:group + GROUP].reshape(GROUP * HALF, LANES)
            terms = jnp.dot(picked, panel, preferred_element_type=jnp.float32)
            for pair in range(len(pairs)):
                slot = group + 2 * pair
                scale = jnp.where(top, scales[lag, 0, 0, slot], scales[lag, 0, 0, slot + 1])
                term = terms[8 * pair:8 * pair + 8] * scale
                for part, addend in enumerate([jnp.where(top, term, 0.0), jnp.where(top, 0.0, term)]):
                    at = pl.ds(pl.multiple_of(rows[lag, 0, 0, slot + part] * 8, 8), 8)
                    acc[at, :] = acc[at, :] + addend
        return carry

    lax.fori_loop(0, lags, one_lag, 0)
    handed_on = pltpu.make_async_copy(panel_buf.at[recent_lags], recent, out_sem)
    handed_on.start()

    def partials(first_row, count, step):
        low, high = [
            acc[pl.ds(first_row * 8 + start, count, stride=8), :] for start in (step, STEPS + step)
        ]
        return low + high

    pack_messages(send, lambda first, count: partials(first, count, 0), own_blocks, n_src, n_rcv)
    for step in range(1, STEPS):
        rest[step - 1] = partials(0, recv_blocks, step)
    guess[...] = sources[pl.ds(LEAD + lags - 1, src_blocks // 2, stride=2 * TAPS), :]
    handed_on.wait()


def spread_sources(slip_rate, sources):
    pairs = slip_rate.shape[0]
    low = lax.broadcasted_iota(jnp.int32, slip_rate.shape, 1) < HALF
    turned = pltpu.roll(slip_rate, HALF, 1)
    sources[pl.ds(0, pairs, stride=2), :] = jnp.where(low, slip_rate, turned)
    sources[pl.ds(1, pairs, stride=2), :] = jnp.where(low, turned, slip_rate)


def new_terms(lag, panels, sources, gather, scatter, weights):
    slots, width, wide = panels.shape[1:]
    rounded = sources[...].astype(jnp.bfloat16)
    picked = jnp.dot(gather[lag][:, :rounded.shape[0]], rounded, preferred_element_type=jnp.float32)
    lane = lax.broadcasted_iota(jnp.int32, picked.shape, 1)
    row = lax.broadcasted_iota(jnp.int32, picked.shape, 0)
    first = row - jnp.where(lane < HALF, 0, 1)
    tiles = [
        jnp.where(first == slot, picked, 0.0).astype(jnp.bfloat16) for slot in range(0, slots, 2)
    ]
    panel = panels[lag].reshape(slots * width, wide)
    terms = jnp.dot(jnp.concatenate(tiles, axis=1), panel, preferred_element_type=jnp.float32)
    left = terms * weights[lag]
    parts = []
    for part in range(PARTS):
        parts.append(left.astype(jnp.bfloat16))
        left = left - parts[-1].astype(jnp.float32)
    stacked = jnp.concatenate(parts, axis=0)
    return jnp.dot(scatter[lag][:, :stacked.shape[0]], stacked, preferred_element_type=jnp.float32)


def step_kernel(
    recv, fields, guess, state_in, rest, panels, gather, scatter, weights,
    send, slip_out, state_out, *refs, step_no, n_src, n_rcv, own_blocks, dups, later,
):
    rest_out, (total, sources, acc) = refs[:-3], refs[-3:]
    shear, normal = split_stress(*sum_messages(recv, total, own_blocks, n_src, n_rcv))
    slip_rate, next_state = friction_solve(
        shear, normal, step_no, guess[...], state_in[...], [fields[kind] for kind in range(4)]
    )
    spread_sources(slip_rate, sources)
    acc[...] = rest[0] + new_terms(0, panels, sources, gather, scatter, weights)
    pack_messages(send, lambda first, count: acc[pl.ds(first, count), :], own_blocks, n_src, dups)
    slip_out[...] = slip_rate
    state_out[...] = next_state
    for at in range(later):
        terms = new_terms(at + 1, panels, sources, gather, scatter, weights)
        rest_out[0][at] = rest[at + 1] + terms


def last_kernel(
    recv, shear_pre, sigma_pre, friction_a, state_rate, state_in, *refs, step_no, n_src,
):
    slips, (slip_out, state_out, total) = refs[:step_no], refs[step_no:]
    pairs = slip_out.shape[1] // LANES
    mine = pl.ds(lax.axis_index("rcv") * pairs, pairs)
    shear, normal = split_stress(*sum_messages(recv, total, 2 * pairs, n_src, 1))
    fields = [ref[...] for ref in (shear_pre, sigma_pre, friction_a, state_rate)]
    slip_rate, next_state = friction_solve(
        shear, normal, step_no, slips[-1][mine, :], state_in[mine, :], fields
    )
    for step, field in enumerate([ref[mine, :] for ref in slips] + [slip_rate]):
        for row in range(pairs):
            slip_out[step:step + 1, row * LANES:(row + 1) * LANES] = field[row:row + 1]
    state_out[...] = next_state


def per_device(
    history, kernel, scales, block_rows, block_cols,
    shear_pre, sigma_pre, friction_a, state_rate, state_init,
):
    lags = kernel.shape[0]
    slots = kernel.shape[3]
    width = kernel.shape[4]
    n_src = lax.axis_size("src")
    n_rcv = lax.axis_size("rcv")
    own = shear_pre.shape[0]
    own_blocks = own // width
    pairs = own // LANES
    src_blocks = n_rcv * own_blocks
    recv_rows = n_src * own_blocks
    message = (ROWS, own_blocks // ROWS * LANES)
    panels = kernel.reshape(lags, slots, width, 2 * width)
    f32 = jnp.float32
    hbm = pl.BlockSpec(memory_space=pltpu.HBM)
    vmem = pl.BlockSpec(memory_space=pltpu.VMEM)
    sizes = dict(slots=slots, n_src=n_src, n_rcv=n_rcv, own_blocks=own_blocks)
    def shape(*dims, dtype=f32):
        return jax.ShapeDtypeStruct(dims, dtype)

    def call(body, ins, outs, scratch, name, args, flops, limit=VMEM_LIMIT):
        return pl.pallas_call(
            body, in_specs=ins, out_specs=[vmem] * len(outs), out_shape=outs, scratch_shapes=scratch,
            compiler_params=pltpu.CompilerParams(vmem_limit_bytes=limit), name=name,
            cost_estimate=pl.CostEstimate(flops=flops, bytes_accessed=flops // 64, transcendentals=0),
        )(*args)

    own_fields = [
        field.reshape(pairs, LANES)
        for field in (shear_pre, sigma_pre, friction_a, state_rate, state_init)
    ]
    fields = lax.all_gather(jnp.stack(own_fields), "rcv", axis=1, tiled=True)

    panels, history, *table = [
        pltpu.with_memory_space_constraint(array, pltpu.HBM)
        for array in (panels, history, block_rows, block_cols, scales)
    ]
    one_lag = 2 * slots * width * 2 * width * 8
    send, rest, guess, recent, *tables = call(
        functools.partial(older_kernel, lags=lags, **sizes),
        [hbm] * 5,
        [
            shape(n_src * n_rcv, *message, dtype=jnp.bfloat16),
            shape(STEPS - 1, recv_rows, LANES),
            shape(src_blocks // 2, LANES),
            shape(STEPS - 1, slots, width, 2 * width, dtype=panels.dtype),
            shape(STEPS - 1, SLOT_ROWS, LANES, dtype=jnp.bfloat16),
            shape(STEPS - 1, recv_rows, LANES, dtype=jnp.bfloat16),
            shape(STEPS - 1, SLOT_ROWS, LANES),
        ],
        [
            pltpu.VMEM(panels.shape, panels.dtype),
            pltpu.VMEM(history.shape, history.dtype),
            *[pltpu.SMEM(array.shape, array.dtype) for array in table],
            *[pltpu.VMEM((STEPS - 1, *array.shape[1:]), array.dtype) for array in table],
            pltpu.VMEM((LEAD + src_blocks * TAPS, LANES), f32),
            pltpu.VMEM((recv_rows * 8, LANES), f32),
            pltpu.SemaphoreType.DMA((lags,)),
            pltpu.SemaphoreType.DMA((7,)),
            pltpu.SemaphoreType.DMA,
        ],
        "older", [panels, history, *table], 60 * one_lag, limit=32 * 1024 * 1024,
    )

    state = fields[4]
    slips = []
    recv = lax.all_to_all(send, ("src", "rcv"), 0, 0, tiled=True)
    for step_no in range(STEPS - 1):
        last = step_no == STEPS - 2
        dups = 1 if last else n_rcv
        later = STEPS - 2 - step_no
        send, slip_rate, state, *rest_out = call(
            functools.partial(
                step_kernel, step_no=step_no, dups=dups, later=later,
                n_src=n_src, n_rcv=n_rcv, own_blocks=own_blocks,
            ),
            [vmem] * 9,
            [
                shape(n_src * dups, *message, dtype=jnp.bfloat16),
                shape(src_blocks // 2, LANES),
                shape(src_blocks // 2, LANES),
            ] + [shape(later, recv_rows, LANES)] * bool(later),
            [
                pltpu.VMEM((src_blocks, LANES), f32),
                pltpu.VMEM((src_blocks, LANES), f32),
                pltpu.VMEM((recv_rows, LANES), f32),
            ],
            "step", [recv, fields, guess, state, rest, recent, *tables], one_lag,
        )
        guess = slip_rate
        rest = rest_out[0] if later else rest
        slips.append(slip_rate)
        recv = lax.all_to_all(send, "src" if last else ("src", "rcv"), 0, 0, tiled=True)

    slip_rates, state = call(
        functools.partial(last_kernel, step_no=STEPS - 1, n_src=n_src),
        [vmem] * (6 + len(slips)),
        [shape(STEPS, own), shape(pairs, LANES)],
        [pltpu.VMEM((own_blocks, LANES), f32)],
        "last", [recv, *own_fields[:4], state, *slips], 10 ** 6,
    )
    return (slip_rates, state.reshape(own))


def solution(mesh):
    return jax.shard_map(
        per_device,
        mesh=mesh,
        in_specs=(
            P(None, "src"),
            P(None, "src", "rcv", None, None, None),
            P(None, "src", "rcv", None),
            P(None, "src", "rcv", None),
            P(None, "src", "rcv", None),
            P(("src", "rcv")),
            P(("src", "rcv")),
            P(("src", "rcv")),
            P(("src", "rcv")),
            P(("src", "rcv")),
        ),
        out_specs=(P(None, ("src", "rcv")), P(("src", "rcv"))),
        check_vma=False,
    )
```

```python
import functools

import jax
import jax.numpy as jnp
from jax import lax
from jax.experimental import pallas as pl
from jax.experimental.pallas import tpu as pltpu
from jax.sharding import PartitionSpec as P

STEPS = 4
NEWTON_ITERS = 4
DAMPING = 1.0
LOADING = 0.05
TIME_STEP = 0.2
LANES = 128
HALF = LANES // 2
ROWS = 4
IN_FLIGHT = 5
GROUP = 4
SLOT_ROWS = 32
PARTS = 3
MESSAGE_SCALE = 2.0 ** 22
TAPS = 24
LEAD = 8
VMEM_LIMIT = 16 * 1024 * 1024


def inverse_sinh(value):
    magnitude = jnp.abs(value)
    result = jnp.log(magnitude + jnp.sqrt(1.0 + magnitude * magnitude))
    return jnp.where(value < 0.0, -result, result)


def friction_solve(shear, normal_stress, step_no, guess, state_now, fields):
    shear_pre, sigma_pre, friction_a, state_rate = fields
    shear_total = shear + shear_pre + LOADING * (step_no + 1)
    normal = sigma_pre * (1.0 + 0.5 * jnp.tanh(normal_stress))
    strength = friction_a * normal
    factor = 0.5 * jnp.exp(state_now)
    slip_rate = guess
    for attempt in range(NEWTON_ITERS):
        scaled = slip_rate * factor
        misfit = shear_total - DAMPING * slip_rate - strength * inverse_sinh(scaled)
        derivative = -DAMPING - strength * factor / jnp.sqrt(1.0 + scaled * scaled)
        slip_rate = slip_rate - misfit / derivative
    next_state = state_now + TIME_STEP * state_rate * jnp.tanh(
        jnp.exp(-state_now) - jnp.abs(slip_rate)
    )
    return slip_rate, next_state


def split_stress(even, odd):
    low = lax.broadcasted_iota(jnp.int32, even.shape, 1) < HALF
    shear = jnp.where(low, even, pltpu.roll(odd, HALF, 1))
    normal = jnp.where(low, pltpu.roll(even, HALF, 1), odd)
    return shear, normal


def encode(partial):
    scaled = partial * (1.0 / MESSAGE_SCALE)
    return (scaled * scaled * scaled).astype(jnp.bfloat16)


def decode(message):
    cube = message.astype(jnp.float32)
    magnitude = jnp.abs(cube)
    root = jnp.exp2(jnp.log2(jnp.maximum(magnitude, 1e-38)) * (1.0 / 3.0)) * MESSAGE_SCALE
    root = jnp.where(cube < 0.0, -root, root)
    return jnp.where(magnitude > 0.0, root, 0.0)


def pack_messages(send, partials, own_blocks, n_dest, dups):
    for dest in range(n_dest):
        for tile in range(own_blocks // ROWS):
            piece = encode(partials(dest * own_blocks + tile * ROWS, ROWS))
            for dup in range(dups):
                send[dest * dups + dup, :, tile * LANES:(tile + 1) * LANES] = piece


def sum_messages(recv, total, own_blocks, n_src, owners):
    for owner in range(owners):
        part = decode(recv[owner])
        for src in range(1, n_src):
            part = part + decode(recv[src * owners + owner])
        for tile in range(own_blocks // ROWS):
            first = owner * own_blocks + tile * ROWS
            total[first:first + ROWS, :] = part[:, tile * LANES:(tile + 1) * LANES]
    pairs = owners * own_blocks // 2
    return total[pl.ds(0, pairs, stride=2), :], total[pl.ds(1, pairs, stride=2), :]


def make_tables(rows, cols, scales, gather, scatter, weights):
    slots = rows.shape[-1]
    lane = lax.broadcasted_iota(jnp.int32, (SLOT_ROWS, LANES), 1)
    diagonal = lax.broadcasted_iota(jnp.int32, (SLOT_ROWS, LANES), 0) == lane
    rest = jnp.full((1, LANES - slots), -1.0, jnp.float32)

    def widened(values):
        return jnp.concatenate([values.astype(jnp.float32), rest], axis=1)

    def column(values):
        spread = jnp.where(diagonal, jnp.broadcast_to(values, diagonal.shape), 0.0)
        return jnp.sum(spread, axis=1, keepdims=True)

    one_row = lax.broadcasted_iota(jnp.int32, (1, LANES), 1)
    block = lax.broadcasted_iota(jnp.int32, (scatter.shape[1], LANES), 0).astype(jnp.float32)
    for lag in range(STEPS - 1):
        row_ids = widened(rows[lag, 0])
        for part in range(1, PARTS):
            at = one_row >= part * SLOT_ROWS
            row_ids = jnp.where(at, pltpu.roll(widened(rows[lag, 0]), part * SLOT_ROWS, 1), row_ids)
        row_ids = jnp.where(one_row < PARTS * SLOT_ROWS, row_ids, -1.0)
        scatter[lag] = (block == row_ids).astype(jnp.float32).astype(jnp.bfloat16)
        picks = column(widened(cols[lag, 0])) == lane.astype(jnp.float32)
        gather[lag] = picks.astype(jnp.float32).astype(jnp.bfloat16)
        weights[lag] = jnp.broadcast_to(column(widened(scales[lag, 0])), weights.shape[1:])


def older_kernel(
    panels, history, rows_in, cols_in, scales_in,
    send, rest, guess, recent, gather, scatter, weights,
    panel_buf, history_buf, rows, cols, scales, rows_now, cols_now, scales_now, sources, acc, messages,
    sems, small_sems, out_sems,
    *, lags, slots, n_src, n_rcv, own_blocks,
):
    src_blocks = n_rcv * own_blocks
    recv_blocks = n_src * own_blocks
    recent_lags = pl.ds(0, STEPS - 1)
    smalls = [
        pltpu.make_async_copy(source, target, small_sems.at[at])
        for at, (source, target) in enumerate([
            (history, history_buf), (cols_in, cols), (rows_in, rows), (scales_in, scales),
            (rows_in.at[recent_lags], rows_now), (cols_in.at[recent_lags], cols_now),
            (scales_in.at[recent_lags], scales_now),
        ])
    ]

    def panel_copy(lag):
        return pltpu.make_async_copy(panels.at[lag], panel_buf.at[lag], sems.at[lag])

    for copy in smalls:
        copy.start()
    for lag in range(IN_FLIGHT):
        panel_copy(lag).start()
    acc[...] = jnp.zeros_like(acc)
    tail = jnp.zeros((TAPS - lags, LANES), jnp.float32)
    sources[0:LEAD, :] = jnp.zeros((LEAD, LANES), jnp.float32)
    smalls[0].wait()
    for pair in range(src_blocks // 2):
        tile = history_buf[:, pair * LANES:(pair + 1) * LANES].astype(jnp.float32)
        for half in range(2):
            base = LEAD + (2 * pair + half) * TAPS
            sources[base:base + lags, :] = tile if half == 0 else pltpu.roll(tile, HALF, 1)
            sources[base + lags:base + TAPS, :] = tail
    for copy in smalls[1:]:
        copy.wait()
    top = lax.broadcasted_iota(jnp.int32, (8, LANES), 0) < STEPS
    match = top == (lax.broadcasted_iota(jnp.int32, (8, LANES), 1) < HALF)
    zero = jnp.zeros((8, LANES), jnp.float32)

    def one_lag(lag, carry):
        panel_copy(lag).wait()

        @pl.when(lag + IN_FLIGHT < lags)
        def _():
            panel_copy(lag + IN_FLIGHT).start()

        first_tap = LEAD + (lags - 1) - lag
        for group in range(0, slots, GROUP):
            pairs = []
            for slot in range(group, group + GROUP, 2):
                low = sources[pl.ds(cols[lag, 0, 0, slot] * TAPS + first_tap, 8), :]
                partner = cols[lag, 0, 0, slot + 1] ^ 1
                high = sources[pl.ds(partner * TAPS + first_tap - STEPS, 8), :]
                pairs.append(jnp.where(match, jnp.where(top, low, high), 0.0))
            columns = [
                jnp.concatenate([pair if at == to else zero for at in range(len(pairs))], axis=0)
                for to, pair in enumerate(pairs)
            ]
            picked = jnp.concatenate(columns, axis=1).astype(jnp.bfloat16)
            panel = panel_buf[lag, group:group + GROUP].reshape(GROUP * HALF, LANES)
            terms = jnp.dot(picked, panel, preferred_element_type=jnp.float32)
            for pair in range(len(pairs)):
                slot = group + 2 * pair
                scale = jnp.where(top, scales[lag, 0, 0, slot], scales[lag, 0, 0, slot + 1])
                term = terms[8 * pair:8 * pair + 8] * scale
                for part, addend in enumerate([jnp.where(top, term, 0.0), jnp.where(top, 0.0, term)]):
                    at = pl.ds(pl.multiple_of(rows[lag, 0, 0, slot + part] * 8, 8), 8)
                    acc[at, :] = acc[at, :] + addend
        return carry

    lax.fori_loop(0, lags, one_lag, 0)
    def partials(first_row, count, step):
        low, high = [
            acc[pl.ds(first_row * 8 + start, count, stride=8), :] for start in (step, STEPS + step)
        ]
        return low + high

    pack_messages(messages, lambda first, count: partials(first, count, 0), own_blocks, n_src, 1)
    outgoing = [
        pltpu.make_async_copy(messages, send.at[:, dup], out_sems.at[dup]) for dup in range(n_rcv)
    ]
    outgoing.append(pltpu.make_async_copy(panel_buf.at[recent_lags], recent, out_sems.at[n_rcv]))
    for copy in outgoing:
        copy.start()
    make_tables(rows_now, cols_now, scales_now, gather, scatter, weights)
    for step in range(1, STEPS):
        rest[step - 1] = partials(0, recv_blocks, step)
    guess[...] = sources[pl.ds(LEAD + lags - 1, src_blocks // 2, stride=2 * TAPS), :]
    for copy in outgoing:
        copy.wait()


def spread_sources(slip_rate, sources):
    pairs = slip_rate.shape[0]
    low = lax.broadcasted_iota(jnp.int32, slip_rate.shape, 1) < HALF
    turned = pltpu.roll(slip_rate, HALF, 1)
    sources[pl.ds(0, pairs, stride=2), :] = jnp.where(low, slip_rate, turned)
    sources[pl.ds(1, pairs, stride=2), :] = jnp.where(low, turned, slip_rate)


def new_terms(lag, panels, sources, gather, scatter, weights):
    slots, width, wide = panels.shape[1:]
    rounded = sources[...].astype(jnp.bfloat16)
    picked = jnp.dot(gather[lag][:, :rounded.shape[0]], rounded, preferred_element_type=jnp.float32)
    lane = lax.broadcasted_iota(jnp.int32, picked.shape, 1)
    row = lax.broadcasted_iota(jnp.int32, picked.shape, 0)
    first = row - jnp.where(lane < HALF, 0, 1)
    tiles = [
        jnp.where(first == slot, picked, 0.0).astype(jnp.bfloat16) for slot in range(0, slots, 2)
    ]
    panel = panels[lag].reshape(slots * width, wide)
    terms = jnp.dot(jnp.concatenate(tiles, axis=1), panel, preferred_element_type=jnp.float32)
    left = terms * weights[lag]
    parts = []
    for part in range(PARTS):
        parts.append(left.astype(jnp.bfloat16))
        left = left - parts[-1].astype(jnp.float32)
    stacked = jnp.concatenate(parts, axis=0)
    return jnp.dot(scatter[lag][:, :stacked.shape[0]], stacked, preferred_element_type=jnp.float32)


def step_kernel(
    recv, fields, guess, state_in, rest, panels, gather, scatter, weights,
    send, slip_out, state_out, *refs, step_no, n_src, n_rcv, own_blocks, dups, later,
):
    rest_out, (total, sources, acc) = refs[:-3], refs[-3:]
    shear, normal = split_stress(*sum_messages(recv, total, own_blocks, n_src, n_rcv))
    slip_rate, next_state = friction_solve(
        shear, normal, step_no, guess[...], state_in[...], [fields[kind] for kind in range(4)]
    )
    spread_sources(slip_rate, sources)
    acc[...] = rest[0] + new_terms(0, panels, sources, gather, scatter, weights)
    pack_messages(send, lambda first, count: acc[pl.ds(first, count), :], own_blocks, n_src, dups)
    slip_out[...] = slip_rate
    state_out[...] = next_state
    for at in range(later):
        terms = new_terms(at + 1, panels, sources, gather, scatter, weights)
        rest_out[0][at] = rest[at + 1] + terms


def last_kernel(
    recv, shear_pre, sigma_pre, friction_a, state_rate, state_in, *refs, step_no, n_src,
):
    slips, (slip_out, state_out, total) = refs[:step_no], refs[step_no:]
    pairs = slip_out.shape[1] // LANES
    mine = pl.ds(lax.axis_index("rcv") * pairs, pairs)
    shear, normal = split_stress(*sum_messages(recv, total, 2 * pairs, n_src, 1))
    fields = [ref[...] for ref in (shear_pre, sigma_pre, friction_a, state_rate)]
    slip_rate, next_state = friction_solve(
        shear, normal, step_no, slips[-1][mine, :], state_in[mine, :], fields
    )
    for step, field in enumerate([ref[mine, :] for ref in slips] + [slip_rate]):
        for row in range(pairs):
            slip_out[step:step + 1, row * LANES:(row + 1) * LANES] = field[row:row + 1]
    state_out[...] = next_state


def per_device(
    history, kernel, scales, block_rows, block_cols,
    shear_pre, sigma_pre, friction_a, state_rate, state_init,
):
    lags = kernel.shape[0]
    slots = kernel.shape[3]
    width = kernel.shape[4]
    n_src = lax.axis_size("src")
    n_rcv = lax.axis_size("rcv")
    own = shear_pre.shape[0]
    own_blocks = own // width
    pairs = own // LANES
    src_blocks = n_rcv * own_blocks
    recv_rows = n_src * own_blocks
    message = (ROWS, own_blocks // ROWS * LANES)
    panels = kernel.reshape(lags, slots, width, 2 * width)
    f32 = jnp.float32
    hbm = pl.BlockSpec(memory_space=pltpu.HBM)
    vmem = pl.BlockSpec(memory_space=pltpu.VMEM)
    sizes = dict(slots=slots, n_src=n_src, n_rcv=n_rcv, own_blocks=own_blocks)
    def shape(*dims, dtype=f32):
        return jax.ShapeDtypeStruct(dims, dtype)

    def call(body, ins, outs, scratch, name, args, flops, limit=VMEM_LIMIT, out_specs=None):
        return pl.pallas_call(
            body, in_specs=ins, out_specs=out_specs or [vmem] * len(outs), out_shape=outs, scratch_shapes=scratch,
            compiler_params=pltpu.CompilerParams(vmem_limit_bytes=limit), name=name,
            cost_estimate=pl.CostEstimate(flops=flops, bytes_accessed=flops // 64, transcendentals=0),
        )(*args)

    own_fields = [
        field.reshape(pairs, LANES)
        for field in (shear_pre, sigma_pre, friction_a, state_rate, state_init)
    ]
    fields = lax.all_gather(jnp.stack(own_fields), "rcv", axis=1, tiled=True)

    panels, history, *table = [
        pltpu.with_memory_space_constraint(array, pltpu.HBM)
        for array in (panels, history, block_rows, block_cols, scales)
    ]
    one_lag = 2 * slots * width * 2 * width * 8
    send, rest, guess, recent, *tables = call(
        functools.partial(older_kernel, lags=lags, **sizes),
        [hbm] * 5,
        [
            shape(n_src, n_rcv, *message, dtype=jnp.bfloat16),
            shape(STEPS - 1, recv_rows, LANES),
            shape(src_blocks // 2, LANES),
            shape(STEPS - 1, slots, width, 2 * width, dtype=panels.dtype),
            shape(STEPS - 1, SLOT_ROWS, LANES, dtype=jnp.bfloat16),
            shape(STEPS - 1, recv_rows, LANES, dtype=jnp.bfloat16),
            shape(STEPS - 1, SLOT_ROWS, LANES),
        ],
        [
            pltpu.VMEM(panels.shape, panels.dtype),
            pltpu.VMEM(history.shape, history.dtype),
            *[pltpu.SMEM(array.shape, array.dtype) for array in table],
            *[pltpu.VMEM((STEPS - 1, *array.shape[1:]), array.dtype) for array in table],
            pltpu.VMEM((LEAD + src_blocks * TAPS, LANES), f32),
            pltpu.VMEM((recv_rows * 8, LANES), f32),
            pltpu.VMEM((n_src, *message), jnp.bfloat16),
            pltpu.SemaphoreType.DMA((lags,)),
            pltpu.SemaphoreType.DMA((7,)),
            pltpu.SemaphoreType.DMA((n_rcv + 1,)),
        ],
        "older", [panels, history, *table], 60 * one_lag, limit=32 * 1024 * 1024,
        out_specs=[hbm] + [vmem] * 6,
    )

    state = fields[4]
    slips = []
    recv = lax.all_to_all(send.reshape(n_src * n_rcv, *message), ("src", "rcv"), 0, 0, tiled=True)
    for step_no in range(STEPS - 1):
        last = step_no == STEPS - 2
        dups = 1 if last else n_rcv
        later = STEPS - 2 - step_no
        send, slip_rate, state, *rest_out = call(
            functools.partial(
                step_kernel, step_no=step_no, dups=dups, later=later,
                n_src=n_src, n_rcv=n_rcv, own_blocks=own_blocks,
            ),
            [vmem] * 9,
            [
                shape(n_src * dups, *message, dtype=jnp.bfloat16),
                shape(src_blocks // 2, LANES),
                shape(src_blocks // 2, LANES),
            ] + [shape(later, recv_rows, LANES)] * bool(later),
            [
                pltpu.VMEM((src_blocks, LANES), f32),
                pltpu.VMEM((src_blocks, LANES), f32),
                pltpu.VMEM((recv_rows, LANES), f32),
            ],
            "step", [recv, fields, guess, state, rest, recent, *tables], one_lag,
        )
        guess = slip_rate
        rest = rest_out[0] if later else rest
        slips.append(slip_rate)
        recv = lax.all_to_all(send, "src" if last else ("src", "rcv"), 0, 0, tiled=True)

    slip_rates, state = call(
        functools.partial(last_kernel, step_no=STEPS - 1, n_src=n_src),
        [vmem] * (6 + len(slips)),
        [shape(STEPS, own), shape(pairs, LANES)],
        [pltpu.VMEM((own_blocks, LANES), f32)],
        "last", [recv, *own_fields[:4], state, *slips], 10 ** 6,
    )
    return (slip_rates, state.reshape(own))


def solution(mesh):
    return jax.shard_map(
        per_device,
        mesh=mesh,
        in_specs=(
            P(None, "src"),
            P(None, "src", "rcv", None, None, None),
            P(None, "src", "rcv", None),
            P(None, "src", "rcv", None),
            P(None, "src", "rcv", None),
            P(("src", "rcv")),
            P(("src", "rcv")),
            P(("src", "rcv")),
            P(("src", "rcv")),
            P(("src", "rcv")),
        ),
        out_specs=(P(None, ("src", "rcv")), P(("src", "rcv"))),
        check_vma=False,
    )
```

```python
import functools

import jax
import jax.numpy as jnp
from jax import lax
from jax.experimental import pallas as pl
from jax.experimental.pallas import tpu as pltpu
from jax.sharding import PartitionSpec as P

STEPS = 4
NEWTON_ITERS = 4
DAMPING = 1.0
LOADING = 0.05
TIME_STEP = 0.2
LANES = 128
HALF = LANES // 2
ROWS = 4
IN_FLIGHT = 5
GROUP = 4
SLOT_ROWS = 32
PARTS = 3
MESSAGE_SCALE = 2.0 ** 22
TAPS = 24
LEAD = 8
VMEM_LIMIT = 16 * 1024 * 1024


def inverse_sinh(value):
    magnitude = jnp.abs(value)
    result = jnp.log(magnitude + jnp.sqrt(1.0 + magnitude * magnitude))
    return jnp.where(value < 0.0, -result, result)


def friction_solve(shear, normal_stress, step_no, guess, state_now, fields):
    shear_pre, sigma_pre, friction_a, state_rate = fields
    shear_total = shear + shear_pre + LOADING * (step_no + 1)
    normal = sigma_pre * (1.0 + 0.5 * jnp.tanh(normal_stress))
    strength = friction_a * normal
    factor = 0.5 * jnp.exp(state_now)
    slip_rate = guess
    for attempt in range(NEWTON_ITERS):
        scaled = slip_rate * factor
        misfit = shear_total - DAMPING * slip_rate - strength * inverse_sinh(scaled)
        derivative = -DAMPING - strength * factor / jnp.sqrt(1.0 + scaled * scaled)
        slip_rate = slip_rate - misfit / derivative
    next_state = state_now + TIME_STEP * state_rate * jnp.tanh(
        jnp.exp(-state_now) - jnp.abs(slip_rate)
    )
    return slip_rate, next_state


def split_stress(even, odd):
    low = lax.broadcasted_iota(jnp.int32, even.shape, 1) < HALF
    shear = jnp.where(low, even, pltpu.roll(odd, HALF, 1))
    normal = jnp.where(low, pltpu.roll(even, HALF, 1), odd)
    return shear, normal


def encode(partial):
    scaled = partial * (1.0 / MESSAGE_SCALE)
    return (scaled * scaled * scaled).astype(jnp.bfloat16)


def decode(message):
    cube = message.astype(jnp.float32)
    magnitude = jnp.abs(cube)
    root = jnp.exp2(jnp.log2(jnp.maximum(magnitude, 1e-38)) * (1.0 / 3.0)) * MESSAGE_SCALE
    root = jnp.where(cube < 0.0, -root, root)
    return jnp.where(magnitude > 0.0, root, 0.0)


def pack_messages(send, partials, own_blocks, n_dest, dups):
    for dest in range(n_dest):
        for tile in range(own_blocks // ROWS):
            piece = encode(partials(dest * own_blocks + tile * ROWS, ROWS))
            for dup in range(dups):
                send[dest * dups + dup, :, tile * LANES:(tile + 1) * LANES] = piece


def sum_messages(recv, total, own_blocks, n_src, owners):
    for owner in range(owners):
        part = decode(recv[owner])
        for src in range(1, n_src):
            part = part + decode(recv[src * owners + owner])
        for tile in range(own_blocks // ROWS):
            first = owner * own_blocks + tile * ROWS
            total[first:first + ROWS, :] = part[:, tile * LANES:(tile + 1) * LANES]
    pairs = owners * own_blocks // 2
    return total[pl.ds(0, pairs, stride=2), :], total[pl.ds(1, pairs, stride=2), :]


def make_tables(rows, cols, scales, gather, scatter, weights):
    slots = rows.shape[-1]
    lane = lax.broadcasted_iota(jnp.int32, (SLOT_ROWS, LANES), 1)
    diagonal = lax.broadcasted_iota(jnp.int32, (SLOT_ROWS, LANES), 0) == lane
    rest = jnp.full((1, LANES - slots), -1.0, jnp.float32)

    def widened(values):
        return jnp.concatenate([values.astype(jnp.float32), rest], axis=1)

    def column(values):
        spread = jnp.where(diagonal, jnp.broadcast_to(values, diagonal.shape), 0.0)
        return jnp.sum(spread, axis=1, keepdims=True)

    one_row = lax.broadcasted_iota(jnp.int32, (1, LANES), 1)
    block = lax.broadcasted_iota(jnp.int32, (scatter.shape[1], LANES), 0).astype(jnp.float32)
    for lag in range(STEPS - 1):
        row_ids = widened(rows[lag, 0])
        for part in range(1, PARTS):
            at = one_row >= part * SLOT_ROWS
            row_ids = jnp.where(at, pltpu.roll(widened(rows[lag, 0]), part * SLOT_ROWS, 1), row_ids)
        row_ids = jnp.where(one_row < PARTS * SLOT_ROWS, row_ids, -1.0)
        scatter[lag] = (block == row_ids).astype(jnp.float32).astype(jnp.bfloat16)
        picks = jnp.maximum(column(widened(cols[lag, 0])), 0.0).astype(jnp.int32)
        gather[lag] = jnp.broadcast_to(picks, gather.shape[1:])
        weights[lag] = jnp.broadcast_to(column(widened(scales[lag, 0])), weights.shape[1:])


def older_kernel(
    panels, history, rows_in, cols_in, scales_in,
    send, rest, guess, recent, gather, scatter, weights,
    panel_buf, history_buf, rows, cols, scales, rows_now, cols_now, scales_now, sources, acc, messages,
    sems, small_sems, out_sems,
    *, lags, slots, n_src, n_rcv, own_blocks,
):
    src_blocks = n_rcv * own_blocks
    recv_blocks = n_src * own_blocks
    recent_lags = pl.ds(0, STEPS - 1)
    smalls = [
        pltpu.make_async_copy(source, target, small_sems.at[at])
        for at, (source, target) in enumerate([
            (history, history_buf), (cols_in, cols), (rows_in, rows), (scales_in, scales),
            (rows_in.at[recent_lags], rows_now), (cols_in.at[recent_lags], cols_now),
            (scales_in.at[recent_lags], scales_now),
        ])
    ]

    def panel_copy(lag):
        return pltpu.make_async_copy(panels.at[lag], panel_buf.at[lag], sems.at[lag])

    for copy in smalls:
        copy.start()
    for lag in range(IN_FLIGHT):
        panel_copy(lag).start()
    acc[...] = jnp.zeros_like(acc)
    tail = jnp.zeros((TAPS - lags, LANES), jnp.float32)
    sources[0:LEAD, :] = jnp.zeros((LEAD, LANES), jnp.float32)
    smalls[0].wait()
    for pair in range(src_blocks // 2):
        tile = history_buf[:, pair * LANES:(pair + 1) * LANES].astype(jnp.float32)
        for half in range(2):
            base = LEAD + (2 * pair + half) * TAPS
            sources[base:base + lags, :] = tile if half == 0 else pltpu.roll(tile, HALF, 1)
            sources[base + lags:base + TAPS, :] = tail
    for copy in smalls[1:]:
        copy.wait()
    top = lax.broadcasted_iota(jnp.int32, (8, LANES), 0) < STEPS
    match = top == (lax.broadcasted_iota(jnp.int32, (8, LANES), 1) < HALF)
    zero = jnp.zeros((8, LANES), jnp.float32)

    def one_lag(lag, carry):
        panel_copy(lag).wait()

        @pl.when(lag + IN_FLIGHT < lags)
        def _():
            panel_copy(lag + IN_FLIGHT).start()

        first_tap = LEAD + (lags - 1) - lag
        for group in range(0, slots, GROUP):
            pairs = []
            for slot in range(group, group + GROUP, 2):
                low = sources[pl.ds(cols[lag, 0, 0, slot] * TAPS + first_tap, 8), :]
                partner = cols[lag, 0, 0, slot + 1] ^ 1
                high = sources[pl.ds(partner * TAPS + first_tap - STEPS, 8), :]
                pairs.append(jnp.where(match, jnp.where(top, low, high), 0.0))
            columns = [
                jnp.concatenate([pair if at == to else zero for at in range(len(pairs))], axis=0)
                for to, pair in enumerate(pairs)
            ]
            picked = jnp.concatenate(columns, axis=1).astype(jnp.bfloat16)
            panel = panel_buf[lag, group:group + GROUP].reshape(GROUP * HALF, LANES)
            terms = jnp.dot(picked, panel, preferred_element_type=jnp.float32)
            for pair in range(len(pairs)):
                slot = group + 2 * pair
                scale = jnp.where(top, scales[lag, 0, 0, slot], scales[lag, 0, 0, slot + 1])
                term = terms[8 * pair:8 * pair + 8] * scale
                for part, addend in enumerate([jnp.where(top, term, 0.0), jnp.where(top, 0.0, term)]):
                    at = pl.ds(pl.multiple_of(rows[lag, 0, 0, slot + part] * 8, 8), 8)
                    acc[at, :] = acc[at, :] + addend
        return carry

    lax.fori_loop(0, lags, one_lag, 0)
    def partials(first_row, count, step):
        low, high = [
            acc[pl.ds(first_row * 8 + start, count, stride=8), :] for start in (step, STEPS + step)
        ]
        return low + high

    pack_messages(messages, lambda first, count: partials(first, count, 0), own_blocks, n_src, 1)
    outgoing = [
        pltpu.make_async_copy(messages, send.at[:, dup], out_sems.at[dup]) for dup in range(n_rcv)
    ]
    outgoing.append(pltpu.make_async_copy(panel_buf.at[recent_lags], recent, out_sems.at[n_rcv]))
    for copy in outgoing:
        copy.start()
    make_tables(rows_now, cols_now, scales_now, gather, scatter, weights)
    for step in range(1, STEPS):
        rest[step - 1] = partials(0, recv_blocks, step)
    guess[...] = sources[pl.ds(LEAD + lags - 1, src_blocks // 2, stride=2 * TAPS), :]
    for copy in outgoing:
        copy.wait()


def spread_sources(slip_rate, sources):
    pairs = slip_rate.shape[0]
    low = lax.broadcasted_iota(jnp.int32, slip_rate.shape, 1) < HALF
    turned = pltpu.roll(slip_rate, HALF, 1)
    sources[pl.ds(0, pairs, stride=2), :] = jnp.where(low, slip_rate, turned)
    sources[pl.ds(1, pairs, stride=2), :] = jnp.where(low, turned, slip_rate)


def take_rows(groups, rows):
    taken = []
    for first in range(0, rows.shape[0], 8):
        row = rows[first:first + 8]
        within = row & 7
        block = row - within
        piece = jnp.zeros(groups[0].shape, jnp.float32)
        for at, group in enumerate(groups):
            found = jnp.take_along_axis(group, within, axis=0, mode="promise_in_bounds")
            piece = jnp.where(block == 8 * at, found, piece)
        taken.append(piece)
    return jnp.concatenate(taken, axis=0)


def new_terms(lags, panels, sources, gather, scatter, weights):
    slots, width, wide = panels.shape[1:]
    groups = [sources[at:at + 8, :] for at in range(0, sources.shape[0], 8)]
    picked = [take_rows(groups, gather[lag]) for lag in lags]
    lane = lax.broadcasted_iota(jnp.int32, picked[0].shape, 1)
    row = lax.broadcasted_iota(jnp.int32, picked[0].shape, 0)
    first = row - jnp.where(lane < HALF, 0, 1)
    terms = []
    for lag, rates in zip(lags, picked):
        tiles = [
            jnp.where(first == slot, rates, 0.0).astype(jnp.bfloat16) for slot in range(0, slots, 2)
        ]
        panel = panels[lag].reshape(slots * width, wide)
        terms.append(
            jnp.dot(jnp.concatenate(tiles, axis=1), panel, preferred_element_type=jnp.float32)
        )
    sums = []
    for lag, left in zip(lags, terms):
        left = left * weights[lag]
        parts = []
        for part in range(PARTS):
            parts.append(left.astype(jnp.bfloat16))
            left = left - parts[-1].astype(jnp.float32)
        stacked = jnp.concatenate(parts, axis=0)
        table = scatter[lag][:, :stacked.shape[0]]
        sums.append(jnp.dot(table, stacked, preferred_element_type=jnp.float32))
    return sums


def step_kernel(
    recv, fields, guess, state_in, rest, panels, gather, scatter, weights,
    send, slip_out, state_out, *refs, step_no, n_src, n_rcv, own_blocks, dups, later,
):
    rest_out, (total, sources, acc) = refs[:-3], refs[-3:]
    shear, normal = split_stress(*sum_messages(recv, total, own_blocks, n_src, n_rcv))
    slip_rate, next_state = friction_solve(
        shear, normal, step_no, guess[...], state_in[...], [fields[kind] for kind in range(4)]
    )
    spread_sources(slip_rate, sources)
    terms = new_terms(range(later + 1), panels, sources, gather, scatter, weights)
    acc[...] = rest[0] + terms[0]
    pack_messages(send, lambda first, count: acc[pl.ds(first, count), :], own_blocks, n_src, dups)
    slip_out[...] = slip_rate
    state_out[...] = next_state
    for at in range(later):
        rest_out[0][at] = rest[at + 1] + terms[at + 1]


def last_kernel(
    recv, shear_pre, sigma_pre, friction_a, state_rate, state_in, *refs, step_no, n_src,
):
    slips, (slip_out, state_out, total) = refs[:step_no], refs[step_no:]
    pairs = slip_out.shape[1] // LANES
    mine = pl.ds(lax.axis_index("rcv") * pairs, pairs)
    shear, normal = split_stress(*sum_messages(recv, total, 2 * pairs, n_src, 1))
    fields = [ref[...] for ref in (shear_pre, sigma_pre, friction_a, state_rate)]
    slip_rate, next_state = friction_solve(
        shear, normal, step_no, slips[-1][mine, :], state_in[mine, :], fields
    )
    for step, field in enumerate([ref[mine, :] for ref in slips] + [slip_rate]):
        for row in range(pairs):
            slip_out[step:step + 1, row * LANES:(row + 1) * LANES] = field[row:row + 1]
    state_out[...] = next_state


def per_device(
    history, kernel, scales, block_rows, block_cols,
    shear_pre, sigma_pre, friction_a, state_rate, state_init,
):
    lags = kernel.shape[0]
    slots = kernel.shape[3]
    width = kernel.shape[4]
    n_src = lax.axis_size("src")
    n_rcv = lax.axis_size("rcv")
    own = shear_pre.shape[0]
    own_blocks = own // width
    pairs = own // LANES
    src_blocks = n_rcv * own_blocks
    recv_rows = n_src * own_blocks
    message = (ROWS, own_blocks // ROWS * LANES)
    panels = kernel.reshape(lags, slots, width, 2 * width)
    f32 = jnp.float32
    hbm = pl.BlockSpec(memory_space=pltpu.HBM)
    vmem = pl.BlockSpec(memory_space=pltpu.VMEM)
    sizes = dict(slots=slots, n_src=n_src, n_rcv=n_rcv, own_blocks=own_blocks)
    def shape(*dims, dtype=f32):
        return jax.ShapeDtypeStruct(dims, dtype)

    def call(body, ins, outs, scratch, name, args, flops, limit=VMEM_LIMIT, out_specs=None):
        return pl.pallas_call(
            body, in_specs=ins, out_specs=out_specs or [vmem] * len(outs), out_shape=outs, scratch_shapes=scratch,
            compiler_params=pltpu.CompilerParams(vmem_limit_bytes=limit), name=name,
            cost_estimate=pl.CostEstimate(flops=flops, bytes_accessed=flops // 64, transcendentals=0),
        )(*args)

    own_fields = [
        field.reshape(pairs, LANES)
        for field in (shear_pre, sigma_pre, friction_a, state_rate, state_init)
    ]
    fields = lax.all_gather(jnp.stack(own_fields), "rcv", axis=1, tiled=True)

    panels, history, *table = [
        pltpu.with_memory_space_constraint(array, pltpu.HBM)
        for array in (panels, history, block_rows, block_cols, scales)
    ]
    one_lag = 2 * slots * width * 2 * width * 8
    send, rest, guess, recent, *tables = call(
        functools.partial(older_kernel, lags=lags, **sizes),
        [hbm] * 5,
        [
            shape(n_src, n_rcv, *message, dtype=jnp.bfloat16),
            shape(STEPS - 1, recv_rows, LANES),
            shape(src_blocks // 2, LANES),
            shape(STEPS - 1, slots, width, 2 * width, dtype=panels.dtype),
            shape(STEPS - 1, SLOT_ROWS, LANES, dtype=jnp.int32),
            shape(STEPS - 1, recv_rows, LANES, dtype=jnp.bfloat16),
            shape(STEPS - 1, SLOT_ROWS, LANES),
        ],
        [
            pltpu.VMEM(panels.shape, panels.dtype),
            pltpu.VMEM(history.shape, history.dtype),
            *[pltpu.SMEM(array.shape, array.dtype) for array in table],
            *[pltpu.VMEM((STEPS - 1, *array.shape[1:]), array.dtype) for array in table],
            pltpu.VMEM((LEAD + src_blocks * TAPS, LANES), f32),
            pltpu.VMEM((recv_rows * 8, LANES), f32),
            pltpu.VMEM((n_src, *message), jnp.bfloat16),
            pltpu.SemaphoreType.DMA((lags,)),
            pltpu.SemaphoreType.DMA((7,)),
            pltpu.SemaphoreType.DMA((n_rcv + 1,)),
        ],
        "older", [panels, history, *table], 60 * one_lag, limit=32 * 1024 * 1024,
        out_specs=[hbm] + [vmem] * 6,
    )

    state = fields[4]
    slips = []
    recv = lax.all_to_all(send.reshape(n_src * n_rcv, *message), ("src", "rcv"), 0, 0, tiled=True)
    for step_no in range(STEPS - 1):
        last = step_no == STEPS - 2
        dups = 1 if last else n_rcv
        later = STEPS - 2 - step_no
        send, slip_rate, state, *rest_out = call(
            functools.partial(
                step_kernel, step_no=step_no, dups=dups, later=later,
                n_src=n_src, n_rcv=n_rcv, own_blocks=own_blocks,
            ),
            [vmem] * 9,
            [
                shape(n_src * dups, *message, dtype=jnp.bfloat16),
                shape(src_blocks // 2, LANES),
                shape(src_blocks // 2, LANES),
            ] + [shape(later, recv_rows, LANES)] * bool(later),
            [
                pltpu.VMEM((src_blocks, LANES), f32),
                pltpu.VMEM((src_blocks, LANES), f32),
                pltpu.VMEM((recv_rows, LANES), f32),
            ],
            "step", [recv, fields, guess, state, rest, recent, *tables], one_lag,
        )
        guess = slip_rate
        rest = rest_out[0] if later else rest
        slips.append(slip_rate)
        recv = lax.all_to_all(send, "src" if last else ("src", "rcv"), 0, 0, tiled=True)

    slip_rates, state = call(
        functools.partial(last_kernel, step_no=STEPS - 1, n_src=n_src),
        [vmem] * (6 + len(slips)),
        [shape(STEPS, own), shape(pairs, LANES)],
        [pltpu.VMEM((own_blocks, LANES), f32)],
        "last", [recv, *own_fields[:4], state, *slips], 10 ** 6,
    )
    return (slip_rates, state.reshape(own))


def solution(mesh):
    return jax.shard_map(
        per_device,
        mesh=mesh,
        in_specs=(
            P(None, "src"),
            P(None, "src", "rcv", None, None, None),
            P(None, "src", "rcv", None),
            P(None, "src", "rcv", None),
            P(None, "src", "rcv", None),
            P(("src", "rcv")),
            P(("src", "rcv")),
            P(("src", "rcv")),
            P(("src", "rcv")),
            P(("src", "rcv")),
        ),
        out_specs=(P(None, ("src", "rcv")), P(("src", "rcv"))),
        check_vma=False,
    )
```

```python
import functools

import jax
import jax.numpy as jnp
from jax import lax
from jax.experimental import pallas as pl
from jax.experimental.pallas import tpu as pltpu
from jax.sharding import PartitionSpec as P

STEPS = 4
NEWTON_ITERS = 4
DAMPING = 1.0
LOADING = 0.05
TIME_STEP = 0.2
LANES = 128
HALF = LANES // 2
ROWS = 4
IN_FLIGHT = 5
GROUP = 4
SLOT_ROWS = 32
PARTS = 3
MESSAGE_SCALE = 2.0 ** 22
TAPS = 24
LEAD = 8
VMEM_LIMIT = 16 * 1024 * 1024


def inverse_sinh(value):
    magnitude = jnp.abs(value)
    result = jnp.log(magnitude + jnp.sqrt(1.0 + magnitude * magnitude))
    return jnp.where(value < 0.0, -result, result)


def friction_solve(shear, normal_stress, step_no, guess, state_now, fields):
    shear_pre, sigma_pre, friction_a, state_rate = fields
    shear_total = shear + shear_pre + LOADING * (step_no + 1)
    normal = sigma_pre * (1.0 + 0.5 * jnp.tanh(normal_stress))
    strength = friction_a * normal
    factor = 0.5 * jnp.exp(state_now)
    slip_rate = guess
    for attempt in range(NEWTON_ITERS):
        scaled = slip_rate * factor
        misfit = shear_total - DAMPING * slip_rate - strength * inverse_sinh(scaled)
        derivative = -DAMPING - strength * factor / jnp.sqrt(1.0 + scaled * scaled)
        slip_rate = slip_rate - misfit / derivative
    next_state = state_now + TIME_STEP * state_rate * jnp.tanh(
        jnp.exp(-state_now) - jnp.abs(slip_rate)
    )
    return slip_rate, next_state


def split_stress(even, odd):
    low = lax.broadcasted_iota(jnp.int32, even.shape, 1) < HALF
    shear = jnp.where(low, even, pltpu.roll(odd, HALF, 1))
    normal = jnp.where(low, pltpu.roll(even, HALF, 1), odd)
    return shear, normal


def encode(partial):
    scaled = partial * (1.0 / MESSAGE_SCALE)
    return (scaled * scaled * scaled).astype(jnp.bfloat16)


def decode(message):
    cube = message.astype(jnp.float32)
    magnitude = jnp.abs(cube)
    root = jnp.exp2(jnp.log2(jnp.maximum(magnitude, 1e-38)) * (1.0 / 3.0)) * MESSAGE_SCALE
    root = jnp.where(cube < 0.0, -root, root)
    return jnp.where(magnitude > 0.0, root, 0.0)


def pack_messages(send, partials, own_blocks, n_dest, dups):
    for dest in range(n_dest):
        for tile in range(own_blocks // ROWS):
            piece = encode(partials(dest * own_blocks + tile * ROWS, ROWS))
            for dup in range(dups):
                send[dest * dups + dup, :, tile * LANES:(tile + 1) * LANES] = piece


def sum_messages(recv, total, own_blocks, n_src, owners):
    for owner in range(owners):
        part = decode(recv[owner])
        for src in range(1, n_src):
            part = part + decode(recv[src * owners + owner])
        for tile in range(own_blocks // ROWS):
            first = owner * own_blocks + tile * ROWS
            total[first:first + ROWS, :] = part[:, tile * LANES:(tile + 1) * LANES]
    pairs = owners * own_blocks // 2
    return total[pl.ds(0, pairs, stride=2), :], total[pl.ds(1, pairs, stride=2), :]


def make_tables(rows, cols, scales, gather, scatter, weights):
    slots = rows.shape[-1]
    lane = lax.broadcasted_iota(jnp.int32, (SLOT_ROWS, LANES), 1)
    diagonal = lax.broadcasted_iota(jnp.int32, (SLOT_ROWS, LANES), 0) == lane
    rest = jnp.full((1, LANES - slots), -1.0, jnp.float32)

    def widened(values):
        return jnp.concatenate([values.astype(jnp.float32), rest], axis=1)

    def column(values):
        spread = jnp.where(diagonal, jnp.broadcast_to(values, diagonal.shape), 0.0)
        return jnp.sum(spread, axis=1, keepdims=True)

    one_row = lax.broadcasted_iota(jnp.int32, (1, LANES), 1)
    block = lax.broadcasted_iota(jnp.int32, (scatter.shape[1], LANES), 0).astype(jnp.float32)
    for lag in range(STEPS - 1):
        row_ids = widened(rows[lag, 0])
        for part in range(1, PARTS):
            at = one_row >= part * SLOT_ROWS
            row_ids = jnp.where(at, pltpu.roll(widened(rows[lag, 0]), part * SLOT_ROWS, 1), row_ids)
        row_ids = jnp.where(one_row < PARTS * SLOT_ROWS, row_ids, -1.0)
        scatter[lag] = (block == row_ids).astype(jnp.float32).astype(jnp.bfloat16)
        picks = jnp.maximum(column(widened(cols[lag, 0])), 0.0).astype(jnp.int32)
        gather[lag] = jnp.broadcast_to(picks, gather.shape[1:])
        weights[lag] = jnp.broadcast_to(column(widened(scales[lag, 0])), weights.shape[1:])


def older_kernel(
    panels, history, rows_in, cols_in, scales_in, *refs,
    lags, slots, n_src, n_rcv, own_blocks, n_fields,
):
    own_fields, refs = refs[:n_fields], refs[n_fields:]
    send, rest, guess, recent, gather, scatter, weights, fields, *refs = refs
    (
        panel_buf, history_buf, rows, cols, scales, rows_now, cols_now, scales_now, sources, acc, messages,
        sems, small_sems, out_sems,
    ) = refs
    src_blocks = n_rcv * own_blocks
    recv_blocks = n_src * own_blocks
    recent_lags = pl.ds(0, STEPS - 1)
    smalls = [
        pltpu.make_async_copy(source, target, small_sems.at[at])
        for at, (source, target) in enumerate([
            (history, history_buf), (cols_in, cols), (rows_in, rows), (scales_in, scales),
            (rows_in.at[recent_lags], rows_now), (cols_in.at[recent_lags], cols_now),
            (scales_in.at[recent_lags], scales_now),
            *[(field, fields.at[at]) for at, field in enumerate(own_fields)],
        ])
    ]

    def panel_copy(lag):
        return pltpu.make_async_copy(panels.at[lag], panel_buf.at[lag], sems.at[lag])

    for copy in smalls:
        copy.start()
    for lag in range(IN_FLIGHT):
        panel_copy(lag).start()
    acc[...] = jnp.zeros_like(acc)
    tail = jnp.zeros((TAPS - lags, LANES), jnp.float32)
    sources[0:LEAD, :] = jnp.zeros((LEAD, LANES), jnp.float32)
    smalls[0].wait()
    for pair in range(src_blocks // 2):
        tile = history_buf[:, pair * LANES:(pair + 1) * LANES].astype(jnp.float32)
        for half in range(2):
            base = LEAD + (2 * pair + half) * TAPS
            sources[base:base + lags, :] = tile if half == 0 else pltpu.roll(tile, HALF, 1)
            sources[base + lags:base + TAPS, :] = tail
    for copy in smalls[1:7]:
        copy.wait()
    top = lax.broadcasted_iota(jnp.int32, (8, LANES), 0) < STEPS
    match = top == (lax.broadcasted_iota(jnp.int32, (8, LANES), 1) < HALF)
    zero = jnp.zeros((8, LANES), jnp.float32)

    def one_lag(lag, carry):
        panel_copy(lag).wait()

        @pl.when(lag + IN_FLIGHT < lags)
        def _():
            panel_copy(lag + IN_FLIGHT).start()

        first_tap = LEAD + (lags - 1) - lag
        for group in range(0, slots, GROUP):
            pairs = []
            for slot in range(group, group + GROUP, 2):
                low = sources[pl.ds(cols[lag, 0, 0, slot] * TAPS + first_tap, 8), :]
                partner = cols[lag, 0, 0, slot + 1] ^ 1
                high = sources[pl.ds(partner * TAPS + first_tap - STEPS, 8), :]
                pairs.append(jnp.where(match, jnp.where(top, low, high), 0.0))
            columns = [
                jnp.concatenate([pair if at == to else zero for at in range(len(pairs))], axis=0)
                for to, pair in enumerate(pairs)
            ]
            picked = jnp.concatenate(columns, axis=1).astype(jnp.bfloat16)
            panel = panel_buf[lag, group:group + GROUP].reshape(GROUP * HALF, LANES)
            terms = jnp.dot(picked, panel, preferred_element_type=jnp.float32)
            for pair in range(len(pairs)):
                slot = group + 2 * pair
                scale = jnp.where(top, scales[lag, 0, 0, slot], scales[lag, 0, 0, slot + 1])
                term = terms[8 * pair:8 * pair + 8] * scale
                for part, addend in enumerate([jnp.where(top, term, 0.0), jnp.where(top, 0.0, term)]):
                    at = pl.ds(pl.multiple_of(rows[lag, 0, 0, slot + part] * 8, 8), 8)
                    acc[at, :] = acc[at, :] + addend
        return carry

    lax.fori_loop(0, lags, one_lag, 0)
    def partials(first_row, count, step):
        low, high = [
            acc[pl.ds(first_row * 8 + start, count, stride=8), :] for start in (step, STEPS + step)
        ]
        return low + high

    pack_messages(messages, lambda first, count: partials(first, count, 0), own_blocks, n_src, 1)
    outgoing = [
        pltpu.make_async_copy(messages, send.at[:, dup], out_sems.at[dup]) for dup in range(n_rcv)
    ]
    outgoing.append(pltpu.make_async_copy(panel_buf.at[recent_lags], recent, out_sems.at[n_rcv]))
    for copy in outgoing:
        copy.start()
    make_tables(rows_now, cols_now, scales_now, gather, scatter, weights)
    for step in range(1, STEPS):
        rest[step - 1] = partials(0, recv_blocks, step)
    guess[...] = sources[pl.ds(LEAD + lags - 1, src_blocks // 2, stride=2 * TAPS), :]
    for copy in outgoing + smalls[7:]:
        copy.wait()


def spread_sources(slip_rate, sources):
    pairs = slip_rate.shape[0]
    low = lax.broadcasted_iota(jnp.int32, slip_rate.shape, 1) < HALF
    turned = pltpu.roll(slip_rate, HALF, 1)
    sources[pl.ds(0, pairs, stride=2), :] = jnp.where(low, slip_rate, turned)
    sources[pl.ds(1, pairs, stride=2), :] = jnp.where(low, turned, slip_rate)


def take_rows(groups, rows):
    taken = []
    for first in range(0, rows.shape[0], 8):
        row = rows[first:first + 8]
        within = row & 7
        block = row - within
        piece = jnp.zeros(groups[0].shape, jnp.float32)
        for at, group in enumerate(groups):
            found = jnp.take_along_axis(group, within, axis=0, mode="promise_in_bounds")
            piece = jnp.where(block == 8 * at, found, piece)
        taken.append(piece)
    return jnp.concatenate(taken, axis=0)


def new_terms(lags, panels, sources, gather, scatter, weights):
    slots, width, wide = panels.shape[1:]
    groups = [sources[at:at + 8, :] for at in range(0, sources.shape[0], 8)]
    picked = [take_rows(groups, gather[lag]) for lag in lags]
    lane = lax.broadcasted_iota(jnp.int32, picked[0].shape, 1)
    row = lax.broadcasted_iota(jnp.int32, picked[0].shape, 0)
    first = row - jnp.where(lane < HALF, 0, 1)
    terms = []
    for lag, rates in zip(lags, picked):
        tiles = [
            jnp.where(first == slot, rates, 0.0).astype(jnp.bfloat16) for slot in range(0, slots, 2)
        ]
        panel = panels[lag].reshape(slots * width, wide)
        terms.append(
            jnp.dot(jnp.concatenate(tiles, axis=1), panel, preferred_element_type=jnp.float32)
        )
    sums = []
    for lag, left in zip(lags, terms):
        left = left * weights[lag]
        parts = []
        for part in range(PARTS):
            parts.append(left.astype(jnp.bfloat16))
            left = left - parts[-1].astype(jnp.float32)
        stacked = jnp.concatenate(parts, axis=0)
        table = scatter[lag][:, :stacked.shape[0]]
        sums.append(jnp.dot(table, stacked, preferred_element_type=jnp.float32))
    return sums


def order_fields(parts, fields):
    here = lax.axis_index("rcv")
    pairs = parts[0].shape[1]
    for owner in range(len(parts)):
        chosen = parts[0][...]
        for turn in range(1, len(parts)):
            chosen = jnp.where(here ^ owner == turn, parts[turn][...], chosen)
        for kind in range(fields.shape[0]):
            fields[kind, owner * pairs:(owner + 1) * pairs, :] = chosen[kind]


def step_kernel(
    recv, guess, rest, panels, gather, scatter, weights, *refs,
    step_no, n_src, n_rcv, own_blocks, dups, later,
):
    if step_no == 0:
        parts, (send, slip_out, state_out, fields), refs = refs[:n_rcv], refs[n_rcv:n_rcv + 4], refs[n_rcv + 4:]
        order_fields(parts, fields)
        state_in = fields.at[4]
    else:
        (fields, state_in, send, slip_out, state_out), refs = refs[:5], refs[5:]
    rest_out, (total, sources, acc) = refs[:-3], refs[-3:]
    shear, normal = split_stress(*sum_messages(recv, total, own_blocks, n_src, n_rcv))
    slip_rate, next_state = friction_solve(
        shear, normal, step_no, guess[...], state_in[...], [fields[kind] for kind in range(4)]
    )
    spread_sources(slip_rate, sources)
    terms = new_terms(range(later + 1), panels, sources, gather, scatter, weights)
    acc[...] = rest[0] + terms[0]
    pack_messages(send, lambda first, count: acc[pl.ds(first, count), :], own_blocks, n_src, dups)
    slip_out[...] = slip_rate
    state_out[...] = next_state
    for at in range(later):
        rest_out[0][at] = rest[at + 1] + terms[at + 1]


def last_kernel(
    recv, shear_pre, sigma_pre, friction_a, state_rate, state_in, *refs, step_no, n_src,
):
    slips, (slip_out, state_out, total) = refs[:step_no], refs[step_no:]
    pairs = slip_out.shape[1] // LANES
    mine = pl.ds(lax.axis_index("rcv") * pairs, pairs)
    shear, normal = split_stress(*sum_messages(recv, total, 2 * pairs, n_src, 1))
    fields = [ref[...] for ref in (shear_pre, sigma_pre, friction_a, state_rate)]
    slip_rate, next_state = friction_solve(
        shear, normal, step_no, slips[-1][mine, :], state_in[mine, :], fields
    )
    for step, field in enumerate([ref[mine, :] for ref in slips] + [slip_rate]):
        for row in range(pairs):
            slip_out[step:step + 1, row * LANES:(row + 1) * LANES] = field[row:row + 1]
    state_out[...] = next_state


def per_device(
    history, kernel, scales, block_rows, block_cols,
    shear_pre, sigma_pre, friction_a, state_rate, state_init,
):
    lags = kernel.shape[0]
    slots = kernel.shape[3]
    width = kernel.shape[4]
    n_src = lax.axis_size("src")
    n_rcv = lax.axis_size("rcv")
    own = shear_pre.shape[0]
    own_blocks = own // width
    pairs = own // LANES
    src_blocks = n_rcv * own_blocks
    recv_rows = n_src * own_blocks
    message = (ROWS, own_blocks // ROWS * LANES)
    panels = kernel.reshape(lags, slots, width, 2 * width)
    f32 = jnp.float32
    hbm = pl.BlockSpec(memory_space=pltpu.HBM)
    vmem = pl.BlockSpec(memory_space=pltpu.VMEM)
    sizes = dict(slots=slots, n_src=n_src, n_rcv=n_rcv, own_blocks=own_blocks)
    def shape(*dims, dtype=f32):
        return jax.ShapeDtypeStruct(dims, dtype)

    def call(body, ins, outs, scratch, name, args, flops, limit=VMEM_LIMIT, out_specs=None):
        return pl.pallas_call(
            body, in_specs=ins, out_specs=out_specs or [vmem] * len(outs), out_shape=outs, scratch_shapes=scratch,
            compiler_params=pltpu.CompilerParams(vmem_limit_bytes=limit), name=name,
            cost_estimate=pl.CostEstimate(flops=flops, bytes_accessed=flops // 64, transcendentals=0),
        )(*args)

    own_fields = [
        field.reshape(pairs, LANES)
        for field in (shear_pre, sigma_pre, friction_a, state_rate, state_init)
    ]
    own_hbm = [pltpu.with_memory_space_constraint(field, pltpu.HBM) for field in own_fields]

    panels, history, *table = [
        pltpu.with_memory_space_constraint(array, pltpu.HBM)
        for array in (panels, history, block_rows, block_cols, scales)
    ]
    one_lag = 2 * slots * width * 2 * width * 8
    send, rest, guess, recent, *tables, mine = call(
        functools.partial(older_kernel, lags=lags, n_fields=len(own_fields), **sizes),
        [hbm] * (5 + len(own_fields)),
        [
            shape(n_src, n_rcv, *message, dtype=jnp.bfloat16),
            shape(STEPS - 1, recv_rows, LANES),
            shape(src_blocks // 2, LANES),
            shape(STEPS - 1, slots, width, 2 * width, dtype=panels.dtype),
            shape(STEPS - 1, SLOT_ROWS, LANES, dtype=jnp.int32),
            shape(STEPS - 1, recv_rows, LANES, dtype=jnp.bfloat16),
            shape(STEPS - 1, SLOT_ROWS, LANES),
            shape(len(own_fields), pairs, LANES),
        ],
        [
            pltpu.VMEM(panels.shape, panels.dtype),
            pltpu.VMEM(history.shape, history.dtype),
            *[pltpu.SMEM(array.shape, array.dtype) for array in table],
            *[pltpu.VMEM((STEPS - 1, *array.shape[1:]), array.dtype) for array in table],
            pltpu.VMEM((LEAD + src_blocks * TAPS, LANES), f32),
            pltpu.VMEM((recv_rows * 8, LANES), f32),
            pltpu.VMEM((n_src, *message), jnp.bfloat16),
            pltpu.SemaphoreType.DMA((lags,)),
            pltpu.SemaphoreType.DMA((7 + len(own_fields),)),
            pltpu.SemaphoreType.DMA((n_rcv + 1,)),
        ],
        "older", [panels, history, *table, *own_hbm], 60 * one_lag, limit=32 * 1024 * 1024,
        out_specs=[hbm] + [vmem] * 7,
    )

    parts = [mine] + [
        lax.ppermute(mine, "rcv", [(at, at ^ turn) for at in range(n_rcv)]) for turn in range(1, n_rcv)
    ]
    slips = []
    recv = lax.all_to_all(send.reshape(n_src * n_rcv, *message), ("src", "rcv"), 0, 0, tiled=True)
    for step_no in range(STEPS - 1):
        last = step_no == STEPS - 2
        dups = 1 if last else n_rcv
        later = STEPS - 2 - step_no
        first = step_no == 0
        solve_inputs = parts if first else [fields, state]
        packed = shape(src_blocks // 2, LANES)
        send, slip_rate, state, *more = call(
            functools.partial(
                step_kernel, step_no=step_no, dups=dups, later=later,
                n_src=n_src, n_rcv=n_rcv, own_blocks=own_blocks,
            ),
            [vmem] * (7 + len(solve_inputs)),
            [shape(n_src * dups, *message, dtype=jnp.bfloat16), packed, packed]
            + [shape(len(own_fields), src_blocks // 2, LANES)] * first
            + [shape(later, recv_rows, LANES)] * bool(later),
            [
                pltpu.VMEM((src_blocks, LANES), f32),
                pltpu.VMEM((src_blocks, LANES), f32),
                pltpu.VMEM((recv_rows, LANES), f32),
            ],
            "step", [recv, guess, rest, recent, *tables, *solve_inputs], one_lag,
        )
        fields = more.pop(0) if first else fields
        guess = slip_rate
        rest = more[0] if later else rest
        slips.append(slip_rate)
        recv = lax.all_to_all(send, "src" if last else ("src", "rcv"), 0, 0, tiled=True)

    slip_rates, state = call(
        functools.partial(last_kernel, step_no=STEPS - 1, n_src=n_src),
        [vmem] * (6 + len(slips)),
        [shape(STEPS, own), shape(pairs, LANES)],
        [pltpu.VMEM((own_blocks, LANES), f32)],
        "last", [recv, *own_fields[:4], state, *slips], 10 ** 6,
    )
    return (slip_rates, state.reshape(own))


def solution(mesh):
    return jax.shard_map(
        per_device,
        mesh=mesh,
        in_specs=(
            P(None, "src"),
            P(None, "src", "rcv", None, None, None),
            P(None, "src", "rcv", None),
            P(None, "src", "rcv", None),
            P(None, "src", "rcv", None),
            P(("src", "rcv")),
            P(("src", "rcv")),
            P(("src", "rcv")),
            P(("src", "rcv")),
            P(("src", "rcv")),
        ),
        out_specs=(P(None, ("src", "rcv")), P(("src", "rcv"))),
        check_vma=False,
    )
```

```python
import functools

import jax
import jax.numpy as jnp
from jax import lax
from jax.experimental import pallas as pl
from jax.experimental.pallas import tpu as pltpu
from jax.sharding import PartitionSpec as P

STEPS = 4
NEWTON_ITERS = 4
DAMPING = 1.0
LOADING = 0.05
TIME_STEP = 0.2
LANES = 128
HALF = LANES // 2
ROWS = 4
IN_FLIGHT = 6
GROUP = 4
SLOT_ROWS = 32
PARTS = 3
MESSAGE_SCALE = 2.0 ** 22
TAPS = 24
LEAD = 8
VMEM_LIMIT = 16 * 1024 * 1024


def inverse_sinh(value, root):
    result = jnp.log(jnp.abs(value) + root)
    return jnp.where(value < 0.0, -result, result)


def friction_solve(shear, normal_stress, step_no, guess, state_now, fields):
    shear_pre, sigma_pre, friction_a, state_rate = fields
    shear_total = shear + shear_pre + LOADING * (step_no + 1)
    normal = sigma_pre * (1.0 + 0.5 * jnp.tanh(normal_stress))
    strength = friction_a * normal
    factor = 0.5 * jnp.exp(state_now)
    slip_rate = guess
    for attempt in range(NEWTON_ITERS):
        scaled = slip_rate * factor
        root = jnp.sqrt(1.0 + scaled * scaled)
        misfit = shear_total - DAMPING * slip_rate - strength * inverse_sinh(scaled, root)
        derivative = -DAMPING - strength * factor / root
        slip_rate = slip_rate - misfit / derivative
    next_state = state_now + TIME_STEP * state_rate * jnp.tanh(
        jnp.exp(-state_now) - jnp.abs(slip_rate)
    )
    return slip_rate, next_state


def split_stress(even, odd):
    low = lax.broadcasted_iota(jnp.int32, even.shape, 1) < HALF
    shear = jnp.where(low, even, pltpu.roll(odd, HALF, 1))
    normal = jnp.where(low, pltpu.roll(even, HALF, 1), odd)
    return shear, normal


def encode(partial):
    scaled = partial * (1.0 / MESSAGE_SCALE)
    return (scaled * scaled * scaled).astype(jnp.bfloat16)


def decode(message):
    cube = message.astype(jnp.float32)
    magnitude = jnp.abs(cube)
    root = jnp.exp2(jnp.log2(jnp.maximum(magnitude, 1e-38)) * (1.0 / 3.0)) * MESSAGE_SCALE
    root = jnp.where(cube < 0.0, -root, root)
    return jnp.where(magnitude > 0.0, root, 0.0)


def pack_messages(send, partials, own_blocks, n_dest, dups):
    for dest in range(n_dest):
        for tile in range(own_blocks // ROWS):
            piece = encode(partials(dest * own_blocks + tile * ROWS, ROWS))
            for dup in range(dups):
                send[dest * dups + dup, :, tile * LANES:(tile + 1) * LANES] = piece


def sum_messages(recv, total, own_blocks, n_src, owners):
    for owner in range(owners):
        part = decode(recv[owner])
        for src in range(1, n_src):
            part = part + decode(recv[src * owners + owner])
        for tile in range(own_blocks // ROWS):
            first = owner * own_blocks + tile * ROWS
            total[first:first + ROWS, :] = part[:, tile * LANES:(tile + 1) * LANES]
    pairs = owners * own_blocks // 2
    return total[pl.ds(0, pairs, stride=2), :], total[pl.ds(1, pairs, stride=2), :]


def make_tables(rows, cols, scales, gather, scatter, weights):
    slots = rows.shape[-1]
    lane = lax.broadcasted_iota(jnp.int32, (SLOT_ROWS, LANES), 1)
    diagonal = lax.broadcasted_iota(jnp.int32, (SLOT_ROWS, LANES), 0) == lane
    rest = jnp.full((1, LANES - slots), -1.0, jnp.float32)

    def widened(values):
        return jnp.concatenate([values.astype(jnp.float32), rest], axis=1)

    def column(values):
        spread = jnp.where(diagonal, jnp.broadcast_to(values, diagonal.shape), 0.0)
        return jnp.sum(spread, axis=1, keepdims=True)

    one_row = lax.broadcasted_iota(jnp.int32, (1, LANES), 1)
    block = lax.broadcasted_iota(jnp.int32, (scatter.shape[1], LANES), 0).astype(jnp.float32)
    for lag in range(STEPS - 1):
        row_ids = widened(rows[lag, 0])
        for part in range(1, PARTS):
            at = one_row >= part * SLOT_ROWS
            row_ids = jnp.where(at, pltpu.roll(widened(rows[lag, 0]), part * SLOT_ROWS, 1), row_ids)
        row_ids = jnp.where(one_row < PARTS * SLOT_ROWS, row_ids, -1.0)
        scatter[lag] = (block == row_ids).astype(jnp.float32).astype(jnp.bfloat16)
        picks = jnp.maximum(column(widened(cols[lag, 0])), 0.0).astype(jnp.int32)
        gather[lag] = jnp.broadcast_to(picks, gather.shape[1:])
        weights[lag] = jnp.broadcast_to(column(widened(scales[lag, 0])), weights.shape[1:])


def older_kernel(
    panels, history, rows_in, cols_in, scales_in, *refs,
    lags, slots, n_src, n_rcv, own_blocks, n_fields,
):
    own_fields, refs = refs[:n_fields], refs[n_fields:]
    send, rest, guess, recent, gather, scatter, weights, fields, *refs = refs
    (
        panel_buf, history_buf, rows, cols, scales, rows_now, cols_now, scales_now, sources, acc_low, acc_high, messages,
        sems, small_sems, out_sems,
    ) = refs
    src_blocks = n_rcv * own_blocks
    recv_blocks = n_src * own_blocks
    recent_lags = pl.ds(0, STEPS - 1)
    smalls = [
        pltpu.make_async_copy(source, target, small_sems.at[at])
        for at, (source, target) in enumerate([
            (history, history_buf), (cols_in, cols), (rows_in, rows), (scales_in, scales),
            (rows_in.at[recent_lags], rows_now), (cols_in.at[recent_lags], cols_now),
            (scales_in.at[recent_lags], scales_now),
            *[(field, fields.at[at]) for at, field in enumerate(own_fields)],
        ])
    ]

    def panel_copy(lag):
        return pltpu.make_async_copy(panels.at[lag], panel_buf.at[lag], sems.at[lag])

    for copy in smalls:
        copy.start()
    for lag in range(IN_FLIGHT):
        panel_copy(lag).start()
    accs = (acc_low, acc_high)
    for acc in accs:
        acc[...] = jnp.zeros_like(acc)
    tail = jnp.zeros((TAPS - lags, LANES), jnp.float32)
    sources[0:LEAD, :] = jnp.zeros((LEAD, LANES), jnp.float32)
    smalls[0].wait()
    for pair in range(src_blocks // 2):
        tile = history_buf[:, pair * LANES:(pair + 1) * LANES].astype(jnp.float32)
        for half in range(2):
            base = LEAD + (2 * pair + half) * TAPS
            sources[base:base + lags, :] = tile if half == 0 else pltpu.roll(tile, HALF, 1)
            sources[base + lags:base + TAPS, :] = tail
    for copy in smalls[1:7]:
        copy.wait()
    top = lax.broadcasted_iota(jnp.int32, (8, LANES), 0) < STEPS
    match = top == (lax.broadcasted_iota(jnp.int32, (8, LANES), 1) < HALF)
    zero = jnp.zeros((8, LANES), jnp.float32)

    def one_lag(lag, carry):
        panel_copy(lag).wait()

        @pl.when(lag + IN_FLIGHT < lags)
        def _():
            panel_copy(lag + IN_FLIGHT).start()

        first_tap = LEAD + (lags - 1) - lag
        for group in range(0, slots, GROUP):
            pairs = []
            for slot in range(group, group + GROUP, 2):
                low = sources[pl.ds(cols[lag, 0, 0, slot] * TAPS + first_tap, 8), :]
                partner = cols[lag, 0, 0, slot + 1] ^ 1
                high = sources[pl.ds(partner * TAPS + first_tap - STEPS, 8), :]
                pairs.append(jnp.where(match, jnp.where(top, low, high), 0.0))
            columns = [
                jnp.concatenate([pair if at == to else zero for at in range(len(pairs))], axis=0)
                for to, pair in enumerate(pairs)
            ]
            picked = jnp.concatenate(columns, axis=1).astype(jnp.bfloat16)
            panel = panel_buf[lag, group:group + GROUP].reshape(GROUP * HALF, LANES)
            terms = jnp.dot(picked, panel, preferred_element_type=jnp.float32)
            for pair in range(len(pairs)):
                slot = group + 2 * pair
                scale = jnp.where(top, scales[lag, 0, 0, slot], scales[lag, 0, 0, slot + 1])
                term = terms[8 * pair:8 * pair + 8] * scale
                for part, acc in enumerate(accs):
                    at = pl.ds(pl.multiple_of(rows[lag, 0, 0, slot + part] * 8, 8), 8)
                    acc[at, :] = acc[at, :] + term
        return carry

    lax.fori_loop(0, lags, one_lag, 0)
    def partials(first_row, count, step):
        low, high = [
            acc[pl.ds(first_row * 8 + part * STEPS + step, count, stride=8), :]
            for part, acc in enumerate(accs)
        ]
        return low + high

    pack_messages(messages, lambda first, count: partials(first, count, 0), own_blocks, n_src, 1)
    outgoing = [
        pltpu.make_async_copy(messages, send.at[:, dup], out_sems.at[dup]) for dup in range(n_rcv)
    ]
    outgoing.append(pltpu.make_async_copy(panel_buf.at[recent_lags], recent, out_sems.at[n_rcv]))
    for copy in outgoing:
        copy.start()
    make_tables(rows_now, cols_now, scales_now, gather, scatter, weights)
    for step in range(1, STEPS):
        rest[step - 1] = partials(0, recv_blocks, step)
    guess[...] = sources[pl.ds(LEAD + lags - 1, src_blocks // 2, stride=2 * TAPS), :]
    for copy in outgoing + smalls[7:]:
        copy.wait()


def spread_sources(slip_rate, sources):
    pairs = slip_rate.shape[0]
    low = lax.broadcasted_iota(jnp.int32, slip_rate.shape, 1) < HALF
    turned = pltpu.roll(slip_rate, HALF, 1)
    sources[pl.ds(0, pairs, stride=2), :] = jnp.where(low, slip_rate, turned)
    sources[pl.ds(1, pairs, stride=2), :] = jnp.where(low, turned, slip_rate)


def take_rows(groups, rows):
    taken = []
    for first in range(0, rows.shape[0], 8):
        row = rows[first:first + 8]
        within = row & 7
        block = row - within
        piece = jnp.zeros(groups[0].shape, jnp.float32)
        for at, group in enumerate(groups):
            found = jnp.take_along_axis(group, within, axis=0, mode="promise_in_bounds")
            piece = jnp.where(block == 8 * at, found, piece)
        taken.append(piece)
    return jnp.concatenate(taken, axis=0)


def new_terms(lags, panels, sources, gather, scatter, weights):
    slots, width, wide = panels.shape[1:]
    groups = [sources[at:at + 8, :] for at in range(0, sources.shape[0], 8)]
    picked = [take_rows(groups, gather[lag]) for lag in lags]
    lane = lax.broadcasted_iota(jnp.int32, picked[0].shape, 1)
    row = lax.broadcasted_iota(jnp.int32, picked[0].shape, 0)
    first = row - jnp.where(lane < HALF, 0, 1)
    terms = []
    for lag, rates in zip(lags, picked):
        tiles = [
            jnp.where(first == slot, rates, 0.0).astype(jnp.bfloat16) for slot in range(0, slots, 2)
        ]
        panel = panels[lag].reshape(slots * width, wide)
        terms.append(
            jnp.dot(jnp.concatenate(tiles, axis=1), panel, preferred_element_type=jnp.float32)
        )
    sums = []
    for lag, left in zip(lags, terms):
        left = left * weights[lag]
        parts = []
        for part in range(PARTS):
            parts.append(left.astype(jnp.bfloat16))
            left = left - parts[-1].astype(jnp.float32)
        stacked = jnp.concatenate(parts, axis=0)
        table = scatter[lag][:, :stacked.shape[0]]
        sums.append(jnp.dot(table, stacked, preferred_element_type=jnp.float32))
    return sums


def order_fields(parts, fields):
    here = lax.axis_index("rcv")
    pairs = parts[0].shape[1]
    for owner in range(len(parts)):
        chosen = parts[0][...]
        for turn in range(1, len(parts)):
            chosen = jnp.where(here ^ owner == turn, parts[turn][...], chosen)
        for kind in range(fields.shape[0]):
            fields[kind, owner * pairs:(owner + 1) * pairs, :] = chosen[kind]


def step_kernel(
    recv, guess, rest, panels, gather, scatter, weights, *refs,
    step_no, n_src, n_rcv, own_blocks, dups, later,
):
    if step_no == 0:
        parts, (send, slip_out, state_out, fields), refs = refs[:n_rcv], refs[n_rcv:n_rcv + 4], refs[n_rcv + 4:]
        order_fields(parts, fields)
        state_in = fields.at[4]
    else:
        (fields, state_in, send, slip_out, state_out), refs = refs[:5], refs[5:]
    rest_out, (total, sources, acc) = refs[:-3], refs[-3:]
    shear, normal = split_stress(*sum_messages(recv, total, own_blocks, n_src, n_rcv))
    slip_rate, next_state = friction_solve(
        shear, normal, step_no, guess[...], state_in[...], [fields[kind] for kind in range(4)]
    )
    spread_sources(slip_rate, sources)
    terms = new_terms(range(later + 1), panels, sources, gather, scatter, weights)
    acc[...] = rest[0] + terms[0]
    pack_messages(send, lambda first, count: acc[pl.ds(first, count), :], own_blocks, n_src, dups)
    slip_out[...] = slip_rate
    state_out[...] = next_state
    for at in range(later):
        rest_out[0][at] = rest[at + 1] + terms[at + 1]


def last_kernel(
    recv, shear_pre, sigma_pre, friction_a, state_rate, state_in, *refs, step_no, n_src,
):
    slips, (slip_out, state_out, total) = refs[:step_no], refs[step_no:]
    pairs = slip_out.shape[1] // LANES
    mine = pl.ds(lax.axis_index("rcv") * pairs, pairs)
    shear, normal = split_stress(*sum_messages(recv, total, 2 * pairs, n_src, 1))
    fields = [ref[...] for ref in (shear_pre, sigma_pre, friction_a, state_rate)]
    slip_rate, next_state = friction_solve(
        shear, normal, step_no, slips[-1][mine, :], state_in[mine, :], fields
    )
    for step, field in enumerate([ref[mine, :] for ref in slips] + [slip_rate]):
        for row in range(pairs):
            slip_out[step:step + 1, row * LANES:(row + 1) * LANES] = field[row:row + 1]
    state_out[...] = next_state


def per_device(
    history, kernel, scales, block_rows, block_cols,
    shear_pre, sigma_pre, friction_a, state_rate, state_init,
):
    lags = kernel.shape[0]
    slots = kernel.shape[3]
    width = kernel.shape[4]
    n_src = lax.axis_size("src")
    n_rcv = lax.axis_size("rcv")
    own = shear_pre.shape[0]
    own_blocks = own // width
    pairs = own // LANES
    src_blocks = n_rcv * own_blocks
    recv_rows = n_src * own_blocks
    message = (ROWS, own_blocks // ROWS * LANES)
    panels = kernel.reshape(lags, slots, width, 2 * width)
    f32 = jnp.float32
    hbm = pl.BlockSpec(memory_space=pltpu.HBM)
    vmem = pl.BlockSpec(memory_space=pltpu.VMEM)
    sizes = dict(slots=slots, n_src=n_src, n_rcv=n_rcv, own_blocks=own_blocks)
    def shape(*dims, dtype=f32):
        return jax.ShapeDtypeStruct(dims, dtype)

    def call(body, ins, outs, scratch, name, args, flops, limit=VMEM_LIMIT, out_specs=None):
        return pl.pallas_call(
            body, in_specs=ins, out_specs=out_specs or [vmem] * len(outs), out_shape=outs, scratch_shapes=scratch,
            compiler_params=pltpu.CompilerParams(vmem_limit_bytes=limit), name=name,
            cost_estimate=pl.CostEstimate(flops=flops, bytes_accessed=flops // 64, transcendentals=0),
        )(*args)

    own_fields = [
        field.reshape(pairs, LANES)
        for field in (shear_pre, sigma_pre, friction_a, state_rate, state_init)
    ]
    own_hbm = [pltpu.with_memory_space_constraint(field, pltpu.HBM) for field in own_fields]

    panels, history, *table = [
        pltpu.with_memory_space_constraint(array, pltpu.HBM)
        for array in (panels, history, block_rows, block_cols, scales)
    ]
    one_lag = 2 * slots * width * 2 * width * 8
    send, rest, guess, recent, *tables, mine = call(
        functools.partial(older_kernel, lags=lags, n_fields=len(own_fields), **sizes),
        [hbm] * (5 + len(own_fields)),
        [
            shape(n_src, n_rcv, *message, dtype=jnp.bfloat16),
            shape(STEPS - 1, recv_rows, LANES),
            shape(src_blocks // 2, LANES),
            shape(STEPS - 1, slots, width, 2 * width, dtype=panels.dtype),
            shape(STEPS - 1, SLOT_ROWS, LANES, dtype=jnp.int32),
            shape(STEPS - 1, recv_rows, LANES, dtype=jnp.bfloat16),
            shape(STEPS - 1, SLOT_ROWS, LANES),
            shape(len(own_fields), pairs, LANES),
        ],
        [
            pltpu.VMEM(panels.shape, panels.dtype),
            pltpu.VMEM(history.shape, history.dtype),
            *[pltpu.SMEM(array.shape, array.dtype) for array in table],
            *[pltpu.VMEM((STEPS - 1, *array.shape[1:]), array.dtype) for array in table],
            pltpu.VMEM((LEAD + src_blocks * TAPS, LANES), f32),
            pltpu.VMEM((recv_rows * 8, LANES), f32),
            pltpu.VMEM((recv_rows * 8, LANES), f32),
            pltpu.VMEM((n_src, *message), jnp.bfloat16),
            pltpu.SemaphoreType.DMA((lags,)),
            pltpu.SemaphoreType.DMA((7 + len(own_fields),)),
            pltpu.SemaphoreType.DMA((n_rcv + 1,)),
        ],
        "older", [panels, history, *table, *own_hbm], 60 * one_lag, limit=32 * 1024 * 1024,
        out_specs=[hbm] + [vmem] * 7,
    )

    parts = [mine] + [
        lax.ppermute(mine, "rcv", [(at, at ^ turn) for at in range(n_rcv)]) for turn in range(1, n_rcv)
    ]
    slips = []
    recv = lax.all_to_all(send.reshape(n_src * n_rcv, *message), ("src", "rcv"), 0, 0, tiled=True)
    for step_no in range(STEPS - 1):
        last = step_no == STEPS - 2
        dups = 1 if last else n_rcv
        later = STEPS - 2 - step_no
        first = step_no == 0
        solve_inputs = parts if first else [fields, state]
        packed = shape(src_blocks // 2, LANES)
        send, slip_rate, state, *more = call(
            functools.partial(
                step_kernel, step_no=step_no, dups=dups, later=later,
                n_src=n_src, n_rcv=n_rcv, own_blocks=own_blocks,
            ),
            [vmem] * (7 + len(solve_inputs)),
            [shape(n_src * dups, *message, dtype=jnp.bfloat16), packed, packed]
            + [shape(len(own_fields), src_blocks // 2, LANES)] * first
            + [shape(later, recv_rows, LANES)] * bool(later),
            [
                pltpu.VMEM((src_blocks, LANES), f32),
                pltpu.VMEM((src_blocks, LANES), f32),
                pltpu.VMEM((recv_rows, LANES), f32),
            ],
            "step", [recv, guess, rest, recent, *tables, *solve_inputs], one_lag,
        )
        fields = more.pop(0) if first else fields
        guess = slip_rate
        rest = more[0] if later else rest
        slips.append(slip_rate)
        recv = lax.all_to_all(send, "src" if last else ("src", "rcv"), 0, 0, tiled=True)

    slip_rates, state = call(
        functools.partial(last_kernel, step_no=STEPS - 1, n_src=n_src),
        [vmem] * (6 + len(slips)),
        [shape(STEPS, own), shape(pairs, LANES)],
        [pltpu.VMEM((own_blocks, LANES), f32)],
        "last", [recv, *own_fields[:4], state, *slips], 10 ** 6,
    )
    return (slip_rates, state.reshape(own))


def solution(mesh):
    return jax.shard_map(
        per_device,
        mesh=mesh,
        in_specs=(
            P(None, "src"),
            P(None, "src", "rcv", None, None, None),
            P(None, "src", "rcv", None),
            P(None, "src", "rcv", None),
            P(None, "src", "rcv", None),
            P(("src", "rcv")),
            P(("src", "rcv")),
            P(("src", "rcv")),
            P(("src", "rcv")),
            P(("src", "rcv")),
        ),
        out_specs=(P(None, ("src", "rcv")), P(("src", "rcv"))),
        check_vma=False,
    )
```

```python
import functools

import jax
import jax.numpy as jnp
from jax import lax
from jax.experimental import pallas as pl
from jax.experimental.pallas import tpu as pltpu
from jax.sharding import PartitionSpec as P

STEPS = 4
NEWTON_ITERS = 4
DAMPING = 1.0
LOADING = 0.05
TIME_STEP = 0.2
LANES = 128
HALF = LANES // 2
ROWS = 4
IN_FLIGHT = 8
GROUP = 4
SLOT_ROWS = 32
PARTS = 3
MESSAGE_BITS = 22
MESSAGE_SCALE = 2.0 ** MESSAGE_BITS
TAPS = 24
LEAD = 8
VMEM_LIMIT = 16 * 1024 * 1024


def inverse_sinh(value, root):
    result = jnp.log(jnp.abs(value) + root)
    return jnp.where(value < 0.0, -result, result)


def friction_solve(shear, normal_stress, step_no, guess, state_now, fields):
    shear_pre, sigma_pre, friction_a, state_rate = fields
    shear_total = shear + shear_pre + LOADING * (step_no + 1)
    normal = sigma_pre * (1.0 + 0.5 * jnp.tanh(normal_stress))
    strength = friction_a * normal
    factor = 0.5 * jnp.exp(state_now)
    slip_rate = guess
    for attempt in range(NEWTON_ITERS):
        scaled = slip_rate * factor
        root = jnp.sqrt(1.0 + scaled * scaled)
        misfit = shear_total - DAMPING * slip_rate - strength * inverse_sinh(scaled, root)
        derivative = -DAMPING - strength * factor / root
        slip_rate = slip_rate - misfit / derivative
    next_state = state_now + TIME_STEP * state_rate * jnp.tanh(
        jnp.exp(-state_now) - jnp.abs(slip_rate)
    )
    return slip_rate, next_state


def split_stress(even, odd):
    low = lax.broadcasted_iota(jnp.int32, even.shape, 1) < HALF
    shear = jnp.where(low, even, pltpu.roll(odd, HALF, 1))
    normal = jnp.where(low, pltpu.roll(even, HALF, 1), odd)
    return shear, normal


def encode(partial):
    scaled = partial * (1.0 / MESSAGE_SCALE)
    return scaled * scaled * scaled


def decode(message):
    cube = message.astype(jnp.float32)
    root = jnp.exp2(jnp.log2(jnp.abs(cube)) * (1.0 / 3.0) + MESSAGE_BITS)
    return jnp.where(cube < 0.0, -root, root)


def pack_messages(send, partials, own_blocks, n_dest, dups):
    for dest in range(n_dest):
        for tile in range(own_blocks // ROWS):
            piece = partials(dest * own_blocks + tile * ROWS, ROWS).astype(jnp.bfloat16)
            for dup in range(dups):
                send[dest * dups + dup, :, tile * LANES:(tile + 1) * LANES] = piece


def sum_messages(recv, total, own_blocks, n_src, owners):
    for owner in range(owners):
        part = decode(recv[owner])
        for src in range(1, n_src):
            part = part + decode(recv[src * owners + owner])
        for tile in range(own_blocks // ROWS):
            first = owner * own_blocks + tile * ROWS
            total[first:first + ROWS, :] = part[:, tile * LANES:(tile + 1) * LANES]
    pairs = owners * own_blocks // 2
    return total[pl.ds(0, pairs, stride=2), :], total[pl.ds(1, pairs, stride=2), :]


def make_tables(rows, cols, scales, gather, scatter, weights):
    slots = rows.shape[-1]
    lane = lax.broadcasted_iota(jnp.int32, (SLOT_ROWS, LANES), 1)
    diagonal = lax.broadcasted_iota(jnp.int32, (SLOT_ROWS, LANES), 0) == lane
    rest = jnp.full((1, LANES - slots), -1.0, jnp.float32)

    def widened(values):
        return jnp.concatenate([values.astype(jnp.float32), rest], axis=1)

    def column(values):
        spread = jnp.where(diagonal, jnp.broadcast_to(values, diagonal.shape), 0.0)
        return jnp.sum(spread, axis=1, keepdims=True)

    one_row = lax.broadcasted_iota(jnp.int32, (1, LANES), 1)
    block = lax.broadcasted_iota(jnp.int32, (scatter.shape[1], LANES), 0).astype(jnp.float32)
    for lag in range(STEPS - 1):
        row_ids = widened(rows[lag, 0])
        for part in range(1, PARTS):
            at = one_row >= part * SLOT_ROWS
            row_ids = jnp.where(at, pltpu.roll(widened(rows[lag, 0]), part * SLOT_ROWS, 1), row_ids)
        row_ids = jnp.where(one_row < PARTS * SLOT_ROWS, row_ids, -1.0)
        scatter[lag] = (block == row_ids).astype(jnp.float32).astype(jnp.bfloat16)
        picks = jnp.maximum(column(widened(cols[lag, 0])), 0.0).astype(jnp.int32)
        gather[lag] = jnp.broadcast_to(picks, gather.shape[1:])
        weights[lag] = jnp.broadcast_to(column(widened(scales[lag, 0])), weights.shape[1:])


def older_kernel(
    panels, history, rows_in, cols_in, scales_in, *refs,
    lags, slots, n_src, n_rcv, own_blocks, n_fields,
):
    own_fields, refs = refs[:n_fields], refs[n_fields:]
    send, rest, guess, recent, gather, scatter, weights, fields, *refs = refs
    (
        panel_buf, history_buf, rows, cols, scales, rows_now, cols_now, scales_now, sources, acc_low, acc_high, messages,
        sems, small_sems, out_sems,
    ) = refs
    src_blocks = n_rcv * own_blocks
    recv_blocks = n_src * own_blocks
    recent_lags = pl.ds(0, STEPS - 1)
    smalls = [
        pltpu.make_async_copy(source, target, small_sems.at[at])
        for at, (source, target) in enumerate([
            (history, history_buf), (cols_in, cols), (rows_in, rows), (scales_in, scales),
            (rows_in.at[recent_lags], rows_now), (cols_in.at[recent_lags], cols_now),
            (scales_in.at[recent_lags], scales_now),
            *[(field, fields.at[at]) for at, field in enumerate(own_fields)],
        ])
    ]

    def panel_copy(lag):
        return pltpu.make_async_copy(panels.at[lag], panel_buf.at[lag], sems.at[lag])

    for copy in smalls:
        copy.start()
    for lag in range(IN_FLIGHT):
        panel_copy(lag).start()
    accs = (acc_low, acc_high)
    for acc in accs:
        acc[...] = jnp.zeros_like(acc)
    tail = jnp.zeros((TAPS - lags, LANES), jnp.float32)
    sources[0:LEAD, :] = jnp.zeros((LEAD, LANES), jnp.float32)
    smalls[0].wait()
    for pair in range(src_blocks // 2):
        tile = history_buf[:, pair * LANES:(pair + 1) * LANES].astype(jnp.float32)
        for half in range(2):
            base = LEAD + (2 * pair + half) * TAPS
            sources[base:base + lags, :] = tile if half == 0 else pltpu.roll(tile, HALF, 1)
            sources[base + lags:base + TAPS, :] = tail
    for copy in smalls[1:7]:
        copy.wait()
    top = lax.broadcasted_iota(jnp.int32, (8, LANES), 0) < STEPS
    match = top == (lax.broadcasted_iota(jnp.int32, (8, LANES), 1) < HALF)
    zero = jnp.zeros((8, LANES), jnp.float32)

    def one_lag(lag, carry):
        panel_copy(lag).wait()

        @pl.when(lag + IN_FLIGHT < lags)
        def _():
            panel_copy(lag + IN_FLIGHT).start()

        first_tap = LEAD + (lags - 1) - lag
        for group in range(0, slots, GROUP):
            pairs = []
            for slot in range(group, group + GROUP, 2):
                low = sources[pl.ds(cols[lag, 0, 0, slot] * TAPS + first_tap, 8), :]
                partner = cols[lag, 0, 0, slot + 1] ^ 1
                high = sources[pl.ds(partner * TAPS + first_tap - STEPS, 8), :]
                pairs.append(jnp.where(match, jnp.where(top, low, high), 0.0))
            columns = [
                jnp.concatenate([pair if at == to else zero for at in range(len(pairs))], axis=0)
                for to, pair in enumerate(pairs)
            ]
            picked = jnp.concatenate(columns, axis=1).astype(jnp.bfloat16)
            panel = panel_buf[lag, group:group + GROUP].reshape(GROUP * HALF, LANES)
            terms = jnp.dot(picked, panel, preferred_element_type=jnp.float32)
            for pair in range(len(pairs)):
                slot = group + 2 * pair
                scale = jnp.where(top, scales[lag, 0, 0, slot], scales[lag, 0, 0, slot + 1])
                term = terms[8 * pair:8 * pair + 8] * scale
                for part, acc in enumerate(accs):
                    at = pl.ds(pl.multiple_of(rows[lag, 0, 0, slot + part] * 8, 8), 8)
                    acc[at, :] = acc[at, :] + term
        return carry

    lax.fori_loop(0, lags, one_lag, 0)
    def partials(first_row, count, step):
        low, high = [
            acc[pl.ds(first_row * 8 + part * STEPS + step, count, stride=8), :]
            for part, acc in enumerate(accs)
        ]
        return low + high

    pack_messages(messages, lambda first, count: encode(partials(first, count, 0)), own_blocks, n_src, 1)
    outgoing = [
        pltpu.make_async_copy(messages, send.at[:, dup], out_sems.at[dup]) for dup in range(n_rcv)
    ]
    outgoing.append(pltpu.make_async_copy(panel_buf.at[recent_lags], recent, out_sems.at[n_rcv]))
    for copy in outgoing:
        copy.start()
    make_tables(rows_now, cols_now, scales_now, gather, scatter, weights)
    for step in range(1, STEPS):
        rest[step - 1] = partials(0, recv_blocks, step)
    guess[...] = sources[pl.ds(LEAD + lags - 1, src_blocks // 2, stride=2 * TAPS), :]
    for copy in outgoing + smalls[7:]:
        copy.wait()


def spread_sources(slip_rate, sources):
    pairs = slip_rate.shape[0]
    low = lax.broadcasted_iota(jnp.int32, slip_rate.shape, 1) < HALF
    turned = pltpu.roll(slip_rate, HALF, 1)
    sources[pl.ds(0, pairs, stride=2), :] = jnp.where(low, slip_rate, turned)
    sources[pl.ds(1, pairs, stride=2), :] = jnp.where(low, turned, slip_rate)


def take_rows(groups, rows):
    taken = []
    for first in range(0, rows.shape[0], 8):
        row = rows[first:first + 8]
        within = row & 7
        block = row - within
        piece = jnp.zeros(groups[0].shape, jnp.float32)
        for at, group in enumerate(groups):
            found = jnp.take_along_axis(group, within, axis=0, mode="promise_in_bounds")
            piece = jnp.where(block == 8 * at, found, piece)
        taken.append(piece)
    return jnp.concatenate(taken, axis=0)


def new_terms(lags, panels, sources, gather, scatter, weights):
    slots, width, wide = panels.shape[1:]
    groups = [sources[at:at + 8, :] for at in range(0, sources.shape[0], 8)]
    picked = [take_rows(groups, gather[lag]) for lag in lags]
    lane = lax.broadcasted_iota(jnp.int32, picked[0].shape, 1)
    row = lax.broadcasted_iota(jnp.int32, picked[0].shape, 0)
    first = row - jnp.where(lane < HALF, 0, 1)
    terms = []
    for lag, rates in zip(lags, picked):
        tiles = [
            jnp.where(first == slot, rates, 0.0).astype(jnp.bfloat16) for slot in range(0, slots, 2)
        ]
        panel = panels[lag].reshape(slots * width, wide)
        terms.append(
            jnp.dot(jnp.concatenate(tiles, axis=1), panel, preferred_element_type=jnp.float32)
        )
    sums = []
    for lag, left in zip(lags, terms):
        left = left * weights[lag]
        parts = []
        for part in range(PARTS):
            parts.append(left.astype(jnp.bfloat16))
            left = left - parts[-1].astype(jnp.float32)
        stacked = jnp.concatenate(parts, axis=0)
        table = scatter[lag][:, :stacked.shape[0]]
        sums.append(jnp.dot(table, stacked, preferred_element_type=jnp.float32))
    return sums


def order_fields(parts, fields):
    here = lax.axis_index("rcv")
    pairs = parts[0].shape[1]
    for owner in range(len(parts)):
        chosen = parts[0][...]
        for turn in range(1, len(parts)):
            chosen = jnp.where(here ^ owner == turn, parts[turn][...], chosen)
        for kind in range(fields.shape[0]):
            fields[kind, owner * pairs:(owner + 1) * pairs, :] = chosen[kind]


def step_kernel(
    recv, guess, rest, panels, gather, scatter, weights, *refs,
    step_no, n_src, n_rcv, own_blocks, dups, later,
):
    if step_no == 0:
        parts, (send, slip_out, state_out, fields), refs = refs[:n_rcv], refs[n_rcv:n_rcv + 4], refs[n_rcv + 4:]
        order_fields(parts, fields)
        state_in = fields.at[4]
    else:
        (fields, state_in, send, slip_out, state_out), refs = refs[:5], refs[5:]
    rest_out, (total, sources, acc) = refs[:-3], refs[-3:]
    shear, normal = split_stress(*sum_messages(recv, total, own_blocks, n_src, n_rcv))
    slip_rate, next_state = friction_solve(
        shear, normal, step_no, guess[...], state_in[...], [fields[kind] for kind in range(4)]
    )
    spread_sources(slip_rate, sources)
    terms = new_terms(range(later + 1), panels, sources, gather, scatter, weights)
    acc[...] = encode(rest[0] + terms[0])
    pack_messages(send, lambda first, count: acc[pl.ds(first, count), :], own_blocks, n_src, dups)
    slip_out[...] = slip_rate
    state_out[...] = next_state
    for at in range(later):
        rest_out[0][at] = rest[at + 1] + terms[at + 1]


def last_kernel(
    recv, shear_pre, sigma_pre, friction_a, state_rate, state_in, *refs, step_no, n_src,
):
    slips, (slip_out, state_out, total) = refs[:step_no], refs[step_no:]
    pairs = slip_out.shape[1] // LANES
    mine = pl.ds(lax.axis_index("rcv") * pairs, pairs)
    shear, normal = split_stress(*sum_messages(recv, total, 2 * pairs, n_src, 1))
    fields = [ref[...] for ref in (shear_pre, sigma_pre, friction_a, state_rate)]
    slip_rate, next_state = friction_solve(
        shear, normal, step_no, slips[-1][mine, :], state_in[mine, :], fields
    )
    for step, field in enumerate([ref[mine, :] for ref in slips] + [slip_rate]):
        for row in range(pairs):
            slip_out[step:step + 1, row * LANES:(row + 1) * LANES] = field[row:row + 1]
    state_out[...] = next_state


def per_device(
    history, kernel, scales, block_rows, block_cols,
    shear_pre, sigma_pre, friction_a, state_rate, state_init,
):
    lags = kernel.shape[0]
    slots = kernel.shape[3]
    width = kernel.shape[4]
    n_src = lax.axis_size("src")
    n_rcv = lax.axis_size("rcv")
    own = shear_pre.shape[0]
    own_blocks = own // width
    pairs = own // LANES
    src_blocks = n_rcv * own_blocks
    recv_rows = n_src * own_blocks
    message = (ROWS, own_blocks // ROWS * LANES)
    panels = kernel.reshape(lags, slots, width, 2 * width)
    f32 = jnp.float32
    hbm = pl.BlockSpec(memory_space=pltpu.HBM)
    vmem = pl.BlockSpec(memory_space=pltpu.VMEM)
    sizes = dict(slots=slots, n_src=n_src, n_rcv=n_rcv, own_blocks=own_blocks)
    def shape(*dims, dtype=f32):
        return jax.ShapeDtypeStruct(dims, dtype)

    def call(body, ins, outs, scratch, name, args, flops, limit=VMEM_LIMIT, out_specs=None):
        return pl.pallas_call(
            body, in_specs=ins, out_specs=out_specs or [vmem] * len(outs), out_shape=outs, scratch_shapes=scratch,
            compiler_params=pltpu.CompilerParams(vmem_limit_bytes=limit), name=name,
            cost_estimate=pl.CostEstimate(flops=flops, bytes_accessed=flops // 64, transcendentals=0),
        )(*args)

    own_fields = [
        field.reshape(pairs, LANES)
        for field in (shear_pre, sigma_pre, friction_a, state_rate, state_init)
    ]
    own_hbm = [pltpu.with_memory_space_constraint(field, pltpu.HBM) for field in own_fields]

    panels, history, *table = [
        pltpu.with_memory_space_constraint(array, pltpu.HBM)
        for array in (panels, history, block_rows, block_cols, scales)
    ]
    one_lag = 2 * slots * width * 2 * width * 8
    send, rest, guess, recent, *tables, mine = call(
        functools.partial(older_kernel, lags=lags, n_fields=len(own_fields), **sizes),
        [hbm] * (5 + len(own_fields)),
        [
            shape(n_src, n_rcv, *message, dtype=jnp.bfloat16),
            shape(STEPS - 1, recv_rows, LANES),
            shape(src_blocks // 2, LANES),
            shape(STEPS - 1, slots, width, 2 * width, dtype=panels.dtype),
            shape(STEPS - 1, SLOT_ROWS, LANES, dtype=jnp.int32),
            shape(STEPS - 1, recv_rows, LANES, dtype=jnp.bfloat16),
            shape(STEPS - 1, SLOT_ROWS, LANES),
            shape(len(own_fields), pairs, LANES),
        ],
        [
            pltpu.VMEM(panels.shape, panels.dtype),
            pltpu.VMEM(history.shape, history.dtype),
            *[pltpu.SMEM(array.shape, array.dtype) for array in table],
            *[pltpu.VMEM((STEPS - 1, *array.shape[1:]), array.dtype) for array in table],
            pltpu.VMEM((LEAD + src_blocks * TAPS, LANES), f32),
            pltpu.VMEM((recv_rows * 8, LANES), f32),
            pltpu.VMEM((recv_rows * 8, LANES), f32),
            pltpu.VMEM((n_src, *message), jnp.bfloat16),
            pltpu.SemaphoreType.DMA((lags,)),
            pltpu.SemaphoreType.DMA((7 + len(own_fields),)),
            pltpu.SemaphoreType.DMA((n_rcv + 1,)),
        ],
        "older", [panels, history, *table, *own_hbm], 60 * one_lag, limit=32 * 1024 * 1024,
        out_specs=[hbm] + [vmem] * 7,
    )

    parts = [mine] + [
        lax.ppermute(mine, "rcv", [(at, at ^ turn) for at in range(n_rcv)]) for turn in range(1, n_rcv)
    ]
    slips = []
    recv = lax.all_to_all(send.reshape(n_src * n_rcv, *message), ("src", "rcv"), 0, 0, tiled=True)
    for step_no in range(STEPS - 1):
        last = step_no == STEPS - 2
        dups = 1 if last else n_rcv
        later = STEPS - 2 - step_no
        first = step_no == 0
        solve_inputs = parts if first else [fields, state]
        packed = shape(src_blocks // 2, LANES)
        send, slip_rate, state, *more = call(
            functools.partial(
                step_kernel, step_no=step_no, dups=dups, later=later,
                n_src=n_src, n_rcv=n_rcv, own_blocks=own_blocks,
            ),
            [vmem] * (7 + len(solve_inputs)),
            [shape(n_src * dups, *message, dtype=jnp.bfloat16), packed, packed]
            + [shape(len(own_fields), src_blocks // 2, LANES)] * first
            + [shape(later, recv_rows, LANES)] * bool(later),
            [
                pltpu.VMEM((src_blocks, LANES), f32),
                pltpu.VMEM((src_blocks, LANES), f32),
                pltpu.VMEM((recv_rows, LANES), f32),
            ],
            "step", [recv, guess, rest, recent, *tables, *solve_inputs], one_lag,
        )
        fields = more.pop(0) if first else fields
        guess = slip_rate
        rest = more[0] if later else rest
        slips.append(slip_rate)
        recv = lax.all_to_all(send, "src" if last else ("src", "rcv"), 0, 0, tiled=True)

    slip_rates, state = call(
        functools.partial(last_kernel, step_no=STEPS - 1, n_src=n_src),
        [vmem] * (6 + len(slips)),
        [shape(STEPS, own), shape(pairs, LANES)],
        [pltpu.VMEM((own_blocks, LANES), f32)],
        "last", [recv, *own_fields[:4], state, *slips], 10 ** 6,
    )
    return (slip_rates, state.reshape(own))


def solution(mesh):
    return jax.shard_map(
        per_device,
        mesh=mesh,
        in_specs=(
            P(None, "src"),
            P(None, "src", "rcv", None, None, None),
            P(None, "src", "rcv", None),
            P(None, "src", "rcv", None),
            P(None, "src", "rcv", None),
            P(("src", "rcv")),
            P(("src", "rcv")),
            P(("src", "rcv")),
            P(("src", "rcv")),
            P(("src", "rcv")),
        ),
        out_specs=(P(None, ("src", "rcv")), P(("src", "rcv"))),
        check_vma=False,
    )
```

```python
import functools

import jax
import jax.numpy as jnp
from jax import lax
from jax.experimental import pallas as pl
from jax.experimental.pallas import tpu as pltpu
from jax.sharding import PartitionSpec as P

STEPS = 4
NEWTON_ITERS = 4
DAMPING = 1.0
LOADING = 0.05
TIME_STEP = 0.2
LANES = 128
HALF = LANES // 2
ROWS = 4
IN_FLIGHT = 8
GROUP = 4
SLOT_ROWS = 32
PARTS = 3
MESSAGE_BITS = 22
MESSAGE_SCALE = 2.0 ** MESSAGE_BITS
TAPS = 24
LEAD = 8
VMEM_LIMIT = 16 * 1024 * 1024


def inverse_sinh(value, root):
    result = jnp.log(jnp.abs(value) + root)
    return jnp.where(value < 0.0, -result, result)


def friction_solve(shear, normal_stress, step_no, guess, state_now, fields):
    shear_pre, sigma_pre, friction_a, state_rate = fields
    shear_total = shear + shear_pre + LOADING * (step_no + 1)
    normal = sigma_pre * (1.0 + 0.5 * jnp.tanh(normal_stress))
    strength = friction_a * normal
    factor = 0.5 * jnp.exp(state_now)
    slip_rate = guess
    for attempt in range(NEWTON_ITERS):
        scaled = slip_rate * factor
        root = jnp.sqrt(1.0 + scaled * scaled)
        misfit = shear_total - DAMPING * slip_rate - strength * inverse_sinh(scaled, root)
        derivative = -DAMPING - strength * factor / root
        slip_rate = slip_rate - misfit / derivative
    next_state = state_now + TIME_STEP * state_rate * jnp.tanh(
        jnp.exp(-state_now) - jnp.abs(slip_rate)
    )
    return slip_rate, next_state


def split_stress(even, odd):
    low = lax.broadcasted_iota(jnp.int32, even.shape, 1) < HALF
    shear = jnp.where(low, even, pltpu.roll(odd, HALF, 1))
    normal = jnp.where(low, pltpu.roll(even, HALF, 1), odd)
    return shear, normal


def encode(partial):
    scaled = partial * (1.0 / MESSAGE_SCALE)
    return scaled * scaled * scaled


def decode(message):
    cube = message.astype(jnp.float32)
    root = jnp.exp2(jnp.log2(jnp.abs(cube)) * (1.0 / 3.0) + MESSAGE_BITS)
    return jnp.where(cube < 0.0, -root, root)


def pack_messages(send, partials, own_blocks, n_dest, dups):
    for dest in range(n_dest):
        for tile in range(own_blocks // ROWS):
            piece = partials(dest * own_blocks + tile * ROWS, ROWS).astype(jnp.bfloat16)
            for dup in range(dups):
                send[dest * dups + dup, :, tile * LANES:(tile + 1) * LANES] = piece


def sum_messages(recv, total, own_blocks, n_src, owners):
    for owner in range(owners):
        part = decode(recv[owner])
        for src in range(1, n_src):
            part = part + decode(recv[src * owners + owner])
        for tile in range(own_blocks // ROWS):
            first = owner * own_blocks + tile * ROWS
            total[first:first + ROWS, :] = part[:, tile * LANES:(tile + 1) * LANES]
    pairs = owners * own_blocks // 2
    return total[pl.ds(0, pairs, stride=2), :], total[pl.ds(1, pairs, stride=2), :]


def make_tables(rows, cols, scales, gather, scatter, weights):
    slots = rows.shape[-1]
    lane = lax.broadcasted_iota(jnp.int32, (SLOT_ROWS, LANES), 1)
    diagonal = lax.broadcasted_iota(jnp.int32, (SLOT_ROWS, LANES), 0) == lane
    rest = jnp.full((1, LANES - slots), -1.0, jnp.float32)

    def widened(values):
        return jnp.concatenate([values.astype(jnp.float32), rest], axis=1)

    def column(values):
        spread = jnp.where(diagonal, jnp.broadcast_to(values, diagonal.shape), 0.0)
        return jnp.sum(spread, axis=1, keepdims=True)

    one_row = lax.broadcasted_iota(jnp.int32, (1, LANES), 1)
    block = lax.broadcasted_iota(jnp.int32, (scatter.shape[1], LANES), 0).astype(jnp.float32)
    for lag in range(STEPS - 1):
        row_ids = widened(rows[lag, 0])
        for part in range(1, PARTS):
            at = one_row >= part * SLOT_ROWS
            row_ids = jnp.where(at, pltpu.roll(widened(rows[lag, 0]), part * SLOT_ROWS, 1), row_ids)
        row_ids = jnp.where(one_row < PARTS * SLOT_ROWS, row_ids, -1.0)
        scatter[lag] = (block == row_ids).astype(jnp.float32).astype(jnp.bfloat16)
        picks = jnp.maximum(column(widened(cols[lag, 0])), 0.0).astype(jnp.int32)
        gather[lag] = jnp.broadcast_to(picks, gather.shape[1:])
        weights[lag] = jnp.broadcast_to(column(widened(scales[lag, 0])), weights.shape[1:])


def older_kernel(
    panels, history, rows_in, cols_in, scales_in, *refs,
    lags, slots, n_src, n_rcv, own_blocks, n_fields,
):
    own_fields, refs = refs[:n_fields], refs[n_fields:]
    send, rest, guess, recent, gather, scatter, weights, fields, *refs = refs
    (
        panel_buf, history_buf, rows, cols, scales, rows_now, cols_now, scales_now, sources, acc_low, acc_high, messages,
        sems, small_sems, out_sems,
    ) = refs
    src_blocks = n_rcv * own_blocks
    recv_blocks = n_src * own_blocks
    recent_lags = pl.ds(0, STEPS - 1)
    smalls = [
        pltpu.make_async_copy(source, target, small_sems.at[at])
        for at, (source, target) in enumerate([
            (history, history_buf), (cols_in, cols), (rows_in, rows), (scales_in, scales),
            (rows_in.at[recent_lags], rows_now), (cols_in.at[recent_lags], cols_now),
            (scales_in.at[recent_lags], scales_now),
            *[(field, fields.at[at]) for at, field in enumerate(own_fields)],
        ])
    ]

    def panel_copy(lag):
        return pltpu.make_async_copy(panels.at[lag], panel_buf.at[lag], sems.at[lag])

    for copy in smalls:
        copy.start()
    for lag in range(IN_FLIGHT):
        panel_copy(lag).start()
    accs = (acc_low, acc_high)
    for acc in accs:
        acc[...] = jnp.zeros_like(acc)
    tail = jnp.zeros((TAPS - lags, LANES), jnp.float32)
    sources[0:LEAD, :] = jnp.zeros((LEAD, LANES), jnp.float32)
    smalls[0].wait()
    for pair in range(src_blocks // 2):
        tile = history_buf[:, pair * LANES:(pair + 1) * LANES].astype(jnp.float32)
        for half in range(2):
            base = LEAD + (2 * pair + half) * TAPS
            sources[base:base + lags, :] = tile if half == 0 else pltpu.roll(tile, HALF, 1)
            sources[base + lags:base + TAPS, :] = tail
    for copy in smalls[1:7]:
        copy.wait()
    top = lax.broadcasted_iota(jnp.int32, (8, LANES), 0) < STEPS
    match = top == (lax.broadcasted_iota(jnp.int32, (8, LANES), 1) < HALF)
    zero = jnp.zeros((8, LANES), jnp.float32)

    def one_lag(lag, carry):
        panel_copy(lag).wait()

        @pl.when(lag + IN_FLIGHT < lags)
        def _():
            panel_copy(lag + IN_FLIGHT).start()

        first_tap = LEAD + (lags - 1) - lag
        for group in range(0, slots, GROUP):
            pairs = []
            for slot in range(group, group + GROUP, 2):
                low = sources[pl.ds(cols[lag, 0, 0, slot] * TAPS + first_tap, 8), :]
                partner = cols[lag, 0, 0, slot + 1] ^ 1
                high = sources[pl.ds(partner * TAPS + first_tap - STEPS, 8), :]
                pairs.append(jnp.where(match, jnp.where(top, low, high), 0.0))
            columns = [
                jnp.concatenate([pair if at == to else zero for at in range(len(pairs))], axis=0)
                for to, pair in enumerate(pairs)
            ]
            picked = jnp.concatenate(columns, axis=1).astype(jnp.bfloat16)
            panel = panel_buf[lag, group:group + GROUP].reshape(GROUP * HALF, LANES)
            terms = jnp.dot(picked, panel, preferred_element_type=jnp.float32)
            for pair in range(len(pairs)):
                slot = group + 2 * pair
                scale = jnp.where(top, scales[lag, 0, 0, slot], scales[lag, 0, 0, slot + 1])
                term = terms[8 * pair:8 * pair + 8] * scale
                for part, acc in enumerate(accs):
                    at = pl.ds(pl.multiple_of(rows[lag, 0, 0, slot + part] * 8, 8), 8)
                    acc[at, :] = acc[at, :] + term
        return carry

    lax.fori_loop(0, lags, one_lag, 0, unroll=2)
    def partials(first_row, count, step):
        low, high = [
            acc[pl.ds(first_row * 8 + part * STEPS + step, count, stride=8), :]
            for part, acc in enumerate(accs)
        ]
        return low + high

    pack_messages(messages, lambda first, count: encode(partials(first, count, 0)), own_blocks, n_src, 1)
    outgoing = [
        pltpu.make_async_copy(messages, send.at[:, dup], out_sems.at[dup]) for dup in range(n_rcv)
    ]
    outgoing.append(pltpu.make_async_copy(panel_buf.at[recent_lags], recent, out_sems.at[n_rcv]))
    for copy in outgoing:
        copy.start()
    make_tables(rows_now, cols_now, scales_now, gather, scatter, weights)
    for step in range(1, STEPS):
        rest[step - 1] = partials(0, recv_blocks, step)
    guess[...] = sources[pl.ds(LEAD + lags - 1, src_blocks // 2, stride=2 * TAPS), :]
    for copy in outgoing + smalls[7:]:
        copy.wait()


def spread_sources(slip_rate, sources):
    pairs = slip_rate.shape[0]
    low = lax.broadcasted_iota(jnp.int32, slip_rate.shape, 1) < HALF
    turned = pltpu.roll(slip_rate, HALF, 1)
    sources[pl.ds(0, pairs, stride=2), :] = jnp.where(low, slip_rate, turned)
    sources[pl.ds(1, pairs, stride=2), :] = jnp.where(low, turned, slip_rate)


def take_rows(groups, rows):
    taken = []
    for first in range(0, rows.shape[0], 8):
        row = rows[first:first + 8]
        within = row & 7
        block = row - within
        piece = jnp.zeros(groups[0].shape, jnp.float32)
        for at, group in enumerate(groups):
            found = jnp.take_along_axis(group, within, axis=0, mode="promise_in_bounds")
            piece = jnp.where(block == 8 * at, found, piece)
        taken.append(piece)
    return jnp.concatenate(taken, axis=0)


def new_terms(lags, panels, sources, gather, scatter, weights):
    slots, width, wide = panels.shape[1:]
    groups = [sources[at:at + 8, :] for at in range(0, sources.shape[0], 8)]
    picked = [take_rows(groups, gather[lag]) for lag in lags]
    lane = lax.broadcasted_iota(jnp.int32, picked[0].shape, 1)
    row = lax.broadcasted_iota(jnp.int32, picked[0].shape, 0)
    first = row - jnp.where(lane < HALF, 0, 1)
    terms = []
    for lag, rates in zip(lags, picked):
        tiles = [
            jnp.where(first == slot, rates, 0.0).astype(jnp.bfloat16) for slot in range(0, slots, 2)
        ]
        panel = panels[lag].reshape(slots * width, wide)
        terms.append(
            jnp.dot(jnp.concatenate(tiles, axis=1), panel, preferred_element_type=jnp.float32)
        )
    sums = []
    for lag, left in zip(lags, terms):
        left = left * weights[lag]
        parts = []
        for part in range(PARTS):
            parts.append(left.astype(jnp.bfloat16))
            left = left - parts[-1].astype(jnp.float32)
        stacked = jnp.concatenate(parts, axis=0)
        table = scatter[lag][:, :stacked.shape[0]]
        sums.append(jnp.dot(table, stacked, preferred_element_type=jnp.float32))
    return sums


def order_fields(parts, fields):
    here = lax.axis_index("rcv")
    pairs = parts[0].shape[1]
    for owner in range(len(parts)):
        chosen = parts[0][...]
        for turn in range(1, len(parts)):
            chosen = jnp.where(here ^ owner == turn, parts[turn][...], chosen)
        for kind in range(fields.shape[0]):
            fields[kind, owner * pairs:(owner + 1) * pairs, :] = chosen[kind]


def step_kernel(
    recv, guess, rest, panels, gather, scatter, weights, *refs,
    step_no, n_src, n_rcv, own_blocks, dups, later,
):
    if step_no == 0:
        parts, (send, slip_out, state_out, fields), refs = refs[:n_rcv], refs[n_rcv:n_rcv + 4], refs[n_rcv + 4:]
        order_fields(parts, fields)
        state_in = fields.at[4]
    else:
        (fields, state_in, send, slip_out, state_out), refs = refs[:5], refs[5:]
    rest_out, (total, sources, acc) = refs[:-3], refs[-3:]
    shear, normal = split_stress(*sum_messages(recv, total, own_blocks, n_src, n_rcv))
    slip_rate, next_state = friction_solve(
        shear, normal, step_no, guess[...], state_in[...], [fields[kind] for kind in range(4)]
    )
    spread_sources(slip_rate, sources)
    terms = new_terms(range(later + 1), panels, sources, gather, scatter, weights)
    acc[...] = encode(rest[0] + terms[0])
    pack_messages(send, lambda first, count: acc[pl.ds(first, count), :], own_blocks, n_src, dups)
    slip_out[...] = slip_rate
    state_out[...] = next_state
    for at in range(later):
        rest_out[0][at] = rest[at + 1] + terms[at + 1]


def last_kernel(
    recv, shear_pre, sigma_pre, friction_a, state_rate, state_in, *refs, step_no, n_src,
):
    slips, (slip_out, state_out, total) = refs[:step_no], refs[step_no:]
    pairs = slip_out.shape[1] // LANES
    mine = pl.ds(lax.axis_index("rcv") * pairs, pairs)
    shear, normal = split_stress(*sum_messages(recv, total, 2 * pairs, n_src, 1))
    fields = [ref[...] for ref in (shear_pre, sigma_pre, friction_a, state_rate)]
    slip_rate, next_state = friction_solve(
        shear, normal, step_no, slips[-1][mine, :], state_in[mine, :], fields
    )
    for step, field in enumerate([ref[mine, :] for ref in slips] + [slip_rate]):
        for row in range(pairs):
            slip_out[step:step + 1, row * LANES:(row + 1) * LANES] = field[row:row + 1]
    state_out[...] = next_state


def per_device(
    history, kernel, scales, block_rows, block_cols,
    shear_pre, sigma_pre, friction_a, state_rate, state_init,
):
    lags = kernel.shape[0]
    slots = kernel.shape[3]
    width = kernel.shape[4]
    n_src = lax.axis_size("src")
    n_rcv = lax.axis_size("rcv")
    own = shear_pre.shape[0]
    own_blocks = own // width
    pairs = own // LANES
    src_blocks = n_rcv * own_blocks
    recv_rows = n_src * own_blocks
    message = (ROWS, own_blocks // ROWS * LANES)
    panels = kernel.reshape(lags, slots, width, 2 * width)
    f32 = jnp.float32
    hbm = pl.BlockSpec(memory_space=pltpu.HBM)
    vmem = pl.BlockSpec(memory_space=pltpu.VMEM)
    sizes = dict(slots=slots, n_src=n_src, n_rcv=n_rcv, own_blocks=own_blocks)
    def shape(*dims, dtype=f32):
        return jax.ShapeDtypeStruct(dims, dtype)

    def call(body, ins, outs, scratch, name, args, flops, limit=VMEM_LIMIT, out_specs=None):
        return pl.pallas_call(
            body, in_specs=ins, out_specs=out_specs or [vmem] * len(outs), out_shape=outs, scratch_shapes=scratch,
            compiler_params=pltpu.CompilerParams(vmem_limit_bytes=limit), name=name,
            cost_estimate=pl.CostEstimate(flops=flops, bytes_accessed=flops // 64, transcendentals=0),
        )(*args)

    own_fields = [
        field.reshape(pairs, LANES)
        for field in (shear_pre, sigma_pre, friction_a, state_rate, state_init)
    ]
    own_hbm = [pltpu.with_memory_space_constraint(field, pltpu.HBM) for field in own_fields]

    panels, history, *table = [
        pltpu.with_memory_space_constraint(array, pltpu.HBM)
        for array in (panels, history, block_rows, block_cols, scales)
    ]
    one_lag = 2 * slots * width * 2 * width * 8
    send, rest, guess, recent, *tables, mine = call(
        functools.partial(older_kernel, lags=lags, n_fields=len(own_fields), **sizes),
        [hbm] * (5 + len(own_fields)),
        [
            shape(n_src, n_rcv, *message, dtype=jnp.bfloat16),
            shape(STEPS - 1, recv_rows, LANES),
            shape(src_blocks // 2, LANES),
            shape(STEPS - 1, slots, width, 2 * width, dtype=panels.dtype),
            shape(STEPS - 1, SLOT_ROWS, LANES, dtype=jnp.int32),
            shape(STEPS - 1, recv_rows, LANES, dtype=jnp.bfloat16),
            shape(STEPS - 1, SLOT_ROWS, LANES),
            shape(len(own_fields), pairs, LANES),
        ],
        [
            pltpu.VMEM(panels.shape, panels.dtype),
            pltpu.VMEM(history.shape, history.dtype),
            *[pltpu.SMEM(array.shape, array.dtype) for array in table],
            *[pltpu.VMEM((STEPS - 1, *array.shape[1:]), array.dtype) for array in table],
            pltpu.VMEM((LEAD + src_blocks * TAPS, LANES), f32),
            pltpu.VMEM((recv_rows * 8, LANES), f32),
            pltpu.VMEM((recv_rows * 8, LANES), f32),
            pltpu.VMEM((n_src, *message), jnp.bfloat16),
            pltpu.SemaphoreType.DMA((lags,)),
            pltpu.SemaphoreType.DMA((7 + len(own_fields),)),
            pltpu.SemaphoreType.DMA((n_rcv + 1,)),
        ],
        "older", [panels, history, *table, *own_hbm], 60 * one_lag, limit=32 * 1024 * 1024,
        out_specs=[hbm] + [vmem] * 7,
    )

    parts = [mine] + [
        lax.ppermute(mine, "rcv", [(at, at ^ turn) for at in range(n_rcv)]) for turn in range(1, n_rcv)
    ]
    slips = []
    recv = lax.all_to_all(send.reshape(n_src * n_rcv, *message), ("src", "rcv"), 0, 0, tiled=True)
    for step_no in range(STEPS - 1):
        last = step_no == STEPS - 2
        dups = 1 if last else n_rcv
        later = STEPS - 2 - step_no
        first = step_no == 0
        solve_inputs = parts if first else [fields, state]
        packed = shape(src_blocks // 2, LANES)
        send, slip_rate, state, *more = call(
            functools.partial(
                step_kernel, step_no=step_no, dups=dups, later=later,
                n_src=n_src, n_rcv=n_rcv, own_blocks=own_blocks,
            ),
            [vmem] * (7 + len(solve_inputs)),
            [shape(n_src * dups, *message, dtype=jnp.bfloat16), packed, packed]
            + [shape(len(own_fields), src_blocks // 2, LANES)] * first
            + [shape(later, recv_rows, LANES)] * bool(later),
            [
                pltpu.VMEM((src_blocks, LANES), f32),
                pltpu.VMEM((src_blocks, LANES), f32),
                pltpu.VMEM((recv_rows, LANES), f32),
            ],
            "step", [recv, guess, rest, recent, *tables, *solve_inputs], one_lag,
        )
        fields = more.pop(0) if first else fields
        guess = slip_rate
        rest = more[0] if later else rest
        slips.append(slip_rate)
        recv = lax.all_to_all(send, "src" if last else ("src", "rcv"), 0, 0, tiled=True)

    slip_rates, state = call(
        functools.partial(last_kernel, step_no=STEPS - 1, n_src=n_src),
        [vmem] * (6 + len(slips)),
        [shape(STEPS, own), shape(pairs, LANES)],
        [pltpu.VMEM((own_blocks, LANES), f32)],
        "last", [recv, *own_fields[:4], state, *slips], 10 ** 6,
    )
    return (slip_rates, state.reshape(own))


def solution(mesh):
    return jax.shard_map(
        per_device,
        mesh=mesh,
        in_specs=(
            P(None, "src"),
            P(None, "src", "rcv", None, None, None),
            P(None, "src", "rcv", None),
            P(None, "src", "rcv", None),
            P(None, "src", "rcv", None),
            P(("src", "rcv")),
            P(("src", "rcv")),
            P(("src", "rcv")),
            P(("src", "rcv")),
            P(("src", "rcv")),
        ),
        out_specs=(P(None, ("src", "rcv")), P(("src", "rcv"))),
        check_vma=False,
    )
```

```python
import functools

import jax
import jax.numpy as jnp
from jax import lax
from jax.experimental import pallas as pl
from jax.experimental.pallas import tpu as pltpu
from jax.sharding import PartitionSpec as P

STEPS = 4
NEWTON_ITERS = 4
DAMPING = 1.0
LOADING = 0.05
TIME_STEP = 0.2
LANES = 128
HALF = LANES // 2
ROWS = 4
IN_FLIGHT = 8
GROUP = 4
SLOT_ROWS = 32
PARTS = 3
MESSAGE_BITS = 22
MESSAGE_SCALE = 2.0 ** MESSAGE_BITS
TAPS = 24
LEAD = 8
VMEM_LIMIT = 16 * 1024 * 1024


def inverse_sinh(value, root):
    result = jnp.log(jnp.abs(value) + root)
    return jnp.where(value < 0.0, -result, result)


def friction_solve(shear, normal_stress, step_no, guess, state_now, fields):
    shear_pre, sigma_pre, friction_a, state_rate = fields
    shear_total = shear + shear_pre + LOADING * (step_no + 1)
    normal = sigma_pre * (1.0 + 0.5 * jnp.tanh(normal_stress))
    strength = friction_a * normal
    factor = 0.5 * jnp.exp(state_now)
    slip_rate = guess
    for attempt in range(NEWTON_ITERS):
        scaled = slip_rate * factor
        square = 1.0 + scaled * scaled
        inverse_root = lax.rsqrt(square)
        misfit = shear_total - DAMPING * slip_rate - strength * inverse_sinh(scaled, square * inverse_root)
        derivative = -DAMPING - strength * factor * inverse_root
        slip_rate = slip_rate - misfit / derivative
    next_state = state_now + TIME_STEP * state_rate * jnp.tanh(
        jnp.exp(-state_now) - jnp.abs(slip_rate)
    )
    return slip_rate, next_state


def split_stress(even, odd):
    low = lax.broadcasted_iota(jnp.int32, even.shape, 1) < HALF
    shear = jnp.where(low, even, pltpu.roll(odd, HALF, 1))
    normal = jnp.where(low, pltpu.roll(even, HALF, 1), odd)
    return shear, normal


def encode(partial):
    scaled = partial * (1.0 / MESSAGE_SCALE)
    return scaled * scaled * scaled


def decode(message):
    cube = message.astype(jnp.float32)
    root = jnp.exp2(jnp.log2(jnp.abs(cube)) * (1.0 / 3.0) + MESSAGE_BITS)
    return jnp.where(cube < 0.0, -root, root)


def pack_messages(send, partials, own_blocks, n_dest, dups):
    for dest in range(n_dest):
        for tile in range(own_blocks // ROWS):
            piece = partials(dest * own_blocks + tile * ROWS, ROWS).astype(jnp.bfloat16)
            for dup in range(dups):
                send[dest * dups + dup, :, tile * LANES:(tile + 1) * LANES] = piece


def sum_messages(recv, total, own_blocks, n_src, owners):
    for owner in range(owners):
        part = decode(recv[owner])
        for src in range(1, n_src):
            part = part + decode(recv[src * owners + owner])
        for tile in range(own_blocks // ROWS):
            first = owner * own_blocks + tile * ROWS
            total[first:first + ROWS, :] = part[:, tile * LANES:(tile + 1) * LANES]
    pairs = owners * own_blocks // 2
    return total[pl.ds(0, pairs, stride=2), :], total[pl.ds(1, pairs, stride=2), :]


def make_tables(rows, cols, scales, gather, scatter, weights):
    slots = rows.shape[-1]
    lane = lax.broadcasted_iota(jnp.int32, (SLOT_ROWS, LANES), 1)
    diagonal = lax.broadcasted_iota(jnp.int32, (SLOT_ROWS, LANES), 0) == lane
    rest = jnp.full((1, LANES - slots), -1.0, jnp.float32)

    def widened(values):
        return jnp.concatenate([values.astype(jnp.float32), rest], axis=1)

    def column(values):
        spread = jnp.where(diagonal, jnp.broadcast_to(values, diagonal.shape), 0.0)
        return jnp.sum(spread, axis=1, keepdims=True)

    one_row = lax.broadcasted_iota(jnp.int32, (1, LANES), 1)
    block = lax.broadcasted_iota(jnp.int32, (scatter.shape[1], LANES), 0).astype(jnp.float32)
    for lag in range(STEPS - 1):
        row_ids = widened(rows[lag, 0])
        for part in range(1, PARTS):
            at = one_row >= part * SLOT_ROWS
            row_ids = jnp.where(at, pltpu.roll(widened(rows[lag, 0]), part * SLOT_ROWS, 1), row_ids)
        row_ids = jnp.where(one_row < PARTS * SLOT_ROWS, row_ids, -1.0)
        scatter[lag] = (block == row_ids).astype(jnp.float32).astype(jnp.bfloat16)
        picks = jnp.maximum(column(widened(cols[lag, 0])), 0.0).astype(jnp.int32)
        gather[lag] = jnp.broadcast_to(picks, gather.shape[1:])
        weights[lag] = jnp.broadcast_to(column(widened(scales[lag, 0])), weights.shape[1:])


def older_kernel(
    panels, history, rows_in, cols_in, scales_in, *refs,
    lags, slots, n_src, n_rcv, own_blocks, n_fields,
):
    own_fields, refs = refs[:n_fields], refs[n_fields:]
    send, rest, guess, recent, gather, scatter, weights, fields, *refs = refs
    (
        panel_buf, history_buf, rows, cols, scales, rows_now, cols_now, scales_now, sources, acc_low, acc_high, messages,
        sems, small_sems, out_sems,
    ) = refs
    src_blocks = n_rcv * own_blocks
    recv_blocks = n_src * own_blocks
    recent_lags = pl.ds(0, STEPS - 1)
    smalls = [
        pltpu.make_async_copy(source, target, small_sems.at[at])
        for at, (source, target) in enumerate([
            (history, history_buf), (cols_in, cols), (rows_in, rows), (scales_in, scales),
            (rows_in.at[recent_lags], rows_now), (cols_in.at[recent_lags], cols_now),
            (scales_in.at[recent_lags], scales_now),
            *[(field, fields.at[at]) for at, field in enumerate(own_fields)],
        ])
    ]

    def panel_copy(lag):
        return pltpu.make_async_copy(panels.at[lag], panel_buf.at[lag], sems.at[lag])

    for copy in smalls:
        copy.start()
    for lag in range(IN_FLIGHT):
        panel_copy(lag).start()
    accs = (acc_low, acc_high)
    for acc in accs:
        acc[...] = jnp.zeros_like(acc)
    tail = jnp.zeros((TAPS - lags, LANES), jnp.float32)
    sources[0:LEAD, :] = jnp.zeros((LEAD, LANES), jnp.float32)
    smalls[0].wait()
    for pair in range(src_blocks // 2):
        tile = history_buf[:, pair * LANES:(pair + 1) * LANES].astype(jnp.float32)
        for half in range(2):
            base = LEAD + (2 * pair + half) * TAPS
            sources[base:base + lags, :] = tile if half == 0 else pltpu.roll(tile, HALF, 1)
            sources[base + lags:base + TAPS, :] = tail
    for copy in smalls[1:7]:
        copy.wait()
    top = lax.broadcasted_iota(jnp.int32, (8, LANES), 0) < STEPS
    match = top == (lax.broadcasted_iota(jnp.int32, (8, LANES), 1) < HALF)
    zero = jnp.zeros((8, LANES), jnp.float32)

    def one_lag(lag, carry):
        panel_copy(lag).wait()

        @pl.when(lag + IN_FLIGHT < lags)
        def _():
            panel_copy(lag + IN_FLIGHT).start()

        first_tap = LEAD + (lags - 1) - lag
        for group in range(0, slots, GROUP):
            pairs = []
            for slot in range(group, group + GROUP, 2):
                low = sources[pl.ds(cols[lag, 0, 0, slot] * TAPS + first_tap, 8), :]
                partner = cols[lag, 0, 0, slot + 1] ^ 1
                high = sources[pl.ds(partner * TAPS + first_tap - STEPS, 8), :]
                pairs.append(jnp.where(match, jnp.where(top, low, high), 0.0))
            columns = [
                jnp.concatenate([pair if at == to else zero for at in range(len(pairs))], axis=0)
                for to, pair in enumerate(pairs)
            ]
            picked = jnp.concatenate(columns, axis=1).astype(jnp.bfloat16)
            panel = panel_buf[lag, group:group + GROUP].reshape(GROUP * HALF, LANES)
            terms = jnp.dot(picked, panel, preferred_element_type=jnp.float32)
            for pair in range(len(pairs)):
                slot = group + 2 * pair
                scale = jnp.where(top, scales[lag, 0, 0, slot], scales[lag, 0, 0, slot + 1])
                term = terms[8 * pair:8 * pair + 8] * scale
                for part, acc in enumerate(accs):
                    at = pl.ds(pl.multiple_of(rows[lag, 0, 0, slot + part] * 8, 8), 8)
                    acc[at, :] = acc[at, :] + term
        return carry

    lax.fori_loop(0, lags, one_lag, 0, unroll=2)
    def partials(first_row, count, step):
        low, high = [
            acc[pl.ds(first_row * 8 + part * STEPS + step, count, stride=8), :]
            for part, acc in enumerate(accs)
        ]
        return low + high

    pack_messages(messages, lambda first, count: encode(partials(first, count, 0)), own_blocks, n_src, 1)
    outgoing = [
        pltpu.make_async_copy(messages, send.at[:, dup], out_sems.at[dup]) for dup in range(n_rcv)
    ]
    outgoing.append(pltpu.make_async_copy(panel_buf.at[recent_lags], recent, out_sems.at[n_rcv]))
    for copy in outgoing:
        copy.start()
    make_tables(rows_now, cols_now, scales_now, gather, scatter, weights)
    for step in range(1, STEPS):
        rest[step - 1] = partials(0, recv_blocks, step)
    guess[...] = sources[pl.ds(LEAD + lags - 1, src_blocks // 2, stride=2 * TAPS), :]
    for copy in outgoing + smalls[7:]:
        copy.wait()


def spread_sources(slip_rate, sources):
    pairs = slip_rate.shape[0]
    low = lax.broadcasted_iota(jnp.int32, slip_rate.shape, 1) < HALF
    turned = pltpu.roll(slip_rate, HALF, 1)
    sources[pl.ds(0, pairs, stride=2), :] = jnp.where(low, slip_rate, turned)
    sources[pl.ds(1, pairs, stride=2), :] = jnp.where(low, turned, slip_rate)


def take_rows(groups, rows):
    taken = []
    for first in range(0, rows.shape[0], 8):
        row = rows[first:first + 8]
        within = row & 7
        block = row - within
        piece = jnp.zeros(groups[0].shape, jnp.float32)
        for at, group in enumerate(groups):
            found = jnp.take_along_axis(group, within, axis=0, mode="promise_in_bounds")
            piece = jnp.where(block == 8 * at, found, piece)
        taken.append(piece)
    return jnp.concatenate(taken, axis=0)


def new_terms(lags, panels, sources, gather, scatter, weights):
    slots, width, wide = panels.shape[1:]
    groups = [sources[at:at + 8, :] for at in range(0, sources.shape[0], 8)]
    picked = [take_rows(groups, gather[lag]) for lag in lags]
    lane = lax.broadcasted_iota(jnp.int32, picked[0].shape, 1)
    row = lax.broadcasted_iota(jnp.int32, picked[0].shape, 0)
    first = row - jnp.where(lane < HALF, 0, 1)
    terms = []
    for lag, rates in zip(lags, picked):
        tiles = [
            jnp.where(first == slot, rates, 0.0).astype(jnp.bfloat16) for slot in range(0, slots, 2)
        ]
        panel = panels[lag].reshape(slots * width, wide)
        terms.append(
            jnp.dot(jnp.concatenate(tiles, axis=1), panel, preferred_element_type=jnp.float32)
        )
    sums = []
    for lag, left in zip(lags, terms):
        left = left * weights[lag]
        parts = []
        for part in range(PARTS):
            parts.append(left.astype(jnp.bfloat16))
            left = left - parts[-1].astype(jnp.float32)
        stacked = jnp.concatenate(parts, axis=0)
        table = scatter[lag][:, :stacked.shape[0]]
        sums.append(jnp.dot(table, stacked, preferred_element_type=jnp.float32))
    return sums


def order_fields(parts, fields):
    here = lax.axis_index("rcv")
    pairs = parts[0].shape[1]
    for owner in range(len(parts)):
        chosen = parts[0][...]
        for turn in range(1, len(parts)):
            chosen = jnp.where(here ^ owner == turn, parts[turn][...], chosen)
        for kind in range(fields.shape[0]):
            fields[kind, owner * pairs:(owner + 1) * pairs, :] = chosen[kind]


def step_kernel(
    recv, guess, rest, panels, gather, scatter, weights, *refs,
    step_no, n_src, n_rcv, own_blocks, dups, later,
):
    if step_no == 0:
        parts, (send, slip_out, state_out, fields), refs = refs[:n_rcv], refs[n_rcv:n_rcv + 4], refs[n_rcv + 4:]
        order_fields(parts, fields)
        state_in = fields.at[4]
    else:
        (fields, state_in, send, slip_out, state_out), refs = refs[:5], refs[5:]
    rest_out, (total, sources, acc) = refs[:-3], refs[-3:]
    shear, normal = split_stress(*sum_messages(recv, total, own_blocks, n_src, n_rcv))
    slip_rate, next_state = friction_solve(
        shear, normal, step_no, guess[...], state_in[...], [fields[kind] for kind in range(4)]
    )
    spread_sources(slip_rate, sources)
    terms = new_terms(range(later + 1), panels, sources, gather, scatter, weights)
    acc[...] = encode(rest[0] + terms[0])
    pack_messages(send, lambda first, count: acc[pl.ds(first, count), :], own_blocks, n_src, dups)
    slip_out[...] = slip_rate
    state_out[...] = next_state
    for at in range(later):
        rest_out[0][at] = rest[at + 1] + terms[at + 1]


def last_kernel(
    recv, shear_pre, sigma_pre, friction_a, state_rate, state_in, *refs, step_no, n_src,
):
    slips, (slip_out, state_out, total) = refs[:step_no], refs[step_no:]
    pairs = slip_out.shape[1] // LANES
    mine = pl.ds(lax.axis_index("rcv") * pairs, pairs)
    shear, normal = split_stress(*sum_messages(recv, total, 2 * pairs, n_src, 1))
    fields = [ref[...] for ref in (shear_pre, sigma_pre, friction_a, state_rate)]
    slip_rate, next_state = friction_solve(
        shear, normal, step_no, slips[-1][mine, :], state_in[mine, :], fields
    )
    for step, field in enumerate([ref[mine, :] for ref in slips] + [slip_rate]):
        for row in range(pairs):
            slip_out[step:step + 1, row * LANES:(row + 1) * LANES] = field[row:row + 1]
    state_out[...] = next_state


def per_device(
    history, kernel, scales, block_rows, block_cols,
    shear_pre, sigma_pre, friction_a, state_rate, state_init,
):
    lags = kernel.shape[0]
    slots = kernel.shape[3]
    width = kernel.shape[4]
    n_src = lax.axis_size("src")
    n_rcv = lax.axis_size("rcv")
    own = shear_pre.shape[0]
    own_blocks = own // width
    pairs = own // LANES
    src_blocks = n_rcv * own_blocks
    recv_rows = n_src * own_blocks
    message = (ROWS, own_blocks // ROWS * LANES)
    panels = kernel.reshape(lags, slots, width, 2 * width)
    f32 = jnp.float32
    hbm = pl.BlockSpec(memory_space=pltpu.HBM)
    vmem = pl.BlockSpec(memory_space=pltpu.VMEM)
    sizes = dict(slots=slots, n_src=n_src, n_rcv=n_rcv, own_blocks=own_blocks)
    def shape(*dims, dtype=f32):
        return jax.ShapeDtypeStruct(dims, dtype)

    def call(body, ins, outs, scratch, name, args, flops, limit=VMEM_LIMIT, out_specs=None):
        return pl.pallas_call(
            body, in_specs=ins, out_specs=out_specs or [vmem] * len(outs), out_shape=outs, scratch_shapes=scratch,
            compiler_params=pltpu.CompilerParams(vmem_limit_bytes=limit), name=name,
            cost_estimate=pl.CostEstimate(flops=flops, bytes_accessed=flops // 64, transcendentals=0),
        )(*args)

    own_fields = [
        field.reshape(pairs, LANES)
        for field in (shear_pre, sigma_pre, friction_a, state_rate, state_init)
    ]
    own_hbm = [pltpu.with_memory_space_constraint(field, pltpu.HBM) for field in own_fields]

    panels, history, *table = [
        pltpu.with_memory_space_constraint(array, pltpu.HBM)
        for array in (panels, history, block_rows, block_cols, scales)
    ]
    one_lag = 2 * slots * width * 2 * width * 8
    send, rest, guess, recent, *tables, mine = call(
        functools.partial(older_kernel, lags=lags, n_fields=len(own_fields), **sizes),
        [hbm] * (5 + len(own_fields)),
        [
            shape(n_src, n_rcv, *message, dtype=jnp.bfloat16),
            shape(STEPS - 1, recv_rows, LANES),
            shape(src_blocks // 2, LANES),
            shape(STEPS - 1, slots, width, 2 * width, dtype=panels.dtype),
            shape(STEPS - 1, SLOT_ROWS, LANES, dtype=jnp.int32),
            shape(STEPS - 1, recv_rows, LANES, dtype=jnp.bfloat16),
            shape(STEPS - 1, SLOT_ROWS, LANES),
            shape(len(own_fields), pairs, LANES),
        ],
        [
            pltpu.VMEM(panels.shape, panels.dtype),
            pltpu.VMEM(history.shape, history.dtype),
            *[pltpu.SMEM(array.shape, array.dtype) for array in table],
            *[pltpu.VMEM((STEPS - 1, *array.shape[1:]), array.dtype) for array in table],
            pltpu.VMEM((LEAD + src_blocks * TAPS, LANES), f32),
            pltpu.VMEM((recv_rows * 8, LANES), f32),
            pltpu.VMEM((recv_rows * 8, LANES), f32),
            pltpu.VMEM((n_src, *message), jnp.bfloat16),
            pltpu.SemaphoreType.DMA((lags,)),
            pltpu.SemaphoreType.DMA((7 + len(own_fields),)),
            pltpu.SemaphoreType.DMA((n_rcv + 1,)),
        ],
        "older", [panels, history, *table, *own_hbm], 60 * one_lag, limit=32 * 1024 * 1024,
        out_specs=[hbm] + [vmem] * 7,
    )

    parts = [mine] + [
        lax.ppermute(mine, "rcv", [(at, at ^ turn) for at in range(n_rcv)]) for turn in range(1, n_rcv)
    ]
    slips = []
    recv = lax.all_to_all(send.reshape(n_src * n_rcv, *message), ("src", "rcv"), 0, 0, tiled=True)
    for step_no in range(STEPS - 1):
        last = step_no == STEPS - 2
        dups = 1 if last else n_rcv
        later = STEPS - 2 - step_no
        first = step_no == 0
        solve_inputs = parts if first else [fields, state]
        packed = shape(src_blocks // 2, LANES)
        send, slip_rate, state, *more = call(
            functools.partial(
                step_kernel, step_no=step_no, dups=dups, later=later,
                n_src=n_src, n_rcv=n_rcv, own_blocks=own_blocks,
            ),
            [vmem] * (7 + len(solve_inputs)),
            [shape(n_src * dups, *message, dtype=jnp.bfloat16), packed, packed]
            + [shape(len(own_fields), src_blocks // 2, LANES)] * first
            + [shape(later, recv_rows, LANES)] * bool(later),
            [
                pltpu.VMEM((src_blocks, LANES), f32),
                pltpu.VMEM((src_blocks, LANES), f32),
                pltpu.VMEM((recv_rows, LANES), f32),
            ],
            "step", [recv, guess, rest, recent, *tables, *solve_inputs], one_lag,
        )
        fields = more.pop(0) if first else fields
        guess = slip_rate
        rest = more[0] if later else rest
        slips.append(slip_rate)
        recv = lax.all_to_all(send, "src" if last else ("src", "rcv"), 0, 0, tiled=True)

    slip_rates, state = call(
        functools.partial(last_kernel, step_no=STEPS - 1, n_src=n_src),
        [vmem] * (6 + len(slips)),
        [shape(STEPS, own), shape(pairs, LANES)],
        [pltpu.VMEM((own_blocks, LANES), f32)],
        "last", [recv, *own_fields[:4], state, *slips], 10 ** 6,
    )
    return (slip_rates, state.reshape(own))


def solution(mesh):
    return jax.shard_map(
        per_device,
        mesh=mesh,
        in_specs=(
            P(None, "src"),
            P(None, "src", "rcv", None, None, None),
            P(None, "src", "rcv", None),
            P(None, "src", "rcv", None),
            P(None, "src", "rcv", None),
            P(("src", "rcv")),
            P(("src", "rcv")),
            P(("src", "rcv")),
            P(("src", "rcv")),
            P(("src", "rcv")),
        ),
        out_specs=(P(None, ("src", "rcv")), P(("src", "rcv"))),
        check_vma=False,
    )
```

```python
import functools

import jax
import jax.numpy as jnp
from jax import lax
from jax.experimental import pallas as pl
from jax.experimental.pallas import tpu as pltpu
from jax.sharding import PartitionSpec as P

STEPS = 4
NEWTON_ITERS = 4
DAMPING = 1.0
LOADING = 0.05
TIME_STEP = 0.2
LANES = 128
HALF = LANES // 2
ROWS = 4
IN_FLIGHT = 8
GROUP = 4
SLOT_ROWS = 32
PARTS = 3
MESSAGE_BITS = 22
MESSAGE_SCALE = 2.0 ** MESSAGE_BITS
TAPS = 24
LEAD = 8
VMEM_LIMIT = 16 * 1024 * 1024


def inverse_sinh(value, root):
    result = jnp.log(jnp.abs(value) + root)
    return jnp.where(value < 0.0, -result, result)


def friction_solve(shear, normal_stress, step_no, guess, state_now, fields):
    shear_pre, sigma_pre, friction_a, state_rate = fields
    shear_total = shear + shear_pre + LOADING * (step_no + 1)
    normal = sigma_pre * (1.0 + 0.5 * jnp.tanh(normal_stress))
    strength = friction_a * normal
    factor = 0.5 * jnp.exp(state_now)
    slip_rate = guess
    for attempt in range(NEWTON_ITERS):
        scaled = slip_rate * factor
        root = jnp.sqrt(1.0 + scaled * scaled)
        misfit = shear_total - DAMPING * slip_rate - strength * inverse_sinh(scaled, root)
        derivative = -DAMPING - strength * factor / root
        slip_rate = slip_rate - misfit / derivative
    next_state = state_now + TIME_STEP * state_rate * jnp.tanh(
        jnp.exp(-state_now) - jnp.abs(slip_rate)
    )
    return slip_rate, next_state


def split_stress(even, odd):
    low = lax.broadcasted_iota(jnp.int32, even.shape, 1) < HALF
    shear = jnp.where(low, even, pltpu.roll(odd, HALF, 1))
    normal = jnp.where(low, pltpu.roll(even, HALF, 1), odd)
    return shear, normal


def encode(partial):
    scaled = partial * (1.0 / MESSAGE_SCALE)
    return scaled * scaled * scaled


def decode(message):
    cube = message.astype(jnp.float32)
    root = jnp.exp2(jnp.log2(jnp.abs(cube)) * (1.0 / 3.0) + MESSAGE_BITS)
    return jnp.where(cube < 0.0, -root, root)


def pack_messages(send, partials, own_blocks, n_dest, dups):
    for dest in range(n_dest):
        for tile in range(own_blocks // ROWS):
            piece = partials(dest * own_blocks + tile * ROWS, ROWS).astype(jnp.bfloat16)
            for dup in range(dups):
                send[dest * dups + dup, :, tile * LANES:(tile + 1) * LANES] = piece


def sum_messages(recv, total, own_blocks, n_src, owners):
    for owner in range(owners):
        part = decode(recv[owner])
        for src in range(1, n_src):
            part = part + decode(recv[src * owners + owner])
        for tile in range(own_blocks // ROWS):
            first = owner * own_blocks + tile * ROWS
            total[first:first + ROWS, :] = part[:, tile * LANES:(tile + 1) * LANES]
    pairs = owners * own_blocks // 2
    return total[pl.ds(0, pairs, stride=2), :], total[pl.ds(1, pairs, stride=2), :]


def make_tables(rows, cols, scales, gather, scatter, weights):
    slots = rows.shape[-1]
    lane = lax.broadcasted_iota(jnp.int32, (SLOT_ROWS, LANES), 1)
    diagonal = lax.broadcasted_iota(jnp.int32, (SLOT_ROWS, LANES), 0) == lane
    rest = jnp.full((1, LANES - slots), -1.0, jnp.float32)

    def widened(values):
        return jnp.concatenate([values.astype(jnp.float32), rest], axis=1)

    def column(values):
        spread = jnp.where(diagonal, jnp.broadcast_to(values, diagonal.shape), 0.0)
        return jnp.sum(spread, axis=1, keepdims=True)

    one_row = lax.broadcasted_iota(jnp.int32, (1, LANES), 1)
    block = lax.broadcasted_iota(jnp.int32, (scatter.shape[1], LANES), 0).astype(jnp.float32)
    for lag in range(STEPS - 1):
        row_ids = widened(rows[lag, 0])
        for part in range(1, PARTS):
            at = one_row >= part * SLOT_ROWS
            row_ids = jnp.where(at, pltpu.roll(widened(rows[lag, 0]), part * SLOT_ROWS, 1), row_ids)
        row_ids = jnp.where(one_row < PARTS * SLOT_ROWS, row_ids, -1.0)
        scatter[lag] = (block == row_ids).astype(jnp.float32).astype(jnp.bfloat16)
        picks = jnp.maximum(column(widened(cols[lag, 0])), 0.0).astype(jnp.int32)
        gather[lag] = jnp.broadcast_to(picks, gather.shape[1:])
        weights[lag] = jnp.broadcast_to(column(widened(scales[lag, 0])), weights.shape[1:])


def older_kernel(
    panels, history, rows_in, cols_in, scales_in, *refs,
    lags, slots, n_src, n_rcv, own_blocks, n_fields,
):
    own_fields, refs = refs[:n_fields], refs[n_fields:]
    send, rest, guess, recent, gather, scatter, weights, fields, *refs = refs
    (
        panel_buf, history_buf, rows, cols, scales, rows_now, cols_now, scales_now, sources, acc_low, acc_high, messages,
        sems, small_sems, out_sems,
    ) = refs
    src_blocks = n_rcv * own_blocks
    recv_blocks = n_src * own_blocks
    recent_lags = pl.ds(0, STEPS - 1)
    smalls = [
        pltpu.make_async_copy(source, target, small_sems.at[at])
        for at, (source, target) in enumerate([
            (history, history_buf), (cols_in, cols), (rows_in, rows), (scales_in, scales),
            (rows_in.at[recent_lags], rows_now), (cols_in.at[recent_lags], cols_now),
            (scales_in.at[recent_lags], scales_now),
            *[(field, fields.at[at]) for at, field in enumerate(own_fields)],
        ])
    ]

    def panel_copy(lag):
        return pltpu.make_async_copy(panels.at[lag], panel_buf.at[lag], sems.at[lag])

    for copy in smalls:
        copy.start()
    for lag in range(IN_FLIGHT):
        panel_copy(lag).start()
    accs = (acc_low, acc_high)
    for acc in accs:
        acc[...] = jnp.zeros_like(acc)
    tail = jnp.zeros((TAPS - lags, LANES), jnp.float32)
    sources[0:LEAD, :] = jnp.zeros((LEAD, LANES), jnp.float32)
    smalls[0].wait()
    for pair in range(src_blocks // 2):
        tile = history_buf[:, pair * LANES:(pair + 1) * LANES].astype(jnp.float32)
        for half in range(2):
            base = LEAD + (2 * pair + half) * TAPS
            sources[base:base + lags, :] = tile if half == 0 else pltpu.roll(tile, HALF, 1)
            sources[base + lags:base + TAPS, :] = tail
    for copy in smalls[1:7]:
        copy.wait()
    top = lax.broadcasted_iota(jnp.int32, (8, LANES), 0) < STEPS
    match = top == (lax.broadcasted_iota(jnp.int32, (8, LANES), 1) < HALF)
    zero = jnp.zeros((8, LANES), jnp.float32)

    handed_on = pltpu.make_async_copy(panels.at[recent_lags], recent, out_sems.at[n_rcv])

    def one_lag(lag, carry):
        panel_copy(lag).wait()

        @pl.when(lag == STEPS)
        def _():
            handed_on.start()

        @pl.when(lag + IN_FLIGHT < lags)
        def _():
            panel_copy(lag + IN_FLIGHT).start()

        first_tap = LEAD + (lags - 1) - lag
        for group in range(0, slots, GROUP):
            pairs = []
            for slot in range(group, group + GROUP, 2):
                low = sources[pl.ds(cols[lag, 0, 0, slot] * TAPS + first_tap, 8), :]
                partner = cols[lag, 0, 0, slot + 1] ^ 1
                high = sources[pl.ds(partner * TAPS + first_tap - STEPS, 8), :]
                pairs.append(jnp.where(match, jnp.where(top, low, high), 0.0))
            columns = [
                jnp.concatenate([pair if at == to else zero for at in range(len(pairs))], axis=0)
                for to, pair in enumerate(pairs)
            ]
            picked = jnp.concatenate(columns, axis=1).astype(jnp.bfloat16)
            panel = panel_buf[lag, group:group + GROUP].reshape(GROUP * HALF, LANES)
            terms = jnp.dot(picked, panel, preferred_element_type=jnp.float32)
            for pair in range(len(pairs)):
                slot = group + 2 * pair
                scale = jnp.where(top, scales[lag, 0, 0, slot], scales[lag, 0, 0, slot + 1])
                term = terms[8 * pair:8 * pair + 8] * scale
                for part, acc in enumerate(accs):
                    at = pl.ds(pl.multiple_of(rows[lag, 0, 0, slot + part] * 8, 8), 8)
                    acc[at, :] = acc[at, :] + term
        return carry

    lax.fori_loop(0, lags, one_lag, 0, unroll=2)
    def partials(first_row, count, step):
        low, high = [
            acc[pl.ds(first_row * 8 + part * STEPS + step, count, stride=8), :]
            for part, acc in enumerate(accs)
        ]
        return low + high

    pack_messages(messages, lambda first, count: encode(partials(first, count, 0)), own_blocks, n_src, 1)
    outgoing = [
        pltpu.make_async_copy(messages, send.at[:, dup], out_sems.at[dup]) for dup in range(n_rcv)
    ]
    for copy in outgoing:
        copy.start()
    make_tables(rows_now, cols_now, scales_now, gather, scatter, weights)
    for step in range(1, STEPS):
        rest[step - 1] = partials(0, recv_blocks, step)
    guess[...] = sources[pl.ds(LEAD + lags - 1, src_blocks // 2, stride=2 * TAPS), :]
    for copy in outgoing + smalls[7:] + [handed_on]:
        copy.wait()


def spread_sources(slip_rate, sources):
    pairs = slip_rate.shape[0]
    low = lax.broadcasted_iota(jnp.int32, slip_rate.shape, 1) < HALF
    turned = pltpu.roll(slip_rate, HALF, 1)
    sources[pl.ds(0, pairs, stride=2), :] = jnp.where(low, slip_rate, turned)
    sources[pl.ds(1, pairs, stride=2), :] = jnp.where(low, turned, slip_rate)


def take_rows(groups, rows):
    taken = []
    for first in range(0, rows.shape[0], 8):
        row = rows[first:first + 8]
        within = row & 7
        block = row - within
        piece = jnp.zeros(groups[0].shape, jnp.float32)
        for at, group in enumerate(groups):
            found = jnp.take_along_axis(group, within, axis=0, mode="promise_in_bounds")
            piece = jnp.where(block == 8 * at, found, piece)
        taken.append(piece)
    return jnp.concatenate(taken, axis=0)


def new_terms(lags, panels, sources, gather, scatter, weights):
    slots, width, wide = panels.shape[1:]
    groups = [sources[at:at + 8, :] for at in range(0, sources.shape[0], 8)]
    picked = [take_rows(groups, gather[lag]) for lag in lags]
    lane = lax.broadcasted_iota(jnp.int32, picked[0].shape, 1)
    row = lax.broadcasted_iota(jnp.int32, picked[0].shape, 0)
    first = row - jnp.where(lane < HALF, 0, 1)
    terms = []
    for lag, rates in zip(lags, picked):
        tiles = [
            jnp.where(first == slot, rates, 0.0).astype(jnp.bfloat16) for slot in range(0, slots, 2)
        ]
        panel = panels[lag].reshape(slots * width, wide)
        terms.append(
            jnp.dot(jnp.concatenate(tiles, axis=1), panel, preferred_element_type=jnp.float32)
        )
    sums = []
    for lag, left in zip(lags, terms):
        left = left * weights[lag]
        parts = []
        for part in range(PARTS):
            parts.append(left.astype(jnp.bfloat16))
            left = left - parts[-1].astype(jnp.float32)
        stacked = jnp.concatenate(parts, axis=0)
        table = scatter[lag][:, :stacked.shape[0]]
        sums.append(jnp.dot(table, stacked, preferred_element_type=jnp.float32))
    return sums


def order_fields(parts, fields):
    here = lax.axis_index("rcv")
    pairs = parts[0].shape[1]
    for owner in range(len(parts)):
        chosen = parts[0][...]
        for turn in range(1, len(parts)):
            chosen = jnp.where(here ^ owner == turn, parts[turn][...], chosen)
        for kind in range(fields.shape[0]):
            fields[kind, owner * pairs:(owner + 1) * pairs, :] = chosen[kind]


def step_kernel(
    recv, guess, rest, panels, gather, scatter, weights, *refs,
    step_no, n_src, n_rcv, own_blocks, dups, later,
):
    if step_no == 0:
        parts, (send, slip_out, state_out, fields), refs = refs[:n_rcv], refs[n_rcv:n_rcv + 4], refs[n_rcv + 4:]
        order_fields(parts, fields)
        state_in = fields.at[4]
    else:
        (fields, state_in, send, slip_out, state_out), refs = refs[:5], refs[5:]
    rest_out, (total, sources, acc) = refs[:-3], refs[-3:]
    shear, normal = split_stress(*sum_messages(recv, total, own_blocks, n_src, n_rcv))
    slip_rate, next_state = friction_solve(
        shear, normal, step_no, guess[...], state_in[...], [fields[kind] for kind in range(4)]
    )
    spread_sources(slip_rate, sources)
    terms = new_terms(range(later + 1), panels, sources, gather, scatter, weights)
    acc[...] = encode(rest[0] + terms[0])
    pack_messages(send, lambda first, count: acc[pl.ds(first, count), :], own_blocks, n_src, dups)
    slip_out[...] = slip_rate
    state_out[...] = next_state
    for at in range(later):
        rest_out[0][at] = rest[at + 1] + terms[at + 1]


def last_kernel(
    recv, shear_pre, sigma_pre, friction_a, state_rate, state_in, *refs, step_no, n_src,
):
    slips, (slip_out, state_out, total) = refs[:step_no], refs[step_no:]
    pairs = slip_out.shape[1] // LANES
    mine = pl.ds(lax.axis_index("rcv") * pairs, pairs)
    shear, normal = split_stress(*sum_messages(recv, total, 2 * pairs, n_src, 1))
    fields = [ref[...] for ref in (shear_pre, sigma_pre, friction_a, state_rate)]
    slip_rate, next_state = friction_solve(
        shear, normal, step_no, slips[-1][mine, :], state_in[mine, :], fields
    )
    for step, field in enumerate([ref[mine, :] for ref in slips] + [slip_rate]):
        for row in range(pairs):
            slip_out[step:step + 1, row * LANES:(row + 1) * LANES] = field[row:row + 1]
    state_out[...] = next_state


def per_device(
    history, kernel, scales, block_rows, block_cols,
    shear_pre, sigma_pre, friction_a, state_rate, state_init,
):
    lags = kernel.shape[0]
    slots = kernel.shape[3]
    width = kernel.shape[4]
    n_src = lax.axis_size("src")
    n_rcv = lax.axis_size("rcv")
    own = shear_pre.shape[0]
    own_blocks = own // width
    pairs = own // LANES
    src_blocks = n_rcv * own_blocks
    recv_rows = n_src * own_blocks
    message = (ROWS, own_blocks // ROWS * LANES)
    panels = kernel.reshape(lags, slots, width, 2 * width)
    f32 = jnp.float32
    hbm = pl.BlockSpec(memory_space=pltpu.HBM)
    vmem = pl.BlockSpec(memory_space=pltpu.VMEM)
    sizes = dict(slots=slots, n_src=n_src, n_rcv=n_rcv, own_blocks=own_blocks)
    def shape(*dims, dtype=f32):
        return jax.ShapeDtypeStruct(dims, dtype)

    def call(body, ins, outs, scratch, name, args, flops, limit=VMEM_LIMIT, out_specs=None):
        return pl.pallas_call(
            body, in_specs=ins, out_specs=out_specs or [vmem] * len(outs), out_shape=outs, scratch_shapes=scratch,
            compiler_params=pltpu.CompilerParams(vmem_limit_bytes=limit), name=name,
            cost_estimate=pl.CostEstimate(flops=flops, bytes_accessed=flops // 64, transcendentals=0),
        )(*args)

    own_fields = [
        field.reshape(pairs, LANES)
        for field in (shear_pre, sigma_pre, friction_a, state_rate, state_init)
    ]
    own_hbm = [pltpu.with_memory_space_constraint(field, pltpu.HBM) for field in own_fields]

    panels, history, *table = [
        pltpu.with_memory_space_constraint(array, pltpu.HBM)
        for array in (panels, history, block_rows, block_cols, scales)
    ]
    one_lag = 2 * slots * width * 2 * width * 8
    send, rest, guess, recent, *tables, mine = call(
        functools.partial(older_kernel, lags=lags, n_fields=len(own_fields), **sizes),
        [hbm] * (5 + len(own_fields)),
        [
            shape(n_src, n_rcv, *message, dtype=jnp.bfloat16),
            shape(STEPS - 1, recv_rows, LANES),
            shape(src_blocks // 2, LANES),
            shape(STEPS - 1, slots, width, 2 * width, dtype=panels.dtype),
            shape(STEPS - 1, SLOT_ROWS, LANES, dtype=jnp.int32),
            shape(STEPS - 1, recv_rows, LANES, dtype=jnp.bfloat16),
            shape(STEPS - 1, SLOT_ROWS, LANES),
            shape(len(own_fields), pairs, LANES),
        ],
        [
            pltpu.VMEM(panels.shape, panels.dtype),
            pltpu.VMEM(history.shape, history.dtype),
            *[pltpu.SMEM(array.shape, array.dtype) for array in table],
            *[pltpu.VMEM((STEPS - 1, *array.shape[1:]), array.dtype) for array in table],
            pltpu.VMEM((LEAD + src_blocks * TAPS, LANES), f32),
            pltpu.VMEM((recv_rows * 8, LANES), f32),
            pltpu.VMEM((recv_rows * 8, LANES), f32),
            pltpu.VMEM((n_src, *message), jnp.bfloat16),
            pltpu.SemaphoreType.DMA((lags,)),
            pltpu.SemaphoreType.DMA((7 + len(own_fields),)),
            pltpu.SemaphoreType.DMA((n_rcv + 1,)),
        ],
        "older", [panels, history, *table, *own_hbm], 60 * one_lag, limit=32 * 1024 * 1024,
        out_specs=[hbm] + [vmem] * 7,
    )

    parts = [mine] + [
        lax.ppermute(mine, "rcv", [(at, at ^ turn) for at in range(n_rcv)]) for turn in range(1, n_rcv)
    ]
    slips = []
    recv = lax.all_to_all(send.reshape(n_src * n_rcv, *message), ("src", "rcv"), 0, 0, tiled=True)
    for step_no in range(STEPS - 1):
        last = step_no == STEPS - 2
        dups = 1 if last else n_rcv
        later = STEPS - 2 - step_no
        first = step_no == 0
        solve_inputs = parts if first else [fields, state]
        packed = shape(src_blocks // 2, LANES)
        send, slip_rate, state, *more = call(
            functools.partial(
                step_kernel, step_no=step_no, dups=dups, later=later,
                n_src=n_src, n_rcv=n_rcv, own_blocks=own_blocks,
            ),
            [vmem] * (7 + len(solve_inputs)),
            [shape(n_src * dups, *message, dtype=jnp.bfloat16), packed, packed]
            + [shape(len(own_fields), src_blocks // 2, LANES)] * first
            + [shape(later, recv_rows, LANES)] * bool(later),
            [
                pltpu.VMEM((src_blocks, LANES), f32),
                pltpu.VMEM((src_blocks, LANES), f32),
                pltpu.VMEM((recv_rows, LANES), f32),
            ],
            "step", [recv, guess, rest, recent, *tables, *solve_inputs], one_lag,
        )
        fields = more.pop(0) if first else fields
        guess = slip_rate
        rest = more[0] if later else rest
        slips.append(slip_rate)
        recv = lax.all_to_all(send, "src" if last else ("src", "rcv"), 0, 0, tiled=True)

    slip_rates, state = call(
        functools.partial(last_kernel, step_no=STEPS - 1, n_src=n_src),
        [vmem] * (6 + len(slips)),
        [shape(STEPS, own), shape(pairs, LANES)],
        [pltpu.VMEM((own_blocks, LANES), f32)],
        "last", [recv, *own_fields[:4], state, *slips], 10 ** 6,
    )
    return (slip_rates, state.reshape(own))


def solution(mesh):
    return jax.shard_map(
        per_device,
        mesh=mesh,
        in_specs=(
            P(None, "src"),
            P(None, "src", "rcv", None, None, None),
            P(None, "src", "rcv", None),
            P(None, "src", "rcv", None),
            P(None, "src", "rcv", None),
            P(("src", "rcv")),
            P(("src", "rcv")),
            P(("src", "rcv")),
            P(("src", "rcv")),
            P(("src", "rcv")),
        ),
        out_specs=(P(None, ("src", "rcv")), P(("src", "rcv"))),
        check_vma=False,
    )
```
